32 devices in a mesh: row: 4 (over x, core), col: 8 (over z, y).
Axes of the slice: x: 2, y: 2, z: 4, core: 2. Of those that a mesh axis runs over, the one named last changes fastest.
Arguments:
- image_tokens: bfloat16 [1024, 50, 768], P(('row', 'col')), may hold values from -6 to 6
- caption_tokens: bfloat16 [1024, 16, 768], P(('row', 'col')), may hold values from -6 to 6
- caption_mask: int32 [1024, 16], P(('row', 'col')), may hold values 0 or 1
- caption_length: int32 [1024], P(('row', 'col')), may hold values from 4 to 16
- image_gain1: float32 [768], replicated, may hold values from 0.5 to 1.5
- image_shift1: float32 [768], replicated, may hold values from -1.2 to 1.2
- image_qkv: bfloat16 [768, 2304], replicated, may hold values from -0.3125 to 0.3125
- image_out: bfloat16 [768, 768], replicated, may hold values from -0.625 to 0.625
- image_gain2: float32 [768], replicated, may hold values from 0.5 to 1.5
- image_shift2: float32 [768], replicated, may hold values from -1.2 to 1.2
- image_up: bfloat16 [768, 3072], replicated, may hold values from -0.21875 to 0.21875
- image_down: bfloat16 [3072, 768], replicated, may hold values from -0.109375 to 0.109375
- text_gain1: float32 [768], replicated, may hold values from 0.5 to 1.5
- text_shift1: float32 [768], replicated, may hold values from -1.2 to 1.2
- text_qkv: bfloat16 [768, 2304], replicated, may hold values from -0.3125 to 0.3125
- text_out: bfloat16 [768, 768], replicated, may hold values from -0.4375 to 0.4375
- text_gain2: float32 [768], replicated, may hold values from 0.5 to 1.5
- text_shift2: float32 [768], replicated, may hold values from -1.2 to 1.2
- text_up: bfloat16 [768, 3072], replicated, may hold values from -0.21875 to 0.21875
- text_down: bfloat16 [3072, 768], replicated, may hold values from -0.109375 to 0.109375
Outputs:
- grad_tokens: float32 [1024, 16, 768], P(('row', 'col'))
- grad_gain1: float32 [768], P('col')
- grad_shift1: float32 [768], P('col')
- grad_qkv: float32 [768, 2304], P(None, 'col')
- grad_out: float32 [768, 768], P(None, 'col')
- grad_gain2: float32 [768], P('col')
- grad_shift2: float32 [768], P('col')
- grad_up: float32 [768, 3072], P(None, 'col')
- grad_down: float32 [3072, 768], P('col')
The draws below stay inside these ranges and needn't reach their ends.
All inputs are finite; a program needn't handle non-finite values. No bound on the sum of `caption_mask` on one device may be relied on, other than what follows from the above.
Results may differ from the reference program's by a relative error of at most 0.025.
Values may be sent and summed in bfloat16 or wider, within the bound.
A program may use at most 192 MiB of HBM per device.

```python
import math
import jax
import jax.numpy as jnp
from jax import lax

D = 768
H = 12
HD = 64
FF = 3072
IMG = 50
L = 16
PAIRS = 1024


def touch_ends(drawn, key, smallest, largest):
    place = [jax.random.randint(jax.random.fold_in(key, axis), (), 0, length) for axis, length in enumerate(drawn.shape)]
    widest = drawn.shape.index(max(drawn.shape))
    next_to = place[:widest] + [(place[widest] + 1) % drawn.shape[widest]] + place[widest + 1:]
    return drawn.at[tuple(place)].set(smallest).at[tuple(next_to)].set(largest)


def levels(rng, shape, cuts, smallest, largest):
    level = 1.0
    for position, parts in cuts:
        heights = jax.random.uniform(jax.random.fold_in(jax.random.fold_in(rng, 6), position), (parts,), jnp.float32, smallest / len(cuts), largest / len(cuts))
        level = level * jnp.repeat(jnp.exp(heights), shape[position] // parts).reshape((-1,) + (1,) * (len(shape) - 1 - position))
    return level


def noise(rng, dims, scale, most, split=(), kind=jnp.bfloat16):
    level = levels(rng, dims, split, -0.22, 0.18) if split else 1.0
    drawn = jax.random.normal(rng, dims, jnp.float32) * scale * level
    return jnp.minimum(jnp.maximum(drawn, -most), most).astype(kind)


def setup_inputs(seed: int = 0) -> dict:
    key_of = jax.random.split(jax.random.key(seed), 21)
    return {
        "image_tokens": noise(key_of[0], (PAIRS, IMG, D), 1.0, 6.0, ((0, 32),)),
        "caption_tokens": noise(key_of[1], (PAIRS, L, D), 1.0, 6.0, ((0, 32),)),
        "caption_mask": touch_ends((jax.random.randint(key_of[2], (PAIRS, L), 0, 4) < 3).astype(jnp.int32), jax.random.fold_in(key_of[2], 1), 0, 1),
        "caption_length": touch_ends(jax.random.randint(key_of[3], (PAIRS,), 4, L + 1), jax.random.fold_in(key_of[3], 1), 4, L).astype(jnp.int32),
        "image_gain1": jnp.clip(1.0 + 0.1 * jax.random.normal(key_of[4], (D,), jnp.float32), 0.5, 1.5),
        "image_shift1": noise(key_of[5], (D,), 0.2, 1.2, (), jnp.float32),
        "image_qkv": noise(key_of[6], (D, 3 * D), (D // 2) ** -0.5, 0.3125),
        "image_out": noise(key_of[7], (D, D), (D // 8) ** -0.5, 0.625),
        "image_gain2": jnp.clip(1.0 + 0.1 * jax.random.normal(key_of[8], (D,), jnp.float32), 0.5, 1.5),
        "image_shift2": noise(key_of[9], (D,), 0.2, 1.2, (), jnp.float32),
        "image_up": noise(key_of[10], (D, FF), D ** -0.5, 0.21875),
        "image_down": noise(key_of[11], (FF, D), FF ** -0.5, 0.109375),
        "text_gain1": jnp.clip(1.0 + 0.1 * jax.random.normal(key_of[12], (D,), jnp.float32), 0.5, 1.5),
        "text_shift1": noise(key_of[13], (D,), 0.2, 1.2, (), jnp.float32),
        "text_qkv": noise(key_of[14], (D, 3 * D), (D // 2) ** -0.5, 0.3125),
        "text_out": noise(key_of[15], (D, D), (D // 4) ** -0.5, 0.4375),
        "text_gain2": jnp.clip(1.0 + 0.1 * jax.random.normal(key_of[16], (D,), jnp.float32), 0.5, 1.5),
        "text_shift2": noise(key_of[17], (D,), 0.2, 1.2, (), jnp.float32),
        "text_up": noise(key_of[18], (D, FF), D ** -0.5, 0.21875),
        "text_down": noise(key_of[19], (FF, D), FF ** -0.5, 0.109375),
    }


@jax.custom_vjp
def low(v):
    return lax.optimization_barrier(v.astype(jnp.bfloat16)).astype(jnp.float32)

@jax.custom_vjp
def low_back(v):
    return v

def low_keep(v):
    return (low(v), None)

def low_pass(kept, grad):
    return (grad,)

def back_keep(v):
    return (v, None)

def back_low(kept, grad):
    return (low(grad),)
low.defvjp(low_keep, low_pass)
low_back.defvjp(back_keep, back_low)
epsilon = 1e-06
highest = lax.Precision.HIGHEST

def keep_value(value):
    return value

def normalize(x, gain, shift):
    centred = x - lax.optimization_barrier(jnp.mean(x, -1, keepdims=True))
    variance = lax.optimization_barrier(jnp.mean(centred * centred, -1, keepdims=True))
    return centred * lax.rsqrt(variance + epsilon) * gain + shift

def block(tokens, weights, key_valid, tracked):
    back = low_back if tracked else keep_value
    gain1, shift1, w_qkv, w_out, gain2, shift2, w_up, w_down = weights
    groups, seq, width = tokens.shape
    scale = HD ** (-0.5)
    normed1 = low(normalize(tokens, gain1, shift1))
    qkv_act = low(back(jnp.einsum('gsd,de->gse', normed1, w_qkv, precision=highest)))
    qkv_act = qkv_act.reshape(groups, seq, 3, H, HD)
    scores = back(jnp.einsum('gqhe,gkhe->ghqk', qkv_act[:, :, 0], qkv_act[:, :, 1], precision=highest) * scale)
    if key_valid is not None:
        scores = jnp.where(key_valid[:, None, None, :], scores, -1e+30)
    peak = lax.optimization_barrier(jnp.max(scores, -1, keepdims=True))
    expd = jnp.exp(scores - peak)
    probs = low(expd / lax.optimization_barrier(jnp.sum(expd, -1, keepdims=True)))
    attn = low(back(jnp.einsum('ghqk,gkhe->gqhe', probs, qkv_act[:, :, 2], precision=highest)))
    attn = attn.reshape(groups, seq, width)
    mixed = tokens + back(jnp.einsum('gsd,de->gse', attn, w_out, precision=highest))
    normed2 = low(normalize(mixed, gain2, shift2))
    hidden = back(jnp.einsum('gsd,de->gse', normed2, w_up, precision=highest))
    act = low(jax.nn.gelu(hidden, approximate=False))
    return mixed + back(jnp.einsum('gse,ed->gsd', act, w_down, precision=highest))

def unit_rows(pooled):
    return low(pooled * lax.rsqrt(lax.optimization_barrier(jnp.sum(pooled * pooled, -1, keepdims=True)) + epsilon))

def reference(image_tokens, caption_tokens, caption_mask, caption_length, image_gain1, image_shift1, image_qkv, image_out, image_gain2, image_shift2, image_up, image_down, text_gain1, text_shift1, text_qkv, text_out, text_gain2, text_shift2, text_up, text_down):
    logit_scale = 2.0 * math.sqrt(D)
    image_weights = tuple((w.astype(jnp.float32) for w in (image_gain1, image_shift1, image_qkv, image_out, image_gain2, image_shift2, image_up, image_down)))
    text_weights = tuple((w.astype(jnp.float32) for w in (text_gain1, text_shift1, text_qkv, text_out, text_gain2, text_shift2, text_up, text_down)))
    image_group = math.gcd(PAIRS, 64)

    def image_embed(block_tokens):
        result = block(block_tokens.astype(jnp.float32), image_weights, None, False)
        return unit_rows(lax.optimization_barrier(jnp.mean(result, 1)))
    image_unit = lax.map(image_embed, image_tokens.reshape(PAIRS // image_group, image_group, IMG, D)).reshape(PAIRS, D)
    positions = jnp.arange(L, dtype=jnp.int32)
    key_valid = positions[None, :] < caption_length[:, None]
    pool_weight = caption_mask.astype(jnp.float32) * key_valid.astype(jnp.float32)
    text_group = math.gcd(PAIRS, 256)
    group_count = PAIRS // text_group

    def loss_of(tokens, weights):

        def text_embed(pieces):
            block_tokens, block_valid, block_weight = pieces
            result = block(block_tokens, weights, block_valid, True)
            count = jnp.maximum(lax.optimization_barrier(jnp.sum(block_weight, 1)), 1.0)
            pooled = lax.optimization_barrier(jnp.sum(result * block_weight[:, :, None], 1)) / count[:, None]
            return unit_rows(pooled)
        text_unit = lax.map(jax.checkpoint(text_embed), (tokens.reshape(group_count, text_group, L, D), key_valid.reshape(group_count, text_group, L), pool_weight.reshape(group_count, text_group, L))).reshape(PAIRS, D)
        sim = low_back(logit_scale * jnp.dot(image_unit, text_unit.T, precision=highest, preferred_element_type=jnp.float32))
        positive = logit_scale * lax.optimization_barrier(jnp.sum(image_unit * text_unit, -1))
        row_peak = lax.optimization_barrier(jnp.max(sim, 1, keepdims=True))
        row_lse = row_peak[:, 0] + jnp.log(lax.optimization_barrier(jnp.sum(jnp.exp(sim - row_peak), 1)))
        col_peak = lax.optimization_barrier(jnp.max(sim, 0, keepdims=True))
        col_lse = col_peak[0] + jnp.log(lax.optimization_barrier(jnp.sum(jnp.exp(sim - col_peak), 0)))
        return (jnp.sum(row_lse) + jnp.sum(col_lse) - 2.0 * jnp.sum(positive)) / (2.0 * PAIRS)
    objective, pullback = jax.vjp(loss_of, caption_tokens.astype(jnp.float32), text_weights)
    grad_tokens, grads = pullback(jnp.ones_like(objective))
    return (grad_tokens, grads[0], grads[1], grads[2], grads[3], grads[4], grads[5], grads[6], grads[7])
```

```python
import math, functools
import jax, jax.numpy as jnp
from jax import lax
from jax.experimental import pallas as pl
from jax.experimental.pallas import tpu as pltpu
from jax.sharding import PartitionSpec as P

epsilon = 1e-06
log2e = 1.4426950408889634
inv_root2 = 0.7071067811865476
f32 = jnp.float32
bf16 = jnp.bfloat16


def dot(a, b):
    return jnp.dot(a, b, preferred_element_type=f32)


def dot_t(a, b):
    return lax.dot_general(a, b, (((1,), (1,)), ((), ())), preferred_element_type=f32)


def stats(x):
    centred = x - jnp.mean(x, -1, keepdims=True)
    inverse = lax.rsqrt(jnp.mean(centred * centred, -1, keepdims=True) + epsilon)
    return centred * inverse, inverse


def gelu(v):
    u = 0.5 * v
    return u * lax.erf(v * inv_root2) + u


def image_kernel(
    heads, x_ref, g1, s1, wqkv, wout, g2, s2, wup, wdown, out_ref,
    xs, n, qkv, at, mixed, act, pooled
):
    images, tokens, width = x_ref.shape
    pad = -(-tokens // 8) * 8
    rows = images * pad
    i = pl.program_id(0)

    @pl.when(i == 0)
    def _():
        xs[...] = jnp.zeros_like(xs)

    for k in range(images):
        xs[k * pad : k * pad + tokens, :] = x_ref[k].astype(f32)
    scaled, _ = stats(xs[...])
    n[...] = (scaled * g1[...] + s1[...]).astype(bf16)
    for c in range(3):
        cols = slice(c * width, (c + 1) * width)
        qkv[:, cols] = dot(n[...], wqkv[:, cols]).astype(bf16)

    group = 2 * pad
    hd = width // heads
    r_id = lax.broadcasted_iota(jnp.int32, (group, group), 0)
    c_id = lax.broadcasted_iota(jnp.int32, (group, group), 1)
    same = (r_id < pad) == (c_id < pad)
    inside = jnp.where(c_id < pad, c_id, c_id - pad) < tokens
    keep = same & inside
    first = lax.broadcasted_iota(jnp.int32, (group, 2 * hd), 1) < hd
    factor = hd ** (-0.5) * log2e

    def attend(g, carry):
        rs = pl.ds(pl.multiple_of(g * group, 16), group)
        for hp in range(heads // 2):
            lanes = slice(hp * 2 * hd, (hp + 1) * 2 * hd)
            q2 = qkv[rs, lanes]
            k2 = qkv[rs, slice(width + lanes.start, width + lanes.stop)]
            v2 = qkv[rs, slice(2 * width + lanes.start, 2 * width + lanes.stop)]
            outs = []
            for h in range(2):
                kh = jnp.where(first == (h == 0), k2, jnp.zeros_like(k2))
                s = jnp.where(keep, dot_t(q2, kh) * factor, -1e30)
                e = jnp.exp2(s - jnp.max(s, -1, keepdims=True))
                total = jnp.sum(e, -1, keepdims=True)
                outs.append(dot(e.astype(bf16), v2) * (1.0 / total))
            at[rs, lanes] = jnp.where(first, outs[0], outs[1]).astype(bf16)
        return carry

    lax.fori_loop(0, rows // group, attend, 0)
    mixed[...] = xs[...] + dot(at[...], wout[...])
    row = lax.broadcasted_iota(jnp.int32, (pad, 1), 0)
    valid = (row < tokens).astype(f32)
    dst = pl.ds(pl.multiple_of(i * images, 8), images)
    m3 = mixed[...].reshape(images, pad, width)
    pooled[dst, :] = jnp.sum(m3 * valid[None], 1)
    scaled, _ = stats(mixed[...])
    normed = ((scaled * g2[...] + s2[...]).reshape(images, pad, width) * valid[None]).reshape(rows, width)
    n[...] = normed.astype(bf16)
    hidden = wup.shape[1]
    step = 768
    for c in range(0, hidden, step):
        a = gelu(dot(n[...], wup[:, c : c + step]))
        act[dst, c : c + step] = jnp.sum(a.reshape(images, pad, step), 1)

    @pl.when(i == pl.num_programs(0) - 1)
    def _():
        a = act[...] * (1.0 / tokens)
        hi = a.astype(bf16)
        lo = (a - hi.astype(f32)).astype(bf16)
        count = a.shape[0]
        both = dot(jnp.concatenate([hi, lo], 0), wdown[...])
        e = pooled[...] * (1.0 / tokens) + both[:count] + both[count:]
        out_ref[...] = (e * lax.rsqrt(jnp.sum(e * e, -1, keepdims=True) + epsilon)).astype(bf16)


def image_unit(x, g1, s1, wqkv, wout, g2, s2, wup, wdown, heads=12, images=8):
    count, tokens, width = x.shape
    hidden = wup.shape[1]
    pad = -(-tokens // 8) * 8
    rows = images * pad
    full = lambda a: pl.BlockSpec(a.shape, lambda i: (0,) * a.ndim, pipeline_mode=pl.Buffered(1))
    args = (x, g1[None], s1[None], wqkv, wout, g2[None], s2[None], wup, wdown)
    return pl.pallas_call(
        functools.partial(image_kernel, heads),
        name="image",
        grid=(count // images,),
        out_shape=jax.ShapeDtypeStruct((count, width), bf16),
        in_specs=[pl.BlockSpec((images, tokens, width), lambda i: (i, 0, 0))] + [full(a) for a in args[1:]],
        out_specs=pl.BlockSpec((count, width), lambda i: (0, 0)),
        scratch_shapes=[
            pltpu.VMEM((rows, width), f32),
            pltpu.VMEM((rows, width), bf16),
            pltpu.VMEM((rows, 3 * width), bf16),
            pltpu.VMEM((rows, width), bf16),
            pltpu.VMEM((rows, width), f32),
            pltpu.VMEM((count, hidden), f32),
            pltpu.VMEM((count, width), f32),
        ],
    )(*args)

def dot_0(a, b):
    return lax.dot_general(a, b, (((0,), (0,)), ((), ())), preferred_element_type=f32)


def norm_back(grad_normed, scaled, inverse, gain):
    g = grad_normed * gain
    centre = jnp.mean(g, -1, keepdims=True)
    along = jnp.mean(g * scaled, -1, keepdims=True)
    return inverse * (g - centre - scaled * along)


def token_columns(mask_ref, length_ref, seq):
    captions = mask_ref.shape[0]
    rows = captions * seq
    row = lax.broadcasted_iota(jnp.int32, (rows, captions), 0)
    lane = lax.broadcasted_iota(jnp.int32, (rows, captions), 1)
    length = length_ref[...].astype(f32)
    own = row // seq == lane
    length_t = jnp.sum(jnp.where(own, length, 0.0), -1, keepdims=True)
    spread = dot(jnp.where(own, 1.0, 0.0).astype(bf16), mask_ref[...].astype(bf16))
    row = lax.broadcasted_iota(jnp.int32, (rows, seq), 0)
    lane = lax.broadcasted_iota(jnp.int32, (rows, seq), 1)
    mask_t = jnp.sum(jnp.where(row % seq == lane, spread, 0.0), -1, keepdims=True)
    place = (lax.broadcasted_iota(jnp.int32, (rows, 1), 0) % seq).astype(f32)
    weight = jnp.where(place < length_t, mask_t, 0.0)
    eye = lax.broadcasted_iota(jnp.int32, (captions, captions), 0) == lax.broadcasted_iota(
        jnp.int32, (captions, captions), 1
    )
    length_c = jnp.sum(jnp.where(eye, length, 0.0), -1, keepdims=True)
    lane = lax.broadcasted_iota(jnp.int32, (captions, seq), 1).astype(f32)
    count = jnp.sum(jnp.where(lane < length_c, mask_ref[...].astype(f32), 0.0), -1, keepdims=True)
    return length_t, weight, jnp.maximum(count, 1.0)


def text_forward(
    heads, seq, group, x_ref, mask_ref, length_ref, g1, s1, wqkv, wout, g2, s2, wup, wdown,
    n1, qkv, probs, at, mixed, n2, slope, act, cols
):
    rows, width = x_ref.shape
    captions = rows // seq
    hd = width // heads
    length_t, weight, count = token_columns(mask_ref, length_ref, seq)
    cols[:, 0:1] = weight
    cols[:, 1:2] = length_t
    x = x_ref[...].astype(f32)
    scaled, _ = stats(x)
    n1[...] = (scaled * g1[...] + s1[...]).astype(bf16)
    for c in range(3):
        part = slice(c * width, (c + 1) * width)
        qkv[:, part] = dot(n1[...], wqkv[:, part]).astype(bf16)
    r_id = lax.broadcasted_iota(jnp.int32, (group, group), 0)
    c_id = lax.broadcasted_iota(jnp.int32, (group, group), 1)
    same = r_id // seq == c_id // seq
    place = (c_id % seq).astype(f32)
    first = lax.broadcasted_iota(jnp.int32, (group, 2 * hd), 1) < hd
    factor = hd ** (-0.5) * log2e

    def attend(g, carry):
        rs = pl.ds(pl.multiple_of(g * group, 16), group)
        keep = same & (place < cols[rs, 1:2])
        for hp in range(heads // 2):
            lanes = slice(hp * 2 * hd, (hp + 1) * 2 * hd)
            q2 = qkv[rs, lanes]
            k2 = qkv[rs, slice(width + lanes.start, width + lanes.stop)]
            v2 = qkv[rs, slice(2 * width + lanes.start, 2 * width + lanes.stop)]
            outs = []
            for h in range(2):
                kh = jnp.where(first == (h == 0), k2, jnp.zeros_like(k2))
                s = jnp.where(keep, dot_t(q2, kh) * factor, -1e30)
                e = jnp.exp2(s - jnp.max(s, -1, keepdims=True))
                p = e * (1.0 / jnp.sum(e, -1, keepdims=True))
                probs[rs, pl.ds((hp * 2 + h) * group, group)] = p
                outs.append(dot(p.astype(bf16), v2))
            at[rs, lanes] = jnp.where(first, outs[0], outs[1]).astype(bf16)
        return carry

    lax.fori_loop(0, rows // group, attend, 0)
    mixed[...] = x_ref[...].astype(f32) + dot(at[...], wout[...])
    scaled, _ = stats(mixed[...])
    n2[...] = (scaled * g2[...] + s2[...]).astype(bf16)
    hidden = wup.shape[1]
    weight = cols[:, 0:1]
    for c in range(0, hidden, 768):
        h = dot(n2[...], wup[:, c : c + 768])
        phi = 0.5 + 0.5 * lax.erf(h * inv_root2)
        slope[:, c : c + 768] = (phi + h * (jnp.exp(-0.5 * h * h) * inv_root_2pi)).astype(bf16)
        act[:, c : c + 768] = jnp.sum((h * phi * weight).reshape(captions, seq, 768), 1)
    both = split_dot(act[...], wdown)
    pooled = jnp.sum((mixed[...] * weight).reshape(captions, seq, width), 1) + both
    return pooled / count, count


inv_root_2pi = 0.3989422804014327


def split_dot(a, w):
    hi = a.astype(bf16)
    lo = (a - hi.astype(f32)).astype(bf16)
    both = dot(jnp.concatenate([hi, lo], 0), w[...])
    return both[: a.shape[0]] + both[a.shape[0] :]


def text_backward(
    heads, seq, group, gpc, x_ref, g1, wqkv, wout, g2, wup, wdown,
    n1, qkv, probs, at, mixed, n2, slope, cols, gh, gm, gb, gqkv, emit, vec
):
    rows, width = x_ref.shape
    captions = rows // seq
    hd = width // heads
    scale = hd ** (-0.5)
    hidden = wup.shape[1]
    weight = cols[:, 0:1]
    gpc_r = gpc.astype(bf16)
    acc = None
    for c in range(0, hidden, 768):
        hh = dot_t(gpc_r, wdown[c : c + 768, :])
        spread = jnp.broadcast_to(hh[:, None, :], (captions, seq, 768)).reshape(rows, 768)
        gh[:, c : c + 768] = (spread * weight * slope[:, c : c + 768].astype(f32)).astype(bf16)
        emit("up", c, dot_0(gh[:, c : c + 768], n2[...]))
    gn2 = dot_t(gh[...], wup[...])
    scaled, inverse = stats(mixed[...])
    vec(2, jnp.sum(gn2 * scaled, 0, keepdims=True), jnp.sum(gn2, 0, keepdims=True))
    spread = jnp.broadcast_to(gpc[:, None, :], (captions, seq, width)).reshape(rows, width) * weight
    gm[...] = spread + norm_back(gn2, scaled, inverse, g2[...])
    gb[...] = gm[...].astype(bf16)
    emit("out", 0, dot_0(gb[...], at[...]))
    at[...] = dot_t(gb[...], wout[...]).astype(bf16)
    first = lax.broadcasted_iota(jnp.int32, (group, 2 * hd), 1) < hd

    def attend(g, carry):
        rs = pl.ds(pl.multiple_of(g * group, 16), group)
        for hp in range(heads // 2):
            lanes = slice(hp * 2 * hd, (hp + 1) * 2 * hd)
            klanes = slice(width + lanes.start, width + lanes.stop)
            vlanes = slice(2 * width + lanes.start, 2 * width + lanes.stop)
            q2, k2, v2, ga = qkv[rs, lanes], qkv[rs, klanes], qkv[rs, vlanes], at[rs, lanes]
            dq, dk, dv = [], [], []
            for h in range(2):
                p = probs[rs, pl.ds((hp * 2 + h) * group, group)]
                dp = dot_t(jnp.where(first == (h == 0), ga, jnp.zeros_like(ga)), v2)
                ds = (p * (dp - jnp.sum(dp * p, -1, keepdims=True))).astype(bf16)
                dv.append(dot_0(p.astype(bf16), ga))
                dq.append(dot(ds, k2))
                dk.append(dot_0(ds, q2))
            gqkv[rs, lanes] = (jnp.where(first, dq[0], dq[1]) * scale).astype(bf16)
            gqkv[rs, klanes] = (jnp.where(first, dk[0], dk[1]) * scale).astype(bf16)
            gqkv[rs, vlanes] = jnp.where(first, dv[0], dv[1]).astype(bf16)
        return carry

    lax.fori_loop(0, rows // group, attend, 0)
    for c in range(3):
        emit("qkv", c * width, dot_0(gqkv[:, c * width : (c + 1) * width], n1[...]))
    gn1 = dot_t(gqkv[...], wqkv[...])
    scaled, inverse = stats(x_ref[...].astype(f32))
    vec(1, jnp.sum(gn1 * scaled, 0, keepdims=True), jnp.sum(gn1, 0, keepdims=True))
    return gm[...] + norm_back(gn1, scaled, inverse, g1[...])

def forward_call(x, mask, length, g1, s1, wqkv, wout, g2, s2, wup, wdown, heads=12):
    captions, seq, width = x.shape
    rows, hidden, group = captions * seq, wup.shape[1], 128
    def kernel(x_ref, mask_ref, length_ref, g1, s1, wqkv, wout, g2, s2, wup, wdown, pooled, count_ref, n1, qkv, probs, at, mixed, n2, slope, act, cols):
        p, count = text_forward(heads, seq, group, x_ref, mask_ref, length_ref, g1, s1, wqkv, wout, g2, s2, wup, wdown, n1, qkv, probs, at, mixed, n2, slope, act, cols)
        pooled[...] = p
        count_ref[...] = count
    S = jax.ShapeDtypeStruct
    return pl.pallas_call(kernel, name="text_forward",
        out_shape=(S((captions, width), f32), S((captions, 1), f32), S((rows, width), bf16), S((rows, 3*width), bf16), S((rows, heads*group), f32),
          S((rows, width), bf16), S((rows, width), f32), S((rows, width), bf16), S((rows, hidden), bf16), S((captions, hidden), f32), S((rows, 128), f32)),
    )(x.reshape(rows, width), mask, length[None], g1[None], s1[None], wqkv, wout, g2[None], s2[None], wup, wdown)

def backward_call(gpc, x, g1, wqkv, wout, g2, wup, wdown, n1, qkv, probs, at, mixed, n2, slope, act, cols, heads=12):
    captions, seq, width = x.shape
    rows, hidden, group = captions * seq, wup.shape[1], 128
    def kernel(gpc, x_ref, g1, wqkv, wout, g2, wup, wdown, n1, qkv, probs, at_in, mixed, n2, slope, act, cols, gx, up, out, gq, down, vecs, gh, gm, gb, gqkv, at):
        dst = {"up": up, "out": out, "qkv": gq}
        at[...] = at_in[...]
        def emit(name, row, block):
            dst[name][row:row+block.shape[0], :] = block.astype(bf16)
        def vec(which, gain, shift):
            vecs[2*which-2:2*which-1, :] = gain
            vecs[2*which-1:2*which, :] = shift
        down[...] = dot_0(act[...].astype(bf16), gpc[...].astype(bf16)).astype(bf16)
        gx[...] = text_backward(heads, seq, group, gpc[...], x_ref, g1, wqkv, wout, g2, wup, wdown, n1, qkv, probs, at, mixed, n2, slope, cols, gh, gm, gb, gqkv, emit, vec)
    S = jax.ShapeDtypeStruct
    V = pltpu.VMEM
    return pl.pallas_call(kernel, name="text_backward",
        out_shape=(S((rows, width), f32), S((hidden, width), bf16), S((width, width), bf16), S((3*width, width), bf16), S((hidden, width), bf16), S((4, width), f32)),
        scratch_shapes=[V((rows, hidden), bf16), V((rows, width), f32), V((rows, width), bf16), V((rows, 3*width), bf16), V((rows, width), bf16)],
    )(gpc, x.reshape(rows, width), g1[None], wqkv, wout, g2[None], wup, wdown, n1, qkv, probs, at, mixed, n2, slope, act, cols)


def on_device(
    image_tokens, caption_tokens, caption_mask, caption_length,
    image_gain1, image_shift1, image_qkv, image_out, image_gain2, image_shift2, image_up, image_down,
    text_gain1, text_shift1, text_qkv, text_out, text_gain2, text_shift2, text_up, text_down,
):
    both = ("row", "col")
    captions, seq, width = caption_tokens.shape
    t = 2.0 * math.sqrt(width)
    pairs = captions * lax.axis_size("row") * lax.axis_size("col")
    unit = image_unit(
        image_tokens, image_gain1, image_shift1, image_qkv, image_out,
        image_gain2, image_shift2, image_up, image_down,
    )
    images = lax.all_gather(unit, both, axis=0, tiled=True)
    pooled, count, *saved = forward_call(
        caption_tokens, caption_mask, caption_length, text_gain1, text_shift1, text_qkv, text_out,
        text_gain2, text_shift2, text_up, text_down,
    )
    inverse = lax.rsqrt(jnp.sum(pooled * pooled, -1, keepdims=True) + epsilon)
    text_unit = (pooled * inverse).astype(bf16)
    e = jnp.exp(t * dot_t(images, text_unit))
    row_sum = lax.psum(jnp.sum(e, 1), both)
    col_sum = jnp.sum(e, 0)
    grad_sim = (e * (1.0 / row_sum[:, None] + 1.0 / col_sum[None]) * (0.5 / pairs)).astype(bf16)
    grad_unit = t * dot_0(grad_sim, images) - (t / pairs) * unit.astype(f32)
    along = jnp.sum(grad_unit * pooled, -1, keepdims=True)
    grad_pooled = inverse * grad_unit - pooled * (inverse * inverse * inverse * along)
    grad_tokens, up, out, qkv, down, vecs = backward_call(
        grad_pooled / count, caption_tokens, text_gain1, text_qkv, text_out, text_gain2, text_up, text_down, *saved
    )

    def shared(g):
        part = lax.psum_scatter(g, "col", scatter_dimension=0, tiled=True)
        return lax.psum(part, "row").astype(f32)

    vecs = lax.psum(vecs, both)
    part = width // lax.axis_size("col")
    vecs = lax.dynamic_slice(vecs, (0, lax.axis_index("col") * part), (4, part))
    return (
        grad_tokens.reshape(captions, seq, width), vecs[0], vecs[1], shared(qkv).T, shared(out).T,
        vecs[2], vecs[3], shared(up).T, shared(down),
    )


def solution(mesh):
    pair = P(("row", "col"))
    return jax.shard_map(
        on_device,
        mesh=mesh,
        in_specs=(pair,) * 4 + (P(),) * 16,
        out_specs=(pair, P("col"), P("col"), P(None, "col"), P(None, "col"), P("col"), P("col"), P(None, "col"), P("col")),
        check_vma=False,
    )
```

```python
import math, functools
import jax, jax.numpy as jnp
from jax import lax
from jax.experimental import pallas as pl
from jax.experimental.pallas import tpu as pltpu
from jax.sharding import PartitionSpec as P

epsilon = 1e-06
log2e = 1.4426950408889634
inv_root2 = 0.7071067811865476
f32 = jnp.float32
bf16 = jnp.bfloat16


def dot(a, b):
    return jnp.dot(a, b, preferred_element_type=f32)


def dot_t(a, b):
    return lax.dot_general(a, b, (((1,), (1,)), ((), ())), preferred_element_type=f32)


def stats(x):
    centred = x - jnp.mean(x, -1, keepdims=True)
    inverse = lax.rsqrt(jnp.mean(centred * centred, -1, keepdims=True) + epsilon)
    return centred * inverse, inverse


def gelu(v):
    u = 0.5 * v
    return u * lax.erf(v * inv_root2) + u


def image_kernel(
    heads, x_ref, g1, s1, wqkv, wout, g2, s2, wup, wdown, out_ref,
    tok, xs, n, qkv, at, mixed, act, pooled
):
    tokens, images, width = x_ref.shape
    pad = -(-tokens // 8) * 8
    rows = images * pad
    i = pl.program_id(0)

    @pl.when(i == 0)
    def _():
        xs[...] = jnp.zeros_like(xs)

    count = tokens * images
    for j in range(width // 128):
        lanes = slice(j * 128, (j + 1) * 128)
        tok[j * count : (j + 1) * count, :] = x_ref[:, :, lanes].astype(f32).reshape(count, 128)
    for j in range(width // 128):
        for k in range(images):
            xs[k * pad : k * pad + tokens, j * 128 : (j + 1) * 128] = tok[pl.ds(j * count + k, tokens, stride=images), :]
    scaled, _ = stats(xs[...])
    n[...] = (scaled * g1[...] + s1[...]).astype(bf16)
    for c in range(3):
        cols = slice(c * width, (c + 1) * width)
        qkv[:, cols] = dot(n[...], wqkv[:, cols]).astype(bf16)

    group = 2 * pad
    hd = width // heads
    r_id = lax.broadcasted_iota(jnp.int32, (group, group), 0)
    c_id = lax.broadcasted_iota(jnp.int32, (group, group), 1)
    same = (r_id < pad) == (c_id < pad)
    inside = jnp.where(c_id < pad, c_id, c_id - pad) < tokens
    keep = same & inside
    first = lax.broadcasted_iota(jnp.int32, (group, 2 * hd), 1) < hd
    factor = hd ** (-0.5) * log2e

    def attend(g, carry):
        rs = pl.ds(pl.multiple_of(g * group, 16), group)
        for hp in range(heads // 2):
            lanes = slice(hp * 2 * hd, (hp + 1) * 2 * hd)
            q2 = qkv[rs, lanes]
            k2 = qkv[rs, slice(width + lanes.start, width + lanes.stop)]
            v2 = qkv[rs, slice(2 * width + lanes.start, 2 * width + lanes.stop)]
            outs = []
            for h in range(2):
                kh = jnp.where(first == (h == 0), k2, jnp.zeros_like(k2))
                s = jnp.where(keep, dot_t(q2, kh) * factor, -1e30)
                e = jnp.exp2(s - jnp.max(s, -1, keepdims=True))
                total = jnp.sum(e, -1, keepdims=True)
                outs.append(dot(e.astype(bf16), v2) * (1.0 / total))
            at[rs, lanes] = jnp.where(first, outs[0], outs[1]).astype(bf16)
        return carry

    lax.fori_loop(0, rows // group, attend, 0)
    mixed[...] = xs[...] + dot(at[...], wout[...])
    row = lax.broadcasted_iota(jnp.int32, (pad, 1), 0)
    valid = (row < tokens).astype(f32)
    dst = pl.ds(pl.multiple_of(i * images, 8), images)
    m3 = mixed[...].reshape(images, pad, width)
    pooled[dst, :] = jnp.sum(m3 * valid[None], 1)
    scaled, _ = stats(mixed[...])
    normed = ((scaled * g2[...] + s2[...]).reshape(images, pad, width) * valid[None]).reshape(rows, width)
    n[...] = normed.astype(bf16)
    hidden = wup.shape[1]
    step = 768
    for c in range(0, hidden, step):
        a = gelu(dot(n[...], wup[:, c : c + step]))
        act[dst, c : c + step] = jnp.sum(a.reshape(images, pad, step), 1)

    @pl.when(i == pl.num_programs(0) - 1)
    def _():
        a = act[...] * (1.0 / tokens)
        hi = a.astype(bf16)
        lo = (a - hi.astype(f32)).astype(bf16)
        count = a.shape[0]
        both = dot(jnp.concatenate([hi, lo], 0), wdown[...])
        e = pooled[...] * (1.0 / tokens) + both[:count] + both[count:]
        out_ref[...] = (e * lax.rsqrt(jnp.sum(e * e, -1, keepdims=True) + epsilon)).astype(bf16)


def image_unit(x, g1, s1, wqkv, wout, g2, s2, wup, wdown, heads=12, images=8):
    count, tokens, width = x.shape
    hidden = wup.shape[1]
    pad = -(-tokens // 8) * 8
    rows = images * pad
    full = lambda a: pl.BlockSpec(a.shape, lambda i: (0,) * a.ndim, pipeline_mode=pl.Buffered(1))
    args = (jnp.transpose(x, (1, 0, 2)), g1[None], s1[None], wqkv, wout, g2[None], s2[None], wup, wdown)
    return pl.pallas_call(
        functools.partial(image_kernel, heads),
        name="image",
        grid=(count // images,),
        out_shape=jax.ShapeDtypeStruct((count, width), bf16),
        in_specs=[pl.BlockSpec((tokens, images, width), lambda i: (0, i, 0))] + [full(a) for a in args[1:]],
        out_specs=pl.BlockSpec((count, width), lambda i: (0, 0)),
        scratch_shapes=[
            pltpu.VMEM((width // 128 * tokens * images, 128), f32),
            pltpu.VMEM((rows, width), f32),
            pltpu.VMEM((rows, width), bf16),
            pltpu.VMEM((rows, 3 * width), bf16),
            pltpu.VMEM((rows, width), bf16),
            pltpu.VMEM((rows, width), f32),
            pltpu.VMEM((count, hidden), f32),
            pltpu.VMEM((count, width), f32),
        ],
    )(*args)

def dot_0(a, b):
    return lax.dot_general(a, b, (((0,), (0,)), ((), ())), preferred_element_type=f32)


def norm_back(grad_normed, scaled, inverse, gain):
    g = grad_normed * gain
    centre = jnp.mean(g, -1, keepdims=True)
    along = jnp.mean(g * scaled, -1, keepdims=True)
    return inverse * (g - centre - scaled * along)


def token_columns(mask_ref, length_ref, seq):
    captions = mask_ref.shape[1]
    rows = captions * seq
    row = lax.broadcasted_iota(jnp.int32, (rows, captions), 0)
    lane = lax.broadcasted_iota(jnp.int32, (rows, captions), 1)
    length = length_ref[...].astype(f32)
    own = row // seq == lane
    length_t = jnp.sum(jnp.where(own, length, 0.0), -1, keepdims=True)
    spread = dot_t(jnp.where(own, 1.0, 0.0).astype(bf16), mask_ref[...].astype(f32).astype(bf16))
    row = lax.broadcasted_iota(jnp.int32, (rows, seq), 0)
    lane = lax.broadcasted_iota(jnp.int32, (rows, seq), 1)
    mask_t = jnp.sum(jnp.where(row % seq == lane, spread, 0.0), -1, keepdims=True)
    place = (lax.broadcasted_iota(jnp.int32, (rows, 1), 0) % seq).astype(f32)
    weight = jnp.where(place < length_t, mask_t, 0.0)
    count = jnp.sum(weight.reshape(captions, seq, 1), 1)
    return length_t, weight, jnp.maximum(count, 1.0)


def text_attention(heads, seq, group, width, qkv, probs, at, cols):
    hd = width // heads
    r_id = lax.broadcasted_iota(jnp.int32, (group, group), 0)
    c_id = lax.broadcasted_iota(jnp.int32, (group, group), 1)
    same = r_id // seq == c_id // seq
    place = (c_id % seq).astype(f32)
    first = lax.broadcasted_iota(jnp.int32, (group, 2 * hd), 1) < hd
    factor = hd ** (-0.5) * log2e

    def attend(g, carry):
        rs = pl.ds(pl.multiple_of(g * group, 16), group)
        keep = same & (place < cols[rs, 1:2])
        for hp in range(heads // 2):
            lanes = slice(hp * 2 * hd, (hp + 1) * 2 * hd)
            q2 = qkv[rs, lanes]
            k2 = qkv[rs, slice(width + lanes.start, width + lanes.stop)]
            v2 = qkv[rs, slice(2 * width + lanes.start, 2 * width + lanes.stop)]
            outs = []
            for h in range(2):
                kh = jnp.where(first == (h == 0), k2, jnp.zeros_like(k2))
                s = jnp.where(keep, dot_t(q2, kh) * factor, -1e30)
                e = jnp.exp2(s - jnp.max(s, -1, keepdims=True))
                p = e * (1.0 / jnp.sum(e, -1, keepdims=True))
                probs[rs, pl.ds((hp * 2 + h) * group, group)] = p
                outs.append(dot(p.astype(bf16), v2))
            at[rs, lanes] = jnp.where(first, outs[0], outs[1]).astype(bf16)
        return carry

    return attend


inv_root_2pi = 0.3989422804014327


def split_dot(a, w):
    hi = a.astype(bf16)
    lo = (a - hi.astype(f32)).astype(bf16)
    both = dot(jnp.concatenate([hi, lo], 0), w[...])
    return both[: a.shape[0]] + both[a.shape[0] :]


def text_attention_back(heads, group, width, qkv, probs, at):
    hd = width // heads
    scale = hd ** (-0.5)
    first = lax.broadcasted_iota(jnp.int32, (group, 2 * hd), 1) < hd

    def attend(g, carry):
        rs = pl.ds(pl.multiple_of(g * group, 16), group)
        for hp in range(heads // 2):
            lanes = slice(hp * 2 * hd, (hp + 1) * 2 * hd)
            klanes = slice(width + lanes.start, width + lanes.stop)
            vlanes = slice(2 * width + lanes.start, 2 * width + lanes.stop)
            q2, k2, v2, ga = qkv[rs, lanes], qkv[rs, klanes], qkv[rs, vlanes], at[rs, lanes]
            dq, dk, dv = [], [], []
            for h in range(2):
                p = probs[rs, pl.ds((hp * 2 + h) * group, group)]
                dp = dot_t(jnp.where(first == (h == 0), ga, jnp.zeros_like(ga)), v2)
                ds = (p * (dp - jnp.sum(dp * p, -1, keepdims=True))).astype(bf16)
                dv.append(dot_0(p.astype(bf16), ga))
                dq.append(dot(ds, k2))
                dk.append(dot_0(ds, q2))
            qkv[rs, lanes] = (jnp.where(first, dq[0], dq[1]) * scale).astype(bf16)
            qkv[rs, klanes] = (jnp.where(first, dk[0], dk[1]) * scale).astype(bf16)
            qkv[rs, vlanes] = jnp.where(first, dv[0], dv[1]).astype(bf16)
        return carry

    return attend


MESH = pl.DeviceIdType.MESH


def log2(n):
    return n.bit_length() - 1


def text_step(
    shape, heads,
    unit_ref, mask_ref, length_ref, g1, s1, g2, s2, x_hbm, wqkv_hbm, wout_hbm, wup_hbm, wdown_hbm,
    gx_hbm, parts_hbm, vecs_ref, images_hbm,
    x_ref, wqkv, wout, wup, wdown, n1, qkv, probs, at, mixed, n2, slope, act, cols,
    images, rowsum, rowsum_c, rowsum_cs, rowsum_r, pooled_act, act_all, gpc_own, gpc_all,
    g_up, g_rest, r_up, r_rest, d_part, d_recv, d_recv2, final, extra, vec, vec_c, vec_cs, vec_r,
    load_sem, out_sem, ag_send, ag_recv, ps_send, ps_recv, a_send, a_recv, gp_send, gp_recv,
    rs_send, rs_recv, d_send, d_recv_sem, f_send, f_recv, v_send, v_recv,
):
    R, C, captions, seq, group = shape
    rb, cb = log2(R), log2(C)
    r, c = lax.axis_index("row"), lax.axis_index("col")
    rbit = [lax.rem(lax.div(r, 1 << b), 2) for b in range(rb)]
    cbit = [lax.rem(lax.div(c, 1 << b), 2) for b in range(cb)]
    core, xh = rbit[0], rbit[1]
    rows, width = x_ref.shape
    hidden = wup.shape[1]
    half = width // 2
    sub = hidden // (4 * C)

    def flip_r(b):
        return (r + (1 - 2 * rbit[b]) * (1 << b), c)

    def flip_c(b):
        return (r, c + (1 - 2 * cbit[b]) * (1 << b))

    row_peers = [(lax.rem(r + d, R), c) for d in range(1, R)]
    col_peers = [(r, lax.rem(c + d, C)) for d in range(1, C)]

    def remote(src, dst, send, recv, to):
        return pltpu.make_async_remote_copy(
            src_ref=src, dst_ref=dst, send_sem=send, recv_sem=recv, device_id=to, device_id_type=MESH
        )

    sent = []

    def go(copy):
        copy.start()
        sent.append(copy)
        return copy

    barrier = pltpu.get_barrier_semaphore()
    for to in row_peers + col_peers:
        pl.semaphore_signal(barrier, inc=1, device_id=to, device_id_type=MESH)

    loads = []
    for k, (src, dst) in enumerate(
        ((x_hbm, x_ref), (wqkv_hbm, wqkv), (wout_hbm, wout), (wup_hbm, wup), (wdown_hbm, wdown))
    ):
        copy = pltpu.make_async_copy(src, dst, load_sem.at[k])
        copy.start()
        loads.append(copy)

    length_t, weight, count = token_columns(mask_ref, length_ref, seq)
    cols[:, 0:1] = weight
    cols[:, 1:2] = length_t
    loads[0].wait()
    pl.semaphore_wait(barrier, R + C - 2)

    mine = tuple(rbit[b] for b in reversed(range(rb))) + tuple(cbit[b] for b in reversed(range(cb)))
    part = captions // 2
    pairs = captions * R * C
    staged = len(images.shape) < 3 + rb + cb
    gather = images_hbm if staged else images
    for k in range(2):
        if staged:
            copy = pltpu.make_async_copy(unit_ref.at[pl.ds(k * part, part), :], gather.at[(k,) + mine], load_sem.at[5 + k])
            copy.start()
            loads.append(copy)
        else:
            images[(k,) + mine] = unit_ref[k * part : (k + 1) * part, :]
    if staged:
        loads[5].wait()
        loads[6].wait()

    def stage(i):
        if not staged:
            return images[...].reshape(pairs, width)
        lead = 3 + rb + cb - len(images.shape)
        where = tuple((i >> b) & 1 for b in reversed(range(lead)))
        copy = pltpu.make_async_copy(gather.at[where], images, load_sem.at[5])
        copy.start()
        copy.wait()
        return images[...].reshape(pairs >> lead, width)

    stages = pairs // math.prod(images.shape[:-1])
    order = [("c", b) for b in reversed(range(1, cb))]
    tail = [("r", b) for b in reversed(range(1, rb))]
    plans = (order + [("c", 0)] + tail + [("r", 0)], order + tail + [("c", 0)] + [("r", 0)])
    gathered = [set(), set()]
    pending = [None, None]
    phase = [0, 0]

    def gather_step():
        for k in range(2):
            if pending[k] is not None:
                pending[k].wait_recv()
                gathered[k].add(plans[k][phase[k] - 1])
                pending[k] = None
            if phase[k] < len(plans[k]):
                kind, b = plans[k][phase[k]]
                names = [("r", i) for i in reversed(range(rb))] + [("c", i) for i in reversed(range(cb))]
                where = tuple(slice(None) if nm in gathered[k] else v for nm, v in zip(names, mine))
                dst = gather.at[(k,) + where]
                src = unit_ref.at[pl.ds(k * part, part), :] if phase[k] == 0 else dst
                to = flip_r(b) if kind == "r" else flip_c(b)
                pending[k] = go(remote(src, dst, ag_send.at[k, phase[k]], ag_recv.at[k, phase[k]], to))
                phase[k] += 1

    gather_step()
    x = x_ref[...].astype(f32)
    scaled, _ = stats(x)
    n1[...] = (scaled * g1[...] + s1[...]).astype(bf16)
    loads[1].wait()
    for q in range(3):
        cut = slice(q * width, (q + 1) * width)
        qkv[:, cut] = dot(n1[...], wqkv[:, cut]).astype(bf16)
    gather_step()
    attend = text_attention(heads, seq, group, width, qkv, probs, at, cols)
    groups = rows // group
    lax.fori_loop(0, groups // 2, attend, 0)
    gather_step()
    lax.fori_loop(groups // 2, groups, attend, 0)
    gather_step()
    loads[2].wait()
    mixed[...] = x_ref[...].astype(f32) + dot(at[...], wout[...])
    scaled, _ = stats(mixed[...])
    n2[...] = (scaled * g2[...] + s2[...]).astype(bf16)
    weight = cols[:, 0:1]
    loads[3].wait()
    for f in range(0, hidden, width):
        cut = slice(f, f + width)
        h = dot(n2[...], wup[:, cut])
        phi = 0.5 + 0.5 * lax.erf(h * inv_root2)
        slope[:, cut] = (phi + h * (jnp.exp(-0.5 * h * h) * inv_root_2pi)).astype(bf16)
        act[:, cut] = jnp.sum((h * phi * weight).reshape(captions, seq, width), 1)
        if f == 2 * width:
            gather_step()
    loads[4].wait()
    pooled = jnp.sum((mixed[...] * weight).reshape(captions, seq, width), 1) + split_dot(act[...], wdown)
    pooled = pooled / count
    inverse = lax.rsqrt(jnp.sum(pooled * pooled, -1, keepdims=True) + epsilon)
    text_unit = (pooled * inverse).astype(bf16)
    span = hidden // C
    for k in range(C):
        pooled_act[k] = act[:, k * span : (k + 1) * span].astype(bf16)
    while pending[0] is not None or pending[1] is not None:
        gather_step()

    t = 2.0 * math.sqrt(width)
    sims = []
    for i in range(stages):
        every = stage(i)
        sims.append(dot_t(text_unit, every))
    e = jnp.exp2(jnp.concatenate(sims, 1) * (t * log2e))
    rowsum[...] = jnp.sum(e, 0, keepdims=True)
    first = [
        go(remote(rowsum, rowsum_c.at[d], ps_send.at[d], ps_recv.at[d], to)) for d, to in enumerate(col_peers)
    ]
    col_scale = 1.0 / jnp.sum(e, -1, keepdims=True)
    acts = []
    for d, to in enumerate(col_peers):
        acts.append(
            go(remote(pooled_act.at[lax.rem(c + d + 1, C)], act_all.at[d], a_send.at[d], a_recv.at[d], to))
        )
    act_all[C - 1] = pooled_act[c]
    total = rowsum[...]
    for d, copy in enumerate(first):
        copy.wait_recv()
        total += rowsum_c[d]
    rowsum_cs[...] = total
    second = [
        go(remote(rowsum_cs, rowsum_r.at[d], ps_send.at[C - 1 + d], ps_recv.at[C - 1 + d], to))
        for d, to in enumerate(row_peers)
    ]
    for d, copy in enumerate(second):
        copy.wait_recv()
        total += rowsum_r[d]
    grad_sim = (e * (1.0 / total + col_scale) * (0.5 / pairs)).astype(bf16)
    share = pairs // stages
    hits = sum(
        dot(grad_sim[:, i * share : (i + 1) * share], every if stages == 1 else stage(i)) for i in range(stages)
    )
    grad_unit = t * hits - (t / pairs) * unit_ref[...].astype(f32)
    along = jnp.sum(grad_unit * pooled, -1, keepdims=True)
    gpc = (inverse * grad_unit - pooled * (inverse * inverse * inverse * along)) / count
    gpc_r = gpc.astype(bf16)
    gpc_own[...] = gpc_r
    gps = [go(remote(gpc_own, gpc_all.at[d], gp_send.at[d], gp_recv.at[d], to)) for d, to in enumerate(col_peers)]
    gpc_all[C - 1] = gpc_r

    def place(buf, c_index, j, block):
        bits = tuple((c_index >> b) & 1 for b in reversed(range(cb)))
        for s in range(2):
            buf[(s, j // 2, j % 2) + bits] = block[:, s * half : (s + 1) * half].astype(bf16)

    def emit(name, row, block):
        for i in range(0, block.shape[0], sub):
            at_row = row + i
            piece = block[i : i + sub, :]
            if name == "up":
                place(g_up, at_row // (4 * sub), at_row % (4 * sub) // sub, piece)
            elif name == "out":
                place(g_rest, at_row // sub, 0, piece)
            else:
                place(g_rest, at_row // (3 * sub), 1 + at_row % (3 * sub) // sub, piece)

    class Scatter:
        def __init__(self, index, buf, recvs):
            self.index, self.buf, self.recvs = index, buf, recvs
            head = [("r", 1)], [("c", 0)]
            back = [("c", 0)], [("r", 1)]
            rest = [("c", b) for b in range(1, cb)]
            self.plan = [head[k] + back[k] + rest for k in range(2)]
            self.phase = 0
            self.copies = [None, None]

        def start(self):
            for k in range(2):
                self.copies[k] = go(
                    remote(
                        self.buf.at[1 - core, k], self.recvs[k][0],
                        rs_send.at[self.index, k, 0], rs_recv.at[self.index, k, 0], flip_r(0),
                    )
                )

        def step(self):
            p = self.phase
            last = p == len(self.plan[0])
            for k in range(2):
                self.copies[k].wait_recv()
                here = self.recvs[k][p]
                before = self.buf.at[core, k] if p == 0 else self.recvs[k][p - 1].at[self.kept[k]]
                if last:
                    final[core, xh, self.index, k] = before[...] + here[...]
                    continue
                kind, b = self.plan[k][p]
                left = [("r", 1)] + [("c", i) for i in reversed(range(cb))]
                for done in self.plan[k][:p]:
                    left.remove(done)
                axis = left.index((kind, b))
                bit = xh if kind == "r" else cbit[b]
                give = (slice(None),) * axis + (1 - bit,)
                keep = (slice(None),) * axis + (bit,)
                here[give] = before[give] + here[give]
                to = flip_r(1) if kind == "r" else flip_c(b)
                self.copies[k] = go(
                    remote(
                        here.at[give], self.recvs[k][p + 1],
                        rs_send.at[self.index, k, p + 1], rs_recv.at[self.index, k, p + 1], to,
                    )
                )
                here[keep] = before[keep] + here[keep]
                self.next_kept[k] = keep
            self.kept = list(self.next_kept)
            self.phase += 1

        kept = (None, None)
        next_kept = [None, None]

    up = Scatter(0, g_up, r_up)
    rest = Scatter(1, g_rest, r_rest)
    up.next_kept, rest.next_kept = [None, None], [None, None]

    for f in range(0, hidden, width):
        cut = slice(f, f + width)
        hh = dot_t(gpc_r, wdown[cut, :])
        spread = jnp.broadcast_to(hh[:, None, :], (captions, seq, width)).reshape(rows, width)
        slope[:, cut] = (spread * weight * slope[:, cut].astype(f32)).astype(bf16)
        emit("up", f, dot_0(slope[:, cut], n2[...]))
    up.start()
    gn2 = dot_t(slope[...], wup[...])
    scaled, inv2 = stats(mixed[...])
    vec[2:3, :] = jnp.sum(gn2 * scaled, 0, keepdims=True)
    vec[3:4, :] = jnp.sum(gn2, 0, keepdims=True)
    spread = jnp.broadcast_to(gpc[:, None, :], (captions, seq, width)).reshape(rows, width) * weight
    mixed[...] = spread + norm_back(gn2, scaled, inv2, g2[...])
    n2[...] = mixed[...].astype(bf16)
    emit("out", 0, dot_0(n2[...], at[...]))
    at[...] = dot_t(n2[...], wout[...]).astype(bf16)
    up.step()
    attend_back = text_attention_back(heads, group, width, qkv, probs, at)
    lax.fori_loop(0, groups // 2, attend_back, 0)

    for copy in acts + gps:
        copy.wait_recv()
    down = dot_0(act_all[...].reshape(C * captions, span), gpc_all[...].reshape(C * captions, width))
    for j in range(4):
        for s in range(2):
            d_part[s, j // 2, j % 2] = down[j * sub : (j + 1) * sub, s * half : (s + 1) * half].astype(bf16)
    d0 = go(remote(d_part.at[1 - core], d_recv, d_send.at[0], d_recv_sem.at[0], flip_r(0)))

    lax.fori_loop(groups // 2, groups, attend_back, 0)
    up.step()
    for q in range(3):
        emit("qkv", q * width, dot_0(qkv[:, q * width : (q + 1) * width], n1[...]))
    rest.start()
    d0.wait_recv()
    d_recv[:, 1 - xh] = d_part[core, :, 1 - xh] + d_recv[:, 1 - xh]
    d1 = go(remote(d_recv.at[:, 1 - xh], d_recv2, d_send.at[1], d_recv_sem.at[1], flip_r(1)))
    d_recv[:, xh] = d_part[core, :, xh] + d_recv[:, xh]
    gn1 = dot_t(qkv[...], wqkv[...])
    rest.step()
    scaled, inv1 = stats(x_ref[...].astype(f32))
    vec[0:1, :] = jnp.sum(gn1 * scaled, 0, keepdims=True)
    vec[1:2, :] = jnp.sum(gn1, 0, keepdims=True)
    vfirst = [go(remote(vec, vec_c.at[d], v_send.at[d], v_recv.at[d], to)) for d, to in enumerate(col_peers)]
    mixed[...] = mixed[...] + norm_back(gn1, scaled, inv1, g1[...])
    gx_out = pltpu.make_async_copy(mixed, gx_hbm, out_sem.at[0])
    gx_out.start()
    d1.wait_recv()
    final[core, xh, 2] = d_recv[:, xh] + d_recv2[...]
    while up.phase <= cb:
        up.step()
    rest.step()
    up.step()
    vtotal = vec[...]
    for d, copy in enumerate(vfirst):
        copy.wait_recv()
        vtotal += vec_c[d]
    vec_cs[...] = vtotal
    vsecond = [
        go(remote(vec_cs, vec_r.at[d], v_send.at[C - 1 + d], v_recv.at[C - 1 + d], to)) for d, to in enumerate(row_peers)
    ]
    while rest.phase <= cb:
        rest.step()
    rest.step()
    for b in range(2, rb):
        swap = remote(final.at[core, xh], extra.at[b - 2], f_send.at[b], f_recv.at[b], flip_r(b))
        swap.start()
        swap.wait()
        final[core, xh] = final[core, xh] + extra[b - 2]
    f0 = go(remote(final.at[core, xh], final.at[core, xh], f_send.at[0], f_recv.at[0], flip_r(1)))
    for d, copy in enumerate(vsecond):
        copy.wait_recv()
        vtotal += vec_r[d]
    vecs_ref[...] = vtotal
    f0.wait_recv()
    f1 = go(remote(final.at[core], final.at[core], f_send.at[1], f_recv.at[1], flip_r(0)))
    f1.wait_recv()
    parts_out = pltpu.make_async_copy(final, parts_hbm, out_sem.at[1])
    parts_out.start()
    for copy in sent:
        copy.wait_send()
    gx_out.wait()
    parts_out.wait()


def text_call(R, C, unit, tokens, mask, length, g1, s1, wqkv, wout, g2, s2, wup, wdown, heads=12, group=128):
    captions, seq, width = tokens.shape
    rows, hidden = captions * seq, wup.shape[1]
    rb, cb = log2(R), log2(C)
    half, sub, span = width // 2, hidden // (4 * C), hidden // C
    V, S, D = pltpu.VMEM, jax.ShapeDtypeStruct, pltpu.SemaphoreType.DMA
    pairs = captions * R * C
    bits_c = (2,) * cb

    dims, tail = 1 + rb + cb, (captions // 2, width)
    lead = max(log2(pairs // 1024), 0)
    held_dims, staged_dims = dims - lead, dims if lead else 0

    def recvs():
        out = []
        for k in range(2):
            full = [("r", 1)] + [("c", b) for b in reversed(range(cb))]
            plan = ([("r", 1), ("c", 0)] if k == 0 else [("c", 0), ("r", 1)]) + [("c", b) for b in range(1, cb)]
            out.append([V((2,) * (len(full) - p) + (sub, half), bf16) for p in range(len(plan) + 1)])
        return out

    vm = pl.BlockSpec(memory_space=pltpu.VMEM)
    hbm = pl.BlockSpec(memory_space=pl.ANY)
    out = pl.pallas_call(
        functools.partial(text_step, (R, C, captions, seq, group), heads),
        name="text",
        in_specs=[vm] * 7 + [hbm] * 5,
        out_specs=(hbm, hbm, vm, hbm),
        out_shape=(S((rows, width), f32), S((2, 2, 3, 2, sub, half), bf16), S((4, width), f32), S((2,) * staged_dims + tail, bf16)),
        scratch_shapes=[
            V((rows, width), bf16), V(wqkv.shape, bf16), V(wout.shape, bf16), V(wup.shape, bf16), V(wdown.shape, bf16),
            V((rows, width), bf16), V((rows, 3 * width), bf16), V((rows, heads * group), f32), V((rows, width), bf16),
            V((rows, width), f32), V((rows, width), bf16), V((rows, hidden), bf16), V((captions, hidden), f32), V((rows, 128), f32),
            V((2,) * held_dims + tail, bf16),
            V((1, pairs), f32), V((C - 1, 1, pairs), f32), V((1, pairs), f32), V((R - 1, 1, pairs), f32),
            V((C, captions, span), bf16), V((C, captions, span), bf16), V((captions, width), bf16), V((C, captions, width), bf16),
            V((2, 2, 2) + bits_c + (sub, half), bf16), V((2, 2, 2) + bits_c + (sub, half), bf16), recvs(), recvs(),
            V((2, 2, 2, sub, half), bf16), V((2, 2, sub, half), bf16), V((2, sub, half), bf16),
            V((2, 2, 3, 2, sub, half), bf16), V((max(rb - 2, 1), 3, 2, sub, half), bf16),
            V((4, width), f32), V((C - 1, 4, width), f32), V((4, width), f32), V((R - 1, 4, width), f32),
            D((7,)), D((2,)), D((2, rb + cb)), D((2, rb + cb)), D((R + C - 2,)), D((R + C - 2,)),
            D((C - 1,)), D((C - 1,)), D((C - 1,)), D((C - 1,)),
            D((2, 2, cb + 2)), D((2, 2, cb + 2)), D((2,)), D((2,)), D((max(rb, 2),)), D((max(rb, 2),)), D((R + C - 2,)), D((R + C - 2,)),
        ],
        compiler_params=pltpu.CompilerParams(collective_id=0, has_side_effects=True, vmem_limit_bytes=67043328),
    )(unit, mask.T, length[None], g1[None], s1[None], g2[None], s2[None], tokens.reshape(rows, width), wqkv, wout, wup, wdown)
    return out[:3]


def finish_kernel(col_size, parts, vecs, shift, up, out, qkv, down, v0, v1, v2, v3):
    sub, half = parts.shape[-2:]

    def block(m, j):
        return jnp.concatenate([parts[0, j % 2, m, j // 2], parts[1, j % 2, m, j // 2]], -1).astype(f32)

    for j in range(4):
        down[j * sub : (j + 1) * sub, :] = block(2, j)
    up[...] = jnp.concatenate([block(0, j) for j in range(4)], 0).T
    out[...] = block(1, 0).T
    qkv[...] = jnp.concatenate([block(1, j) for j in (1, 2, 3)], 0).T
    width = vecs.shape[1]
    share = width // col_size
    lane = lax.broadcasted_iota(jnp.int32, (width, share), 1)
    row = lax.broadcasted_iota(jnp.int32, (width, share), 0)
    pick = jnp.where(row == lane + shift[0], 1.0, 0.0)
    own = jnp.dot(vecs[...], pick, precision=lax.Precision.HIGHEST, preferred_element_type=f32)
    for k, v in enumerate((v0, v1, v2, v3)):
        v[...] = own[k : k + 1, :]


def finish_call(C, parts, vecs):
    sub, half = parts.shape[-2:]
    width = 2 * half
    share = width // C
    S = jax.ShapeDtypeStruct
    shift = (lax.axis_index("col") * share).astype(jnp.int32)[None]
    vm = pl.BlockSpec(memory_space=pltpu.VMEM)
    return pl.pallas_call(
        functools.partial(finish_kernel, C),
        name="finish",
        in_specs=[vm, vm, pl.BlockSpec(memory_space=pltpu.SMEM)],
        out_specs=(vm,) * 8,
        out_shape=(
            S((width, 4 * sub), f32), S((width, sub), f32), S((width, 3 * sub), f32), S((4 * sub, width), f32),
        ) + (S((1, share), f32),) * 4,
    )(parts, vecs, shift)


def on_device(
    image_tokens, caption_tokens, caption_mask, caption_length,
    image_gain1, image_shift1, image_qkv, image_out, image_gain2, image_shift2, image_up, image_down,
    text_gain1, text_shift1, text_qkv, text_out, text_gain2, text_shift2, text_up, text_down,
):
    R, C = lax.axis_size("row"), lax.axis_size("col")
    unit = image_unit(
        image_tokens, image_gain1, image_shift1, image_qkv, image_out,
        image_gain2, image_shift2, image_up, image_down,
    )
    grad_tokens, parts, vecs = text_call(
        R, C, unit, caption_tokens, caption_mask, caption_length, text_gain1, text_shift1, text_qkv, text_out,
        text_gain2, text_shift2, text_up, text_down,
    )
    up, out, qkv, down, gain1, shift1, gain2, shift2 = finish_call(C, parts, vecs)
    return (
        grad_tokens.reshape(caption_tokens.shape), gain1[0], shift1[0], qkv, out, gain2[0], shift2[0], up, down,
    )


def solution(mesh):
    pair = P(("row", "col"))
    return jax.shard_map(
        on_device,
        mesh=mesh,
        in_specs=(pair,) * 4 + (P(),) * 16,
        out_specs=(pair, P("col"), P("col"), P(None, "col"), P(None, "col"), P("col"), P("col"), P(None, "col"), P("col")),
        check_vma=False,
    )
```

```python
import math, functools
import jax, jax.numpy as jnp
from jax import lax
from jax.experimental import pallas as pl
from jax.experimental.pallas import tpu as pltpu
from jax.sharding import PartitionSpec as P

epsilon = 1e-06
log2e = 1.4426950408889634
inv_root2 = 0.7071067811865476
f32 = jnp.float32
bf16 = jnp.bfloat16


def dot(a, b):
    return jnp.dot(a, b, preferred_element_type=f32)


def dot_t(a, b):
    return lax.dot_general(a, b, (((1,), (1,)), ((), ())), preferred_element_type=f32)


def stats(x):
    centred = x - jnp.mean(x, -1, keepdims=True)
    inverse = lax.rsqrt(jnp.mean(centred * centred, -1, keepdims=True) + epsilon)
    return centred * inverse, inverse


def gelu(v):
    u = 0.5 * v
    return u * lax.erf(v * inv_root2) + u


def image_kernel(
    heads, x_ref, g1, s1, wqkv, wout, g2, s2, wup, wdown, out_ref,
    tok, xs, n, qkv, at, mixed, act, pooled
):
    tokens, images, width = x_ref.shape
    pad = -(-tokens // 8) * 8
    rows = images * pad
    i = pl.program_id(0)

    @pl.when(i == 0)
    def _():
        xs[...] = jnp.zeros_like(xs)

    count = tokens * images
    for j in range(width // 128):
        lanes = slice(j * 128, (j + 1) * 128)
        tok[j * count : (j + 1) * count, :] = x_ref[:, :, lanes].astype(f32).reshape(count, 128)
    for j in range(width // 128):
        for k in range(images):
            xs[k * pad : k * pad + tokens, j * 128 : (j + 1) * 128] = tok[pl.ds(j * count + k, tokens, stride=images), :]
    scaled, _ = stats(xs[...])
    n[...] = (scaled * g1[...][None] + s1[...][None]).astype(bf16)
    for c in range(3):
        cols = slice(c * width, (c + 1) * width)
        qkv[:, cols] = dot(n[...], wqkv[:, cols]).astype(bf16)

    group = 2 * pad
    hd = width // heads
    r_id = lax.broadcasted_iota(jnp.int32, (group, group), 0)
    c_id = lax.broadcasted_iota(jnp.int32, (group, group), 1)
    same = (r_id < pad) == (c_id < pad)
    inside = jnp.where(c_id < pad, c_id, c_id - pad) < tokens
    keep = same & inside
    first = lax.broadcasted_iota(jnp.int32, (group, 2 * hd), 1) < hd
    factor = hd ** (-0.5) * log2e

    def attend(g, carry):
        rs = pl.ds(pl.multiple_of(g * group, 16), group)
        for hp in range(heads // 2):
            lanes = slice(hp * 2 * hd, (hp + 1) * 2 * hd)
            q2 = qkv[rs, lanes]
            k2 = qkv[rs, slice(width + lanes.start, width + lanes.stop)]
            v2 = qkv[rs, slice(2 * width + lanes.start, 2 * width + lanes.stop)]
            outs = []
            for h in range(2):
                kh = jnp.where(first == (h == 0), k2, jnp.zeros_like(k2))
                s = jnp.where(keep, dot_t(q2, kh) * factor, -1e30)
                e = jnp.exp2(s - jnp.max(s, -1, keepdims=True))
                total = jnp.sum(e, -1, keepdims=True)
                outs.append(dot(e.astype(bf16), v2) * (1.0 / total))
            at[rs, lanes] = jnp.where(first, outs[0], outs[1]).astype(bf16)
        return carry

    lax.fori_loop(0, rows // group, attend, 0)
    mixed[...] = xs[...] + dot(at[...], wout[...])
    row = lax.broadcasted_iota(jnp.int32, (pad, 1), 0)
    valid = (row < tokens).astype(f32)
    dst = pl.ds(pl.multiple_of(i * images, 8), images)
    m3 = mixed[...].reshape(images, pad, width)
    pooled[dst, :] = jnp.sum(m3 * valid[None], 1)
    scaled, _ = stats(mixed[...])
    normed = ((scaled * g2[...][None] + s2[...][None]).reshape(images, pad, width) * valid[None]).reshape(rows, width)
    n[...] = normed.astype(bf16)
    hidden = wup.shape[1]
    step = 768
    for c in range(0, hidden, step):
        a = gelu(dot(n[...], wup[:, c : c + step]))
        act[dst, c : c + step] = jnp.sum(a.reshape(images, pad, step), 1)

    @pl.when(i == pl.num_programs(0) - 1)
    def _():
        a = act[...] * (1.0 / tokens)
        hi = a.astype(bf16)
        lo = (a - hi.astype(f32)).astype(bf16)
        count = a.shape[0]
        both = dot(jnp.concatenate([hi, lo], 0), wdown[...])
        e = pooled[...] * (1.0 / tokens) + both[:count] + both[count:]
        out_ref[...] = (e * lax.rsqrt(jnp.sum(e * e, -1, keepdims=True) + epsilon)).astype(bf16)


def image_unit(x, g1, s1, wqkv, wout, g2, s2, wup, wdown, heads=12, images=8):
    count, tokens, width = x.shape
    hidden = wup.shape[1]
    pad = -(-tokens // 8) * 8
    rows = images * pad
    full = lambda a: pl.BlockSpec(a.shape, lambda i: (0,) * a.ndim, pipeline_mode=pl.Buffered(1))
    args = (jnp.transpose(x, (1, 0, 2)), g1, s1, wqkv, wout, g2, s2, wup, wdown)
    return pl.pallas_call(
        functools.partial(image_kernel, heads),
        name="image",
        grid=(count // images,),
        out_shape=jax.ShapeDtypeStruct((count, width), bf16),
        in_specs=[pl.BlockSpec((tokens, images, width), lambda i: (0, i, 0))] + [full(a) for a in args[1:]],
        out_specs=pl.BlockSpec((count, width), lambda i: (0, 0)),
        scratch_shapes=[
            pltpu.VMEM((width // 128 * tokens * images, 128), f32),
            pltpu.VMEM((rows, width), f32),
            pltpu.VMEM((rows, width), bf16),
            pltpu.VMEM((rows, 3 * width), bf16),
            pltpu.VMEM((rows, width), bf16),
            pltpu.VMEM((rows, width), f32),
            pltpu.VMEM((count, hidden), f32),
            pltpu.VMEM((count, width), f32),
        ],
    )(*args)

def dot_0(a, b):
    return lax.dot_general(a, b, (((0,), (0,)), ((), ())), preferred_element_type=f32)


def norm_back(grad_normed, scaled, inverse, gain):
    g = grad_normed * gain
    centre = jnp.mean(g, -1, keepdims=True)
    along = jnp.mean(g * scaled, -1, keepdims=True)
    return inverse * (g - centre - scaled * along)


def token_columns(mask_ref, length_ref, seq):
    captions = mask_ref.shape[1]
    rows = captions * seq
    row = lax.broadcasted_iota(jnp.int32, (rows, captions), 0)
    lane = lax.broadcasted_iota(jnp.int32, (rows, captions), 1)
    length = length_ref[...].astype(f32)
    own = row // seq == lane
    length_t = jnp.sum(jnp.where(own, length, 0.0), -1, keepdims=True)
    spread = dot_t(jnp.where(own, 1.0, 0.0).astype(bf16), mask_ref[...].astype(f32).astype(bf16))
    row = lax.broadcasted_iota(jnp.int32, (rows, seq), 0)
    lane = lax.broadcasted_iota(jnp.int32, (rows, seq), 1)
    mask_t = jnp.sum(jnp.where(row % seq == lane, spread, 0.0), -1, keepdims=True)
    place = (lax.broadcasted_iota(jnp.int32, (rows, 1), 0) % seq).astype(f32)
    weight = jnp.where(place < length_t, mask_t, 0.0)
    count = jnp.sum(weight.reshape(captions, seq, 1), 1)
    return length_t, weight, jnp.maximum(count, 1.0)


def text_attention(heads, seq, group, width, qkv, probs, at, cols):
    hd = width // heads
    r_id = lax.broadcasted_iota(jnp.int32, (group, group), 0)
    c_id = lax.broadcasted_iota(jnp.int32, (group, group), 1)
    same = r_id // seq == c_id // seq
    place = (c_id % seq).astype(f32)
    first = lax.broadcasted_iota(jnp.int32, (group, 2 * hd), 1) < hd
    factor = hd ** (-0.5) * log2e

    def attend(g, carry):
        rs = pl.ds(pl.multiple_of(g * group, 16), group)
        keep = same & (place < cols[rs, 1:2])
        for hp in range(heads // 2):
            lanes = slice(hp * 2 * hd, (hp + 1) * 2 * hd)
            q2 = qkv[rs, lanes]
            k2 = qkv[rs, slice(width + lanes.start, width + lanes.stop)]
            v2 = qkv[rs, slice(2 * width + lanes.start, 2 * width + lanes.stop)]
            outs = []
            for h in range(2):
                kh = jnp.where(first == (h == 0), k2, jnp.zeros_like(k2))
                s = jnp.where(keep, dot_t(q2, kh) * factor, -1e30)
                e = jnp.exp2(s - jnp.max(s, -1, keepdims=True))
                p = e * (1.0 / jnp.sum(e, -1, keepdims=True))
                probs[rs, pl.ds((hp * 2 + h) * group, group)] = p
                outs.append(dot(p.astype(bf16), v2))
            at[rs, lanes] = jnp.where(first, outs[0], outs[1]).astype(bf16)
        return carry

    return attend


inv_root_2pi = 0.3989422804014327


def split_dot(a, w):
    hi = a.astype(bf16)
    lo = (a - hi.astype(f32)).astype(bf16)
    both = dot(jnp.concatenate([hi, lo], 0), w[...])
    return both[: a.shape[0]] + both[a.shape[0] :]


def text_attention_back(heads, group, width, qkv, probs, at):
    hd = width // heads
    scale = hd ** (-0.5)
    first = lax.broadcasted_iota(jnp.int32, (group, 2 * hd), 1) < hd

    def attend(g, carry):
        rs = pl.ds(pl.multiple_of(g * group, 16), group)
        for hp in range(heads // 2):
            lanes = slice(hp * 2 * hd, (hp + 1) * 2 * hd)
            klanes = slice(width + lanes.start, width + lanes.stop)
            vlanes = slice(2 * width + lanes.start, 2 * width + lanes.stop)
            q2, k2, v2, ga = qkv[rs, lanes], qkv[rs, klanes], qkv[rs, vlanes], at[rs, lanes]
            dq, dk, dv = [], [], []
            for h in range(2):
                p = probs[rs, pl.ds((hp * 2 + h) * group, group)]
                dp = dot_t(jnp.where(first == (h == 0), ga, jnp.zeros_like(ga)), v2)
                ds = (p * (dp - jnp.sum(dp * p, -1, keepdims=True))).astype(bf16)
                dv.append(dot_0(p.astype(bf16), ga))
                dq.append(dot(ds, k2))
                dk.append(dot_0(ds, q2))
            qkv[rs, lanes] = (jnp.where(first, dq[0], dq[1]) * scale).astype(bf16)
            qkv[rs, klanes] = (jnp.where(first, dk[0], dk[1]) * scale).astype(bf16)
            qkv[rs, vlanes] = jnp.where(first, dv[0], dv[1]).astype(bf16)
        return carry

    return attend


MESH = pl.DeviceIdType.MESH


def log2(n):
    return n.bit_length() - 1


def text_step(
    shape, heads,
    unit_ref, mask_ref, length_ref, g1, s1, g2, s2, x_hbm, wqkv_hbm, wout_hbm, wup_hbm, wdown_hbm,
    gx_hbm, parts_hbm, vecs_ref, images_hbm,
    x_ref, wqkv, wout, wup, wdown, n1, qkv, probs, at, mixed, n2, slope, act, cols,
    images, rowsum, rowsum_c, rowsum_cs, rowsum_r, pooled_act, act_all, gpc_own, gpc_all,
    g_up, g_rest, r_up, r_rest, d_part, d_recv, d_recv2, final, extra, vec, vec_c, vec_cs, vec_r,
    load_sem, out_sem, ag_send, ag_recv, ps_send, ps_recv, a_send, a_recv, gp_send, gp_recv,
    rs_send, rs_recv, d_send, d_recv_sem, f_send, f_recv, v_send, v_recv,
):
    R, C, captions, seq, group = shape
    rb, cb = log2(R), log2(C)
    r, c = lax.axis_index("row"), lax.axis_index("col")
    rbit = [lax.rem(lax.div(r, 1 << b), 2) for b in range(rb)]
    cbit = [lax.rem(lax.div(c, 1 << b), 2) for b in range(cb)]
    core, xh = rbit[0], rbit[1]
    rows, width = x_ref.shape
    hidden = wup.shape[1]
    half = width // 2
    sub = hidden // (4 * C)

    def flip_r(b):
        return (r + (1 - 2 * rbit[b]) * (1 << b), c)

    def flip_c(b):
        return (r, c + (1 - 2 * cbit[b]) * (1 << b))

    row_peers = [(lax.rem(r + d, R), c) for d in range(1, R)]
    col_peers = [(r, lax.rem(c + d, C)) for d in range(1, C)]

    def remote(src, dst, send, recv, to):
        return pltpu.make_async_remote_copy(
            src_ref=src, dst_ref=dst, send_sem=send, recv_sem=recv, device_id=to, device_id_type=MESH
        )

    sent = []

    def go(copy):
        copy.start()
        sent.append(copy)
        return copy

    barrier = pltpu.get_barrier_semaphore()
    for to in row_peers + col_peers:
        pl.semaphore_signal(barrier, inc=1, device_id=to, device_id_type=MESH)

    loads = []
    for k, (src, dst) in enumerate(
        ((x_hbm, x_ref), (wqkv_hbm, wqkv), (wout_hbm, wout), (wup_hbm, wup), (wdown_hbm, wdown))
    ):
        copy = pltpu.make_async_copy(src, dst, load_sem.at[k])
        copy.start()
        loads.append(copy)

    length_t, weight, count = token_columns(mask_ref, length_ref, seq)
    cols[:, 0:1] = weight
    cols[:, 1:2] = length_t
    loads[0].wait()
    pl.semaphore_wait(barrier, R + C - 2)

    mine = tuple(rbit[b] for b in reversed(range(rb))) + tuple(cbit[b] for b in reversed(range(cb)))
    part = captions // 2
    pairs = captions * R * C
    staged = len(images.shape) < 3 + rb + cb
    gather = images_hbm if staged else images
    for k in range(2):
        if staged:
            copy = pltpu.make_async_copy(unit_ref.at[pl.ds(k * part, part), :], gather.at[(k,) + mine], load_sem.at[5 + k])
            copy.start()
            loads.append(copy)
        else:
            images[(k,) + mine] = unit_ref[k * part : (k + 1) * part, :]
    if staged:
        loads[5].wait()
        loads[6].wait()

    def stage(i):
        if not staged:
            return images[...].reshape(pairs, width)
        lead = 3 + rb + cb - len(images.shape)
        where = tuple((i >> b) & 1 for b in reversed(range(lead)))
        copy = pltpu.make_async_copy(gather.at[where], images, load_sem.at[5])
        copy.start()
        copy.wait()
        return images[...].reshape(pairs >> lead, width)

    stages = pairs // math.prod(images.shape[:-1])
    order = [("c", b) for b in reversed(range(1, cb))]
    tail = [("r", b) for b in reversed(range(1, rb))]
    plans = (order + [("c", 0)] + tail + [("r", 0)], order + tail + [("c", 0)] + [("r", 0)])
    gathered = [set(), set()]
    pending = [None, None]
    phase = [0, 0]

    def gather_step():
        for k in range(2):
            if pending[k] is not None:
                pending[k].wait_recv()
                gathered[k].add(plans[k][phase[k] - 1])
                pending[k] = None
            if phase[k] < len(plans[k]):
                kind, b = plans[k][phase[k]]
                names = [("r", i) for i in reversed(range(rb))] + [("c", i) for i in reversed(range(cb))]
                where = tuple(slice(None) if nm in gathered[k] else v for nm, v in zip(names, mine))
                dst = gather.at[(k,) + where]
                src = unit_ref.at[pl.ds(k * part, part), :] if phase[k] == 0 else dst
                to = flip_r(b) if kind == "r" else flip_c(b)
                pending[k] = go(remote(src, dst, ag_send.at[k, phase[k]], ag_recv.at[k, phase[k]], to))
                phase[k] += 1

    gather_step()
    x = x_ref[...].astype(f32)
    scaled, _ = stats(x)
    n1[...] = (scaled * g1[...][None] + s1[...][None]).astype(bf16)
    loads[1].wait()
    for q in range(3):
        cut = slice(q * width, (q + 1) * width)
        qkv[:, cut] = dot(n1[...], wqkv[:, cut]).astype(bf16)
    gather_step()
    attend = text_attention(heads, seq, group, width, qkv, probs, at, cols)
    groups = rows // group
    lax.fori_loop(0, groups // 2, attend, 0)
    gather_step()
    lax.fori_loop(groups // 2, groups, attend, 0)
    gather_step()
    loads[2].wait()
    mixed[...] = x_ref[...].astype(f32) + dot(at[...], wout[...])
    scaled, _ = stats(mixed[...])
    n2[...] = (scaled * g2[...][None] + s2[...][None]).astype(bf16)
    weight = cols[:, 0:1]
    loads[3].wait()
    for f in range(0, hidden, width):
        cut = slice(f, f + width)
        h = dot(n2[...], wup[:, cut])
        phi = 0.5 + 0.5 * lax.erf(h * inv_root2)
        slope[:, cut] = (phi + h * (jnp.exp(-0.5 * h * h) * inv_root_2pi)).astype(bf16)
        act[:, cut] = jnp.sum((h * phi * weight).reshape(captions, seq, width), 1)
        if f == 2 * width:
            gather_step()
    loads[4].wait()
    pooled = jnp.sum((mixed[...] * weight).reshape(captions, seq, width), 1) + split_dot(act[...], wdown)
    pooled = pooled / count
    inverse = lax.rsqrt(jnp.sum(pooled * pooled, -1, keepdims=True) + epsilon)
    text_unit = (pooled * inverse).astype(bf16)
    span = hidden // C
    for k in range(C):
        pooled_act[k] = act[:, k * span : (k + 1) * span].astype(bf16)
    while pending[0] is not None or pending[1] is not None:
        gather_step()

    t = 2.0 * math.sqrt(width)
    sims = []
    for i in range(stages):
        every = stage(i)
        sims.append(dot_t(text_unit, every))
    e = jnp.exp2(jnp.concatenate(sims, 1) * (t * log2e))
    rowsum[...] = jnp.sum(e, 0, keepdims=True)
    first = [
        go(remote(rowsum, rowsum_c.at[d], ps_send.at[d], ps_recv.at[d], to)) for d, to in enumerate(col_peers)
    ]
    col_scale = 1.0 / jnp.sum(e, -1, keepdims=True)
    acts = []
    for d, to in enumerate(col_peers):
        acts.append(
            go(remote(pooled_act.at[lax.rem(c + d + 1, C)], act_all.at[d], a_send.at[d], a_recv.at[d], to))
        )
    act_all[C - 1] = pooled_act[c]
    total = rowsum[...]
    for d, copy in enumerate(first):
        copy.wait_recv()
        total += rowsum_c[d]
    rowsum_cs[...] = total
    second = [
        go(remote(rowsum_cs, rowsum_r.at[d], ps_send.at[C - 1 + d], ps_recv.at[C - 1 + d], to))
        for d, to in enumerate(row_peers)
    ]
    for d, copy in enumerate(second):
        copy.wait_recv()
        total += rowsum_r[d]
    grad_sim = (e * (1.0 / total + col_scale) * (0.5 / pairs)).astype(bf16)
    share = pairs // stages
    hits = sum(
        dot(grad_sim[:, i * share : (i + 1) * share], every if stages == 1 else stage(i)) for i in range(stages)
    )
    grad_unit = t * hits - (t / pairs) * unit_ref[...].astype(f32)
    along = jnp.sum(grad_unit * pooled, -1, keepdims=True)
    gpc = (inverse * grad_unit - pooled * (inverse * inverse * inverse * along)) / count
    gpc_r = gpc.astype(bf16)
    gpc_own[...] = gpc_r
    gps = [go(remote(gpc_own, gpc_all.at[d], gp_send.at[d], gp_recv.at[d], to)) for d, to in enumerate(col_peers)]
    gpc_all[C - 1] = gpc_r

    def place(buf, c_index, j, block):
        bits = tuple((c_index >> b) & 1 for b in reversed(range(cb)))
        for s in range(2):
            buf[(s, j // 2, j % 2) + bits] = block[:, s * half : (s + 1) * half].astype(bf16)

    def emit(name, row, block):
        for i in range(0, block.shape[0], sub):
            at_row = row + i
            piece = block[i : i + sub, :]
            if name == "up":
                place(g_up, at_row // (4 * sub), at_row % (4 * sub) // sub, piece)
            elif name == "out":
                place(g_rest, at_row // sub, 0, piece)
            else:
                place(g_rest, at_row // (3 * sub), 1 + at_row % (3 * sub) // sub, piece)

    class Scatter:
        def __init__(self, index, buf, recvs):
            self.index, self.buf, self.recvs = index, buf, recvs
            head = [("r", 1)], [("c", 0)]
            back = [("c", 0)], [("r", 1)]
            rest = [("c", b) for b in range(1, cb)]
            self.plan = [head[k] + back[k] + rest for k in range(2)]
            self.phase = 0
            self.copies = [None, None]

        def start(self):
            for k in range(2):
                self.copies[k] = go(
                    remote(
                        self.buf.at[1 - core, k], self.recvs[k][0],
                        rs_send.at[self.index, k, 0], rs_recv.at[self.index, k, 0], flip_r(0),
                    )
                )

        def step(self):
            p = self.phase
            last = p == len(self.plan[0])
            for k in range(2):
                self.copies[k].wait_recv()
                here = self.recvs[k][p]
                before = self.buf.at[core, k] if p == 0 else self.recvs[k][p - 1].at[self.kept[k]]
                if last:
                    final[core, xh, self.index, k] = before[...] + here[...]
                    continue
                kind, b = self.plan[k][p]
                left = [("r", 1)] + [("c", i) for i in reversed(range(cb))]
                for done in self.plan[k][:p]:
                    left.remove(done)
                axis = left.index((kind, b))
                bit = xh if kind == "r" else cbit[b]
                give = (slice(None),) * axis + (1 - bit,)
                keep = (slice(None),) * axis + (bit,)
                here[give] = before[give] + here[give]
                to = flip_r(1) if kind == "r" else flip_c(b)
                self.copies[k] = go(
                    remote(
                        here.at[give], self.recvs[k][p + 1],
                        rs_send.at[self.index, k, p + 1], rs_recv.at[self.index, k, p + 1], to,
                    )
                )
                here[keep] = before[keep] + here[keep]
                self.next_kept[k] = keep
            self.kept = list(self.next_kept)
            self.phase += 1

        kept = (None, None)
        next_kept = [None, None]

    up = Scatter(0, g_up, r_up)
    rest = Scatter(1, g_rest, r_rest)
    up.next_kept, rest.next_kept = [None, None], [None, None]

    for f in range(0, hidden, width):
        cut = slice(f, f + width)
        hh = dot_t(gpc_r, wdown[cut, :])
        spread = jnp.broadcast_to(hh[:, None, :], (captions, seq, width)).reshape(rows, width)
        slope[:, cut] = (spread * weight * slope[:, cut].astype(f32)).astype(bf16)
        emit("up", f, dot_0(slope[:, cut], n2[...]))
    up.start()
    gn2 = dot_t(slope[...], wup[...])
    scaled, inv2 = stats(mixed[...])
    vec[2:3, :] = jnp.sum(gn2 * scaled, 0, keepdims=True)
    vec[3:4, :] = jnp.sum(gn2, 0, keepdims=True)
    spread = jnp.broadcast_to(gpc[:, None, :], (captions, seq, width)).reshape(rows, width) * weight
    mixed[...] = spread + norm_back(gn2, scaled, inv2, g2[...][None])
    n2[...] = mixed[...].astype(bf16)
    emit("out", 0, dot_0(n2[...], at[...]))
    at[...] = dot_t(n2[...], wout[...]).astype(bf16)
    up.step()
    attend_back = text_attention_back(heads, group, width, qkv, probs, at)
    lax.fori_loop(0, groups // 2, attend_back, 0)

    for copy in acts + gps:
        copy.wait_recv()
    down = dot_0(act_all[...].reshape(C * captions, span), gpc_all[...].reshape(C * captions, width))
    for j in range(4):
        for s in range(2):
            d_part[s, j // 2, j % 2] = down[j * sub : (j + 1) * sub, s * half : (s + 1) * half].astype(bf16)
    d0 = go(remote(d_part.at[1 - core], d_recv, d_send.at[0], d_recv_sem.at[0], flip_r(0)))

    lax.fori_loop(groups // 2, groups, attend_back, 0)
    up.step()
    for q in range(3):
        emit("qkv", q * width, dot_0(qkv[:, q * width : (q + 1) * width], n1[...]))
    rest.start()
    d0.wait_recv()
    d_recv[:, 1 - xh] = d_part[core, :, 1 - xh] + d_recv[:, 1 - xh]
    d1 = go(remote(d_recv.at[:, 1 - xh], d_recv2, d_send.at[1], d_recv_sem.at[1], flip_r(1)))
    d_recv[:, xh] = d_part[core, :, xh] + d_recv[:, xh]
    gn1 = dot_t(qkv[...], wqkv[...])
    rest.step()
    scaled, inv1 = stats(x_ref[...].astype(f32))
    vec[0:1, :] = jnp.sum(gn1 * scaled, 0, keepdims=True)
    vec[1:2, :] = jnp.sum(gn1, 0, keepdims=True)
    vfirst = [go(remote(vec, vec_c.at[d], v_send.at[d], v_recv.at[d], to)) for d, to in enumerate(col_peers)]
    mixed[...] = mixed[...] + norm_back(gn1, scaled, inv1, g1[...][None])
    gx_out = pltpu.make_async_copy(mixed, gx_hbm, out_sem.at[0])
    gx_out.start()
    d1.wait_recv()
    final[core, xh, 2] = d_recv[:, xh] + d_recv2[...]
    while up.phase <= cb:
        up.step()
    rest.step()
    up.step()
    vtotal = vec[...]
    for d, copy in enumerate(vfirst):
        copy.wait_recv()
        vtotal += vec_c[d]
    vec_cs[...] = vtotal
    vsecond = [
        go(remote(vec_cs, vec_r.at[d], v_send.at[C - 1 + d], v_recv.at[C - 1 + d], to)) for d, to in enumerate(row_peers)
    ]
    while rest.phase <= cb:
        rest.step()
    rest.step()
    for b in range(2, rb):
        swap = remote(final.at[core, xh], extra.at[b - 2], f_send.at[b], f_recv.at[b], flip_r(b))
        swap.start()
        swap.wait()
        final[core, xh] = final[core, xh] + extra[b - 2]
    f0 = go(remote(final.at[core, xh], final.at[core, xh], f_send.at[0], f_recv.at[0], flip_r(1)))
    for d, copy in enumerate(vsecond):
        copy.wait_recv()
        vtotal += vec_r[d]
    vecs_ref[...] = vtotal
    f0.wait_recv()
    f1 = go(remote(final.at[core], final.at[core], f_send.at[1], f_recv.at[1], flip_r(0)))
    f1.wait_recv()
    parts_out = pltpu.make_async_copy(final, parts_hbm, out_sem.at[1])
    parts_out.start()
    for copy in sent:
        copy.wait_send()
    gx_out.wait()
    parts_out.wait()


def text_call(R, C, unit, tokens, mask, length, g1, s1, wqkv, wout, g2, s2, wup, wdown, heads=12, group=128):
    captions, seq, width = tokens.shape
    rows, hidden = captions * seq, wup.shape[1]
    rb, cb = log2(R), log2(C)
    half, sub, span = width // 2, hidden // (4 * C), hidden // C
    V, S, D = pltpu.VMEM, jax.ShapeDtypeStruct, pltpu.SemaphoreType.DMA
    pairs = captions * R * C
    bits_c = (2,) * cb

    dims, tail = 1 + rb + cb, (captions // 2, width)
    lead = max(log2(pairs // 1024), 0)
    held_dims, staged_dims = dims - lead, dims if lead else 0

    def recvs():
        out = []
        for k in range(2):
            full = [("r", 1)] + [("c", b) for b in reversed(range(cb))]
            plan = ([("r", 1), ("c", 0)] if k == 0 else [("c", 0), ("r", 1)]) + [("c", b) for b in range(1, cb)]
            out.append([V((2,) * (len(full) - p) + (sub, half), bf16) for p in range(len(plan) + 1)])
        return out

    vm = pl.BlockSpec(memory_space=pltpu.VMEM)
    hbm = pl.BlockSpec(memory_space=pl.ANY)
    out = pl.pallas_call(
        functools.partial(text_step, (R, C, captions, seq, group), heads),
        name="text",
        in_specs=[vm] * 7 + [hbm] * 5,
        out_specs=(hbm, hbm, vm, hbm),
        out_shape=(S((rows, width), f32), S((2, 2, 3, 2, sub, half), bf16), S((4, width), f32), S((2,) * staged_dims + tail, bf16)),
        scratch_shapes=[
            V((rows, width), bf16), V(wqkv.shape, bf16), V(wout.shape, bf16), V(wup.shape, bf16), V(wdown.shape, bf16),
            V((rows, width), bf16), V((rows, 3 * width), bf16), V((rows, heads * group), f32), V((rows, width), bf16),
            V((rows, width), f32), V((rows, width), bf16), V((rows, hidden), bf16), V((captions, hidden), f32), V((rows, 128), f32),
            V((2,) * held_dims + tail, bf16),
            V((1, pairs), f32), V((C - 1, 1, pairs), f32), V((1, pairs), f32), V((R - 1, 1, pairs), f32),
            V((C, captions, span), bf16), V((C, captions, span), bf16), V((captions, width), bf16), V((C, captions, width), bf16),
            V((2, 2, 2) + bits_c + (sub, half), bf16), V((2, 2, 2) + bits_c + (sub, half), bf16), recvs(), recvs(),
            V((2, 2, 2, sub, half), bf16), V((2, 2, sub, half), bf16), V((2, sub, half), bf16),
            V((2, 2, 3, 2, sub, half), bf16), V((max(rb - 2, 1), 3, 2, sub, half), bf16),
            V((4, width), f32), V((C - 1, 4, width), f32), V((4, width), f32), V((R - 1, 4, width), f32),
            D((7,)), D((2,)), D((2, rb + cb)), D((2, rb + cb)), D((R + C - 2,)), D((R + C - 2,)),
            D((C - 1,)), D((C - 1,)), D((C - 1,)), D((C - 1,)),
            D((2, 2, cb + 2)), D((2, 2, cb + 2)), D((2,)), D((2,)), D((max(rb, 2),)), D((max(rb, 2),)), D((R + C - 2,)), D((R + C - 2,)),
        ],
        compiler_params=pltpu.CompilerParams(collective_id=0, has_side_effects=True, vmem_limit_bytes=67043328),
    )(unit, mask.T, length[None], g1, s1, g2, s2, tokens.reshape(rows, width), wqkv, wout, wup, wdown)
    return out[:3]


def finish_kernel(
    col_size, parts, vecs, shift, gx_in, gx_out, up_out, out_out, qkv_out, down_out, v0, v1, v2, v3,
    gx, up, out, qkv, down, sems
):
    sub, half = parts.shape[-2:]
    load = pltpu.make_async_copy(gx_in, gx, sems.at[0])
    load.start()
    stores = []

    def store(src, dst):
        copy = pltpu.make_async_copy(src, dst, sems.at[1 + len(stores)])
        copy.start()
        stores.append(copy)

    def block(m, j):
        return jnp.concatenate([parts[0, j % 2, m, j // 2], parts[1, j % 2, m, j // 2]], -1).astype(f32)

    for j in range(4):
        down[j * sub : (j + 1) * sub, :] = block(2, j)
    store(down, down_out)
    out[...] = block(1, 0)
    for j in range(3):
        qkv[j * sub : (j + 1) * sub, :] = block(1, j + 1)
    load.wait()
    store(gx, gx_out)
    store(qkv, qkv_out)
    store(out, out_out)
    up[...] = jnp.concatenate([block(0, j) for j in range(4)], 0).T
    store(up, up_out)
    width = vecs.shape[1]
    share = width // col_size
    lane = lax.broadcasted_iota(jnp.int32, (width, share), 1)
    row = lax.broadcasted_iota(jnp.int32, (width, share), 0)
    pick = jnp.where(row == lane + shift[0], 1.0, 0.0)
    own = jnp.dot(vecs[...], pick, precision=lax.Precision.HIGHEST, preferred_element_type=f32)
    for k, v in enumerate((v0, v1, v2, v3)):
        v[...] = own[k : k + 1, :]
    for copy in stores:
        copy.wait()


def finish_call(C, gx, parts, vecs):
    sub, half = parts.shape[-2:]
    width = 2 * half
    share = width // C
    S, V = jax.ShapeDtypeStruct, pltpu.VMEM
    shift = (lax.axis_index("col") * share).astype(jnp.int32)[None]
    vm = pl.BlockSpec(memory_space=pltpu.VMEM)
    hbm = pl.BlockSpec(memory_space=pl.ANY)
    shapes = [gx.shape, (width, 4 * sub), (sub, width), (3 * sub, width), (4 * sub, width)]
    return pl.pallas_call(
        functools.partial(finish_kernel, C),
        name="finish",
        in_specs=[vm, vm, pl.BlockSpec(memory_space=pltpu.SMEM), hbm],
        out_specs=(hbm,) * 5 + (vm,) * 4,
        out_shape=tuple(S(s, f32) for s in shapes) + (S((1, share), f32),) * 4,
        scratch_shapes=[V(s, f32) for s in shapes] + [pltpu.SemaphoreType.DMA((6,))],
    )(parts, vecs, shift, gx)


def on_device(
    image_tokens, caption_tokens, caption_mask, caption_length,
    image_gain1, image_shift1, image_qkv, image_out, image_gain2, image_shift2, image_up, image_down,
    text_gain1, text_shift1, text_qkv, text_out, text_gain2, text_shift2, text_up, text_down,
):
    R, C = lax.axis_size("row"), lax.axis_size("col")
    unit = image_unit(
        image_tokens, image_gain1, image_shift1, image_qkv, image_out,
        image_gain2, image_shift2, image_up, image_down,
    )
    grad_tokens, parts, vecs = text_call(
        R, C, unit, caption_tokens, caption_mask, caption_length, text_gain1, text_shift1, text_qkv, text_out,
        text_gain2, text_shift2, text_up, text_down,
    )
    grad_tokens, up, out, qkv, down, gain1, shift1, gain2, shift2 = finish_call(C, grad_tokens, parts, vecs)
    return (
        grad_tokens.reshape(caption_tokens.shape), gain1[0], shift1[0], qkv.T, out.T, gain2[0], shift2[0], up, down,
    )


def solution(mesh):
    pair = P(("row", "col"))
    return jax.shard_map(
        on_device,
        mesh=mesh,
        in_specs=(pair,) * 4 + (P(),) * 16,
        out_specs=(pair, P("col"), P("col"), P(None, "col"), P(None, "col"), P("col"), P("col"), P(None, "col"), P("col")),
        check_vma=False,
    )
```

```python
import math, functools
import jax, jax.numpy as jnp
from jax import lax
from jax.experimental import pallas as pl
from jax.experimental.pallas import tpu as pltpu
from jax.sharding import PartitionSpec as P

epsilon = 1e-06
log2e = 1.4426950408889634
inv_root2 = 0.7071067811865476
f32 = jnp.float32
bf16 = jnp.bfloat16


def dot(a, b):
    return jnp.dot(a, b, preferred_element_type=f32)


def dot_t(a, b):
    return lax.dot_general(a, b, (((1,), (1,)), ((), ())), preferred_element_type=f32)


def stats(x):
    centred = x - jnp.mean(x, -1, keepdims=True)
    inverse = lax.rsqrt(jnp.mean(centred * centred, -1, keepdims=True) + epsilon)
    return centred * inverse, inverse


def two_heads(v):
    first = lax.broadcasted_iota(jnp.int32, v.shape, 1) < v.shape[1] // 2
    zero = jnp.zeros_like(v)
    return jnp.concatenate([jnp.where(first, v, zero), jnp.where(first, zero, v)], 0)


def gelu(v):
    u = 0.5 * v
    return u * lax.erf(v * inv_root2) + u


def image_kernel(
    heads, x_ref, g1, s1, wqkv_hbm, wout_hbm, g2, s2, wup_hbm, wdown_hbm, out_ref,
    tok, xs, n, qkv, at, mixed, act, pooled, wqkv, wout, wup, wdown, sems
):
    tokens, images, width = x_ref.shape
    pad = -(-tokens // 8) * 8
    rows = images * pad
    i = pl.program_id(0)
    weights = ((wqkv_hbm, wqkv), (wout_hbm, wout), (wup_hbm, wup), (wdown_hbm, wdown))

    def fetched(k):
        @pl.when(i == 0)
        def _():
            pltpu.make_async_copy(*weights[k], sems.at[k]).wait()

    @pl.when(i == 0)
    def _():
        for k in range(4):
            pltpu.make_async_copy(*weights[k], sems.at[k]).start()
        xs[...] = jnp.zeros_like(xs)
        qkv[rows:, :] = jnp.zeros((qkv.shape[0] - rows, 3 * width), bf16)

    count = tokens * images
    for j in range(width // 128):
        lanes = slice(j * 128, (j + 1) * 128)
        tok[j * count : (j + 1) * count, :] = x_ref[:, :, lanes].astype(f32).reshape(count, 128)
    for j in range(width // 128):
        for k in range(images):
            xs[k * pad : k * pad + tokens, j * 128 : (j + 1) * 128] = tok[pl.ds(j * count + k, tokens, stride=images), :]
    scaled, _ = stats(xs[...])
    n[...] = (scaled * g1[...][None] + s1[...][None]).astype(bf16)
    fetched(0)
    for c in range(3):
        cols = slice(c * width, (c + 1) * width)
        qkv[:rows, cols] = dot(n[...], wqkv[:, cols]).astype(bf16)

    group = 2 * pad
    hd = width // heads
    r_id = lax.broadcasted_iota(jnp.int32, (group, 2 * hd), 0)
    c_id = lax.broadcasted_iota(jnp.int32, (group, 2 * hd), 1)
    same = (r_id < pad) == (c_id < pad)
    inside = jnp.where(c_id < pad, c_id, c_id - pad) < tokens
    keep = same & inside
    first = lax.broadcasted_iota(jnp.int32, (group, 2 * hd), 1) < hd
    factor = hd ** (-0.5) * log2e

    def attend(g, carry):
        rs = pl.ds(pl.multiple_of(g * group, 16), group)
        ks = pl.ds(pl.multiple_of(g * group, 16), 2 * hd)
        for hp in range(heads // 2):
            lanes = slice(hp * 2 * hd, (hp + 1) * 2 * hd)
            q2 = qkv[rs, lanes]
            k2 = two_heads(qkv[ks, slice(width + lanes.start, width + lanes.stop)])
            v2 = two_heads(qkv[ks, slice(2 * width + lanes.start, 2 * width + lanes.stop)])
            s2 = dot_t(q2, k2) * factor
            es, inv = [], []
            for h in range(2):
                s = jnp.where(keep, s2[:, h * 2 * hd : (h + 1) * 2 * hd], -1e30)
                e = jnp.exp2(s - jnp.max(s, -1, keepdims=True))
                inv.append(1.0 / jnp.sum(e, -1, keepdims=True))
                es.append(e.astype(bf16))
            out = dot(jnp.concatenate(es, 1), v2)
            at[rs, lanes] = (out * jnp.where(first, inv[0], inv[1])).astype(bf16)
        return carry

    lax.fori_loop(0, rows // group, attend, 0)
    fetched(1)
    mixed[...] = xs[...] + dot(at[...], wout[...])
    row = lax.broadcasted_iota(jnp.int32, (pad, 1), 0)
    valid = (row < tokens).astype(f32)
    dst = pl.ds(pl.multiple_of(i * images, 8), images)
    m3 = mixed[...].reshape(images, pad, width)
    pooled[dst, :] = jnp.sum(m3 * valid[None], 1)
    scaled, _ = stats(mixed[...])
    normed = ((scaled * g2[...][None] + s2[...][None]).reshape(images, pad, width) * valid[None]).reshape(rows, width)
    n[...] = normed.astype(bf16)
    hidden = wup.shape[1]
    step = 768
    fetched(2)
    for c in range(0, hidden, step):
        a = gelu(dot(n[...], wup[:, c : c + step]))
        act[dst, c : c + step] = jnp.sum(a.reshape(images, pad, step), 1)

    fetched(3)

    @pl.when(i == pl.num_programs(0) - 1)
    def _():
        a = act[...] * (1.0 / tokens)
        hi = a.astype(bf16)
        lo = (a - hi.astype(f32)).astype(bf16)
        count = a.shape[0]
        both = dot(jnp.concatenate([hi, lo], 0), wdown[...])
        e = pooled[...] * (1.0 / tokens) + both[:count] + both[count:]
        out_ref[...] = (e * lax.rsqrt(jnp.sum(e * e, -1, keepdims=True) + epsilon)).astype(bf16)


def image_unit(x, g1, s1, wqkv, wout, g2, s2, wup, wdown, heads=12, images=8):
    count, tokens, width = x.shape
    hidden = wup.shape[1]
    pad = -(-tokens // 8) * 8
    rows = images * pad
    full = lambda a: pl.BlockSpec(a.shape, lambda i: (0,) * a.ndim, pipeline_mode=pl.Buffered(1))
    hbm = pl.BlockSpec(memory_space=pl.ANY)
    args = (jnp.transpose(x, (1, 0, 2)), g1, s1, wqkv, wout, g2, s2, wup, wdown)
    return pl.pallas_call(
        functools.partial(image_kernel, heads),
        name="image",
        grid=(count // images,),
        out_shape=jax.ShapeDtypeStruct((count, width), bf16),
        in_specs=[pl.BlockSpec((tokens, images, width), lambda i: (0, i, 0))]
        + [full(a) if a.ndim == 1 else hbm for a in args[1:]],
        out_specs=pl.BlockSpec((count, width), lambda i: (0, 0)),
        scratch_shapes=[
            pltpu.VMEM((width // 128 * tokens * images, 128), f32),
            pltpu.VMEM((rows, width), f32),
            pltpu.VMEM((rows, width), bf16),
            pltpu.VMEM((rows + 16, 3 * width), bf16),
            pltpu.VMEM((rows, width), bf16),
            pltpu.VMEM((rows, width), f32),
            pltpu.VMEM((count, hidden), f32),
            pltpu.VMEM((count, width), f32),
        ]
        + [pltpu.VMEM(w.shape, bf16) for w in (wqkv, wout, wup, wdown)]
        + [pltpu.SemaphoreType.DMA((4,))],
        compiler_params=pltpu.CompilerParams(vmem_limit_bytes=67043328),
    )(*args)

def dot_0(a, b):
    return lax.dot_general(a, b, (((0,), (0,)), ((), ())), preferred_element_type=f32)


def norm_back(grad_normed, scaled, inverse, gain):
    g = grad_normed * gain
    centre = jnp.mean(g, -1, keepdims=True)
    along = jnp.mean(g * scaled, -1, keepdims=True)
    return inverse * (g - centre - scaled * along)


def token_columns(mask_ref, length_ref, seq):
    captions = mask_ref.shape[1]
    rows = captions * seq
    row = lax.broadcasted_iota(jnp.int32, (rows, captions), 0)
    lane = lax.broadcasted_iota(jnp.int32, (rows, captions), 1)
    length = length_ref[...].astype(f32)
    own = row // seq == lane
    length_t = jnp.sum(jnp.where(own, length, 0.0), -1, keepdims=True)
    spread = dot_t(jnp.where(own, 1.0, 0.0).astype(bf16), mask_ref[...].astype(f32).astype(bf16))
    row = lax.broadcasted_iota(jnp.int32, (rows, seq), 0)
    lane = lax.broadcasted_iota(jnp.int32, (rows, seq), 1)
    mask_t = jnp.sum(jnp.where(row % seq == lane, spread, 0.0), -1, keepdims=True)
    place = (lax.broadcasted_iota(jnp.int32, (rows, 1), 0) % seq).astype(f32)
    weight = jnp.where(place < length_t, mask_t, 0.0)
    count = jnp.sum(weight.reshape(captions, seq, 1), 1)
    return length_t, weight, jnp.maximum(count, 1.0)


def text_attention(heads, seq, group, width, qkv, probs, at, cols):
    hd = width // heads
    r_id = lax.broadcasted_iota(jnp.int32, (group, group), 0)
    c_id = lax.broadcasted_iota(jnp.int32, (group, group), 1)
    same = r_id // seq == c_id // seq
    place = (c_id % seq).astype(f32)
    factor = hd ** (-0.5) * log2e

    def attend(g, carry):
        rs = pl.ds(pl.multiple_of(g * group, 16), group)
        keep = same & (place < cols[rs, 1:2])
        for hp in range(heads // 2):
            lanes = slice(hp * 2 * hd, (hp + 1) * 2 * hd)
            q2 = qkv[rs, lanes]
            k2 = two_heads(qkv[rs, slice(width + lanes.start, width + lanes.stop)])
            v2 = two_heads(qkv[rs, slice(2 * width + lanes.start, 2 * width + lanes.stop)])
            s2 = dot_t(q2, k2) * factor
            ps = []
            for h in range(2):
                s = jnp.where(keep, s2[:, h * group : (h + 1) * group], -1e30)
                e = jnp.exp2(s - jnp.max(s, -1, keepdims=True))
                p = e * (1.0 / jnp.sum(e, -1, keepdims=True))
                probs[rs, pl.ds((hp * 2 + h) * group, group)] = p
                ps.append(p.astype(bf16))
            at[rs, lanes] = dot(jnp.concatenate(ps, 1), v2).astype(bf16)
        return carry

    return attend


inv_root_2pi = 0.3989422804014327


def split_dot(a, w):
    hi = a.astype(bf16)
    lo = (a - hi.astype(f32)).astype(bf16)
    both = dot(jnp.concatenate([hi, lo], 0), w[...])
    return both[: a.shape[0]] + both[a.shape[0] :]


def text_attention_back(heads, group, width, qkv, probs, at):
    hd = width // heads
    scale = hd ** (-0.5)

    def attend(g, carry):
        rs = pl.ds(pl.multiple_of(g * group, 16), group)
        for hp in range(heads // 2):
            lanes = slice(hp * 2 * hd, (hp + 1) * 2 * hd)
            klanes = slice(width + lanes.start, width + lanes.stop)
            vlanes = slice(2 * width + lanes.start, 2 * width + lanes.stop)
            ga = at[rs, lanes]
            q2, k2, v2 = two_heads(qkv[rs, lanes]), two_heads(qkv[rs, klanes]), two_heads(qkv[rs, vlanes])
            dp2 = dot_t(ga, v2)
            ps, ds = [], []
            for h in range(2):
                p = probs[rs, pl.ds((hp * 2 + h) * group, group)]
                dp = dp2[:, h * group : (h + 1) * group]
                ds.append((p * (dp - jnp.sum(dp * p, -1, keepdims=True))).astype(bf16))
                ps.append(p.astype(bf16))
            dv = dot_0(jnp.concatenate(ps, 0), two_heads(ga))
            dq = dot(jnp.concatenate(ds, 1), k2)
            dk = dot_0(jnp.concatenate(ds, 0), q2)
            qkv[rs, lanes] = (dq * scale).astype(bf16)
            qkv[rs, klanes] = (dk * scale).astype(bf16)
            qkv[rs, vlanes] = dv.astype(bf16)
        return carry

    return attend


MESH = pl.DeviceIdType.MESH


def log2(n):
    return n.bit_length() - 1


def text_step(
    shape, heads,
    unit_ref, mask_ref, length_ref, g1, s1, g2, s2, x_hbm, wqkv_hbm, wout_hbm, wup_hbm, wdown_hbm,
    gx_hbm, parts_hbm, vecs_ref, images_hbm,
    x_ref, wqkv, wout, wup, wdown, n1, qkv, probs, at, mixed, n2, slope, act, cols,
    images, rowsum, rowsum_c, rowsum_cs, rowsum_r, pooled_act, act_all, gpc_own, gpc_all,
    g_up, g_rest, r_up, r_rest, d_part, d_recv, d_recv2, final, extra, vec, vec_c, vec_cs, vec_r,
    load_sem, out_sem, ag_send, ag_recv, ps_send, ps_recv, a_send, a_recv, gp_send, gp_recv,
    rs_send, rs_recv, d_send, d_recv_sem, f_send, f_recv, v_send, v_recv,
):
    R, C, captions, seq, group = shape
    rb, cb = log2(R), log2(C)
    r, c = lax.axis_index("row"), lax.axis_index("col")
    rbit = [lax.rem(lax.div(r, 1 << b), 2) for b in range(rb)]
    cbit = [lax.rem(lax.div(c, 1 << b), 2) for b in range(cb)]
    core, xh = rbit[0], rbit[1]
    rows, width = x_ref.shape
    hidden = wup.shape[1]
    half = width // 2
    sub = hidden // (4 * C)

    def flip_r(b):
        return (r + (1 - 2 * rbit[b]) * (1 << b), c)

    def flip_c(b):
        return (r, c + (1 - 2 * cbit[b]) * (1 << b))

    row_peers = [(lax.rem(r + d, R), c) for d in range(1, R)]
    col_peers = [(r, lax.rem(c + d, C)) for d in range(1, C)]

    def remote(src, dst, send, recv, to):
        return pltpu.make_async_remote_copy(
            src_ref=src, dst_ref=dst, send_sem=send, recv_sem=recv, device_id=to, device_id_type=MESH
        )

    sent = []

    def go(copy):
        copy.start()
        sent.append(copy)
        return copy

    barrier = pltpu.get_barrier_semaphore()
    for to in row_peers + col_peers:
        pl.semaphore_signal(barrier, inc=1, device_id=to, device_id_type=MESH)

    loads = []
    for k, (src, dst) in enumerate(
        ((x_hbm, x_ref), (wqkv_hbm, wqkv), (wout_hbm, wout), (wup_hbm, wup), (wdown_hbm, wdown))
    ):
        copy = pltpu.make_async_copy(src, dst, load_sem.at[k])
        copy.start()
        loads.append(copy)

    length_t, weight, count = token_columns(mask_ref, length_ref, seq)
    cols[:, 0:1] = weight
    cols[:, 1:2] = length_t
    loads[0].wait()
    pl.semaphore_wait(barrier, R + C - 2)

    mine = tuple(rbit[b] for b in reversed(range(rb))) + tuple(cbit[b] for b in reversed(range(cb)))
    part = captions // 2
    pairs = captions * R * C
    staged = len(images.shape) < 3 + rb + cb
    gather = images_hbm if staged else images
    for k in range(2):
        if staged:
            copy = pltpu.make_async_copy(unit_ref.at[pl.ds(k * part, part), :], gather.at[(k,) + mine], load_sem.at[5 + k])
            copy.start()
            loads.append(copy)
        else:
            images[(k,) + mine] = unit_ref[k * part : (k + 1) * part, :]
    if staged:
        loads[5].wait()
        loads[6].wait()

    def stage(i):
        if not staged:
            return images[...].reshape(pairs, width)
        lead = 3 + rb + cb - len(images.shape)
        where = tuple((i >> b) & 1 for b in reversed(range(lead)))
        copy = pltpu.make_async_copy(gather.at[where], images, load_sem.at[5])
        copy.start()
        copy.wait()
        return images[...].reshape(pairs >> lead, width)

    stages = pairs // math.prod(images.shape[:-1])
    order = [("c", b) for b in reversed(range(1, cb))]
    tail = [("r", b) for b in reversed(range(1, rb))]
    plans = (order + [("c", 0)] + tail + [("r", 0)], order + tail + [("c", 0)] + [("r", 0)])
    gathered = [set(), set()]
    pending = [None, None]
    phase = [0, 0]

    def gather_step():
        for k in range(2):
            if pending[k] is not None:
                pending[k].wait_recv()
                gathered[k].add(plans[k][phase[k] - 1])
                pending[k] = None
            if phase[k] < len(plans[k]):
                kind, b = plans[k][phase[k]]
                names = [("r", i) for i in reversed(range(rb))] + [("c", i) for i in reversed(range(cb))]
                where = tuple(slice(None) if nm in gathered[k] else v for nm, v in zip(names, mine))
                dst = gather.at[(k,) + where]
                src = unit_ref.at[pl.ds(k * part, part), :] if phase[k] == 0 else dst
                to = flip_r(b) if kind == "r" else flip_c(b)
                pending[k] = go(remote(src, dst, ag_send.at[k, phase[k]], ag_recv.at[k, phase[k]], to))
                phase[k] += 1

    gather_step()
    x = x_ref[...].astype(f32)
    scaled, _ = stats(x)
    n1[...] = (scaled * g1[...][None] + s1[...][None]).astype(bf16)
    loads[1].wait()
    for q in range(3):
        cut = slice(q * width, (q + 1) * width)
        qkv[:, cut] = dot(n1[...], wqkv[:, cut]).astype(bf16)
    gather_step()
    attend = text_attention(heads, seq, group, width, qkv, probs, at, cols)
    groups = rows // group
    lax.fori_loop(0, groups // 2, attend, 0)
    gather_step()
    lax.fori_loop(groups // 2, groups, attend, 0)
    gather_step()
    loads[2].wait()
    mixed[...] = x_ref[...].astype(f32) + dot(at[...], wout[...])
    scaled, _ = stats(mixed[...])
    n2[...] = (scaled * g2[...][None] + s2[...][None]).astype(bf16)
    weight = cols[:, 0:1]
    loads[3].wait()
    for f in range(0, hidden, width):
        cut = slice(f, f + width)
        h = dot(n2[...], wup[:, cut])
        phi = 0.5 + 0.5 * lax.erf(h * inv_root2)
        slope[:, cut] = (phi + h * (jnp.exp(-0.5 * h * h) * inv_root_2pi)).astype(bf16)
        act[:, cut] = jnp.sum((h * phi * weight).reshape(captions, seq, width), 1)
        if f == 2 * width:
            gather_step()
    loads[4].wait()
    pooled = jnp.sum((mixed[...] * weight).reshape(captions, seq, width), 1) + split_dot(act[...], wdown)
    pooled = pooled / count
    inverse = lax.rsqrt(jnp.sum(pooled * pooled, -1, keepdims=True) + epsilon)
    text_unit = (pooled * inverse).astype(bf16)
    span = hidden // C
    for k in range(C):
        pooled_act[k] = act[:, k * span : (k + 1) * span].astype(bf16)
    while pending[0] is not None or pending[1] is not None:
        gather_step()

    t = 2.0 * math.sqrt(width)
    sims = []
    for i in range(stages):
        every = stage(i)
        sims.append(dot_t(text_unit, every))
    e = jnp.exp2(jnp.concatenate(sims, 1) * (t * log2e))
    rowsum[...] = jnp.sum(e, 0, keepdims=True)
    first = [
        go(remote(rowsum, rowsum_c.at[d], ps_send.at[d], ps_recv.at[d], to)) for d, to in enumerate(col_peers)
    ]
    col_scale = 1.0 / jnp.sum(e, -1, keepdims=True)
    acts = []
    for d, to in enumerate(col_peers):
        acts.append(
            go(remote(pooled_act.at[lax.rem(c + d + 1, C)], act_all.at[d], a_send.at[d], a_recv.at[d], to))
        )
    act_all[C - 1] = pooled_act[c]
    total = rowsum[...]
    for d, copy in enumerate(first):
        copy.wait_recv()
        total += rowsum_c[d]
    rowsum_cs[...] = total
    second = [
        go(remote(rowsum_cs, rowsum_r.at[d], ps_send.at[C - 1 + d], ps_recv.at[C - 1 + d], to))
        for d, to in enumerate(row_peers)
    ]
    for d, copy in enumerate(second):
        copy.wait_recv()
        total += rowsum_r[d]
    grad_sim = (e * (1.0 / total + col_scale) * (0.5 / pairs)).astype(bf16)
    share = pairs // stages
    hits = sum(
        dot(grad_sim[:, i * share : (i + 1) * share], every if stages == 1 else stage(i)) for i in range(stages)
    )
    grad_unit = t * hits - (t / pairs) * unit_ref[...].astype(f32)
    along = jnp.sum(grad_unit * pooled, -1, keepdims=True)
    gpc = (inverse * grad_unit - pooled * (inverse * inverse * inverse * along)) / count
    gpc_r = gpc.astype(bf16)
    gpc_own[...] = gpc_r
    gps = [go(remote(gpc_own, gpc_all.at[d], gp_send.at[d], gp_recv.at[d], to)) for d, to in enumerate(col_peers)]
    gpc_all[C - 1] = gpc_r

    def place(buf, c_index, j, block):
        bits = tuple((c_index >> b) & 1 for b in reversed(range(cb)))
        for s in range(2):
            buf[(s, j // 2, j % 2) + bits] = block[:, s * half : (s + 1) * half].astype(bf16)

    def emit(name, row, block):
        for i in range(0, block.shape[0], sub):
            at_row = row + i
            piece = block[i : i + sub, :]
            if name == "up":
                place(g_up, at_row // (4 * sub), at_row % (4 * sub) // sub, piece)
            elif name == "out":
                place(g_rest, at_row // sub, 0, piece)
            else:
                place(g_rest, at_row // (3 * sub), 1 + at_row % (3 * sub) // sub, piece)

    class Scatter:
        def __init__(self, index, buf, recvs):
            self.index, self.buf, self.recvs = index, buf, recvs
            head = [("r", 1)], [("c", 0)]
            back = [("c", 0)], [("r", 1)]
            rest = [("c", b) for b in range(1, cb)]
            self.plan = [head[k] + back[k] + rest for k in range(2)]
            self.phase = 0
            self.copies = [None, None]

        def start(self):
            for k in range(2):
                self.copies[k] = go(
                    remote(
                        self.buf.at[1 - core, k], self.recvs[k][0],
                        rs_send.at[self.index, k, 0], rs_recv.at[self.index, k, 0], flip_r(0),
                    )
                )

        def step(self):
            p = self.phase
            last = p == len(self.plan[0])
            for k in range(2):
                self.copies[k].wait_recv()
                here = self.recvs[k][p]
                before = self.buf.at[core, k] if p == 0 else self.recvs[k][p - 1].at[self.kept[k]]
                if last:
                    final[core, xh, self.index, k] = before[...] + here[...]
                    continue
                kind, b = self.plan[k][p]
                left = [("r", 1)] + [("c", i) for i in reversed(range(cb))]
                for done in self.plan[k][:p]:
                    left.remove(done)
                axis = left.index((kind, b))
                bit = xh if kind == "r" else cbit[b]
                give = (slice(None),) * axis + (1 - bit,)
                keep = (slice(None),) * axis + (bit,)
                here[give] = before[give] + here[give]
                to = flip_r(1) if kind == "r" else flip_c(b)
                self.copies[k] = go(
                    remote(
                        here.at[give], self.recvs[k][p + 1],
                        rs_send.at[self.index, k, p + 1], rs_recv.at[self.index, k, p + 1], to,
                    )
                )
                here[keep] = before[keep] + here[keep]
                self.next_kept[k] = keep
            self.kept = list(self.next_kept)
            self.phase += 1

        kept = (None, None)
        next_kept = [None, None]

    up = Scatter(0, g_up, r_up)
    rest = Scatter(1, g_rest, r_rest)
    up.next_kept, rest.next_kept = [None, None], [None, None]

    for f in range(0, hidden, width):
        cut = slice(f, f + width)
        hh = dot_t(gpc_r, wdown[cut, :])
        spread = jnp.broadcast_to(hh[:, None, :], (captions, seq, width)).reshape(rows, width)
        slope[:, cut] = (spread * weight * slope[:, cut].astype(f32)).astype(bf16)
        emit("up", f, dot_0(slope[:, cut], n2[...]))
    up.start()
    gn2 = dot_t(slope[...], wup[...])
    scaled, inv2 = stats(mixed[...])
    vec[2:3, :] = jnp.sum(gn2 * scaled, 0, keepdims=True)
    vec[3:4, :] = jnp.sum(gn2, 0, keepdims=True)
    spread = jnp.broadcast_to(gpc[:, None, :], (captions, seq, width)).reshape(rows, width) * weight
    mixed[...] = spread + norm_back(gn2, scaled, inv2, g2[...][None])
    n2[...] = mixed[...].astype(bf16)
    emit("out", 0, dot_0(n2[...], at[...]))
    at[...] = dot_t(n2[...], wout[...]).astype(bf16)
    up.step()
    attend_back = text_attention_back(heads, group, width, qkv, probs, at)
    lax.fori_loop(0, groups // 2, attend_back, 0)

    for copy in acts + gps:
        copy.wait_recv()
    down = dot_0(act_all[...].reshape(C * captions, span), gpc_all[...].reshape(C * captions, width))
    for j in range(4):
        for s in range(2):
            d_part[s, j // 2, j % 2] = down[j * sub : (j + 1) * sub, s * half : (s + 1) * half].astype(bf16)
    d0 = go(remote(d_part.at[1 - core], d_recv, d_send.at[0], d_recv_sem.at[0], flip_r(0)))

    lax.fori_loop(groups // 2, groups, attend_back, 0)
    up.step()
    for q in range(3):
        emit("qkv", q * width, dot_0(qkv[:, q * width : (q + 1) * width], n1[...]))
    rest.start()
    d0.wait_recv()
    d_recv[:, 1 - xh] = d_part[core, :, 1 - xh] + d_recv[:, 1 - xh]
    d1 = go(remote(d_recv.at[:, 1 - xh], d_recv2, d_send.at[1], d_recv_sem.at[1], flip_r(1)))
    d_recv[:, xh] = d_part[core, :, xh] + d_recv[:, xh]
    gn1 = dot_t(qkv[...], wqkv[...])
    rest.step()
    scaled, inv1 = stats(x_ref[...].astype(f32))
    vec[0:1, :] = jnp.sum(gn1 * scaled, 0, keepdims=True)
    vec[1:2, :] = jnp.sum(gn1, 0, keepdims=True)
    vfirst = [go(remote(vec, vec_c.at[d], v_send.at[d], v_recv.at[d], to)) for d, to in enumerate(col_peers)]
    mixed[...] = mixed[...] + norm_back(gn1, scaled, inv1, g1[...][None])
    gx_out = pltpu.make_async_copy(mixed, gx_hbm, out_sem.at[0])
    gx_out.start()
    d1.wait_recv()
    final[core, xh, 2] = d_recv[:, xh] + d_recv2[...]
    while up.phase <= cb:
        up.step()
    rest.step()
    up.step()
    vtotal = vec[...]
    for d, copy in enumerate(vfirst):
        copy.wait_recv()
        vtotal += vec_c[d]
    vec_cs[...] = vtotal
    vsecond = [
        go(remote(vec_cs, vec_r.at[d], v_send.at[C - 1 + d], v_recv.at[C - 1 + d], to)) for d, to in enumerate(row_peers)
    ]
    while rest.phase <= cb:
        rest.step()
    rest.step()
    for b in range(2, rb):
        swap = remote(final.at[core, xh], extra.at[b - 2], f_send.at[b], f_recv.at[b], flip_r(b))
        swap.start()
        swap.wait()
        final[core, xh] = final[core, xh] + extra[b - 2]
    f0 = go(remote(final.at[core, xh], final.at[core, xh], f_send.at[0], f_recv.at[0], flip_r(1)))
    for d, copy in enumerate(vsecond):
        copy.wait_recv()
        vtotal += vec_r[d]
    vecs_ref[...] = vtotal
    f0.wait_recv()
    f1 = go(remote(final.at[core], final.at[core], f_send.at[1], f_recv.at[1], flip_r(0)))
    f1.wait_recv()
    parts_out = pltpu.make_async_copy(final, parts_hbm, out_sem.at[1])
    parts_out.start()
    for copy in sent:
        copy.wait_send()
    gx_out.wait()
    parts_out.wait()


def text_call(R, C, unit, tokens, mask, length, g1, s1, wqkv, wout, g2, s2, wup, wdown, heads=12, group=128):
    captions, seq, width = tokens.shape
    rows, hidden = captions * seq, wup.shape[1]
    rb, cb = log2(R), log2(C)
    half, sub, span = width // 2, hidden // (4 * C), hidden // C
    V, S, D = pltpu.VMEM, jax.ShapeDtypeStruct, pltpu.SemaphoreType.DMA
    pairs = captions * R * C
    bits_c = (2,) * cb

    dims, tail = 1 + rb + cb, (captions // 2, width)
    lead = max(log2(pairs // 1024), 0)
    held_dims, staged_dims = dims - lead, dims if lead else 0

    def recvs():
        out = []
        for k in range(2):
            full = [("r", 1)] + [("c", b) for b in reversed(range(cb))]
            plan = ([("r", 1), ("c", 0)] if k == 0 else [("c", 0), ("r", 1)]) + [("c", b) for b in range(1, cb)]
            out.append([V((2,) * (len(full) - p) + (sub, half), bf16) for p in range(len(plan) + 1)])
        return out

    vm = pl.BlockSpec(memory_space=pltpu.VMEM)
    hbm = pl.BlockSpec(memory_space=pl.ANY)
    out = pl.pallas_call(
        functools.partial(text_step, (R, C, captions, seq, group), heads),
        name="text",
        in_specs=[vm] * 7 + [hbm] * 5,
        out_specs=(hbm, hbm, vm, hbm),
        out_shape=(S((rows, width), f32), S((2, 2, 3, 2, sub, half), bf16), S((4, width), f32), S((2,) * staged_dims + tail, bf16)),
        scratch_shapes=[
            V((rows, width), bf16), V(wqkv.shape, bf16), V(wout.shape, bf16), V(wup.shape, bf16), V(wdown.shape, bf16),
            V((rows, width), bf16), V((rows, 3 * width), bf16), V((rows, heads * group), f32), V((rows, width), bf16),
            V((rows, width), f32), V((rows, width), bf16), V((rows, hidden), bf16), V((captions, hidden), f32), V((rows, 128), f32),
            V((2,) * held_dims + tail, bf16),
            V((1, pairs), f32), V((C - 1, 1, pairs), f32), V((1, pairs), f32), V((R - 1, 1, pairs), f32),
            V((C, captions, span), bf16), V((C, captions, span), bf16), V((captions, width), bf16), V((C, captions, width), bf16),
            V((2, 2, 2) + bits_c + (sub, half), bf16), V((2, 2, 2) + bits_c + (sub, half), bf16), recvs(), recvs(),
            V((2, 2, 2, sub, half), bf16), V((2, 2, sub, half), bf16), V((2, sub, half), bf16),
            V((2, 2, 3, 2, sub, half), bf16), V((max(rb - 2, 1), 3, 2, sub, half), bf16),
            V((4, width), f32), V((C - 1, 4, width), f32), V((4, width), f32), V((R - 1, 4, width), f32),
            D((7,)), D((2,)), D((2, rb + cb)), D((2, rb + cb)), D((R + C - 2,)), D((R + C - 2,)),
            D((C - 1,)), D((C - 1,)), D((C - 1,)), D((C - 1,)),
            D((2, 2, cb + 2)), D((2, 2, cb + 2)), D((2,)), D((2,)), D((max(rb, 2),)), D((max(rb, 2),)), D((R + C - 2,)), D((R + C - 2,)),
        ],
        compiler_params=pltpu.CompilerParams(collective_id=0, has_side_effects=True, vmem_limit_bytes=67043328),
    )(unit, mask.T, length[None], g1, s1, g2, s2, tokens.reshape(rows, width), wqkv, wout, wup, wdown)
    return out[:3]


def finish_kernel(
    col_size, parts, vecs, shift, gx_in, gx_out, up_out, out_out, qkv_out, down_out, v0, v1, v2, v3,
    gx, up, out, qkv, down, sems
):
    sub, half = parts.shape[-2:]
    load = pltpu.make_async_copy(gx_in, gx, sems.at[0])
    load.start()
    stores = []

    def store(src, dst):
        copy = pltpu.make_async_copy(src, dst, sems.at[1 + len(stores)])
        copy.start()
        stores.append(copy)

    def block(m, j):
        return jnp.concatenate([parts[0, j % 2, m, j // 2], parts[1, j % 2, m, j // 2]], -1).astype(f32)

    for j in range(4):
        down[j * sub : (j + 1) * sub, :] = block(2, j)
    store(down, down_out)
    out[...] = block(1, 0)
    for j in range(3):
        qkv[j * sub : (j + 1) * sub, :] = block(1, j + 1)
    load.wait()
    store(gx, gx_out)
    store(qkv, qkv_out)
    store(out, out_out)
    up[...] = jnp.concatenate([block(0, j) for j in range(4)], 0).T
    store(up, up_out)
    width = vecs.shape[1]
    share = width // col_size
    lane = lax.broadcasted_iota(jnp.int32, (width, share), 1)
    row = lax.broadcasted_iota(jnp.int32, (width, share), 0)
    pick = jnp.where(row == lane + shift[0], 1.0, 0.0)
    own = jnp.dot(vecs[...], pick, precision=lax.Precision.HIGHEST, preferred_element_type=f32)
    for k, v in enumerate((v0, v1, v2, v3)):
        v[...] = own[k : k + 1, :]
    for copy in stores:
        copy.wait()


def finish_call(C, gx, parts, vecs):
    sub, half = parts.shape[-2:]
    width = 2 * half
    share = width // C
    S, V = jax.ShapeDtypeStruct, pltpu.VMEM
    shift = (lax.axis_index("col") * share).astype(jnp.int32)[None]
    vm = pl.BlockSpec(memory_space=pltpu.VMEM)
    hbm = pl.BlockSpec(memory_space=pl.ANY)
    shapes = [gx.shape, (width, 4 * sub), (sub, width), (3 * sub, width), (4 * sub, width)]
    return pl.pallas_call(
        functools.partial(finish_kernel, C),
        name="finish",
        in_specs=[vm, vm, pl.BlockSpec(memory_space=pltpu.SMEM), hbm],
        out_specs=(hbm,) * 5 + (vm,) * 4,
        out_shape=tuple(S(s, f32) for s in shapes) + (S((1, share), f32),) * 4,
        scratch_shapes=[V(s, f32) for s in shapes] + [pltpu.SemaphoreType.DMA((6,))],
    )(parts, vecs, shift, gx)


def on_device(
    image_tokens, caption_tokens, caption_mask, caption_length,
    image_gain1, image_shift1, image_qkv, image_out, image_gain2, image_shift2, image_up, image_down,
    text_gain1, text_shift1, text_qkv, text_out, text_gain2, text_shift2, text_up, text_down,
):
    R, C = lax.axis_size("row"), lax.axis_size("col")
    unit = image_unit(
        image_tokens, image_gain1, image_shift1, image_qkv, image_out,
        image_gain2, image_shift2, image_up, image_down,
    )
    grad_tokens, parts, vecs = text_call(
        R, C, unit, caption_tokens, caption_mask, caption_length, text_gain1, text_shift1, text_qkv, text_out,
        text_gain2, text_shift2, text_up, text_down,
    )
    grad_tokens, up, out, qkv, down, gain1, shift1, gain2, shift2 = finish_call(C, grad_tokens, parts, vecs)
    return (
        grad_tokens.reshape(caption_tokens.shape), gain1[0], shift1[0], qkv.T, out.T, gain2[0], shift2[0], up, down,
    )


def solution(mesh):
    pair = P(("row", "col"))
    return jax.shard_map(
        on_device,
        mesh=mesh,
        in_specs=(pair,) * 4 + (P(),) * 16,
        out_specs=(pair, P("col"), P("col"), P(None, "col"), P(None, "col"), P("col"), P("col"), P(None, "col"), P("col")),
        check_vma=False,
    )
```

```python
import math, functools
import jax, jax.numpy as jnp
from jax import lax
from jax.experimental import pallas as pl
from jax.experimental.pallas import tpu as pltpu
from jax.sharding import PartitionSpec as P

epsilon = 1e-06
log2e = 1.4426950408889634
inv_root2 = 0.7071067811865476
f32 = jnp.float32
bf16 = jnp.bfloat16


def dot(a, b):
    return jnp.dot(a, b, preferred_element_type=f32)


def dot_t(a, b):
    return lax.dot_general(a, b, (((1,), (1,)), ((), ())), preferred_element_type=f32)


def stats(x):
    centred = x - jnp.mean(x, -1, keepdims=True)
    inverse = lax.rsqrt(jnp.mean(centred * centred, -1, keepdims=True) + epsilon)
    return centred * inverse, inverse


def two_heads(v):
    first = lax.broadcasted_iota(jnp.int32, v.shape, 1) < v.shape[1] // 2
    zero = jnp.zeros_like(v)
    return jnp.concatenate([jnp.where(first, v, zero), jnp.where(first, zero, v)], 0)


def gelu(v):
    u = 0.5 * v
    return u * lax.erf(v * inv_root2) + u


def image_kernel(
    heads, x_ref, g1, s1, wqkv_hbm, wout_hbm, g2, s2, wup_hbm, wdown_hbm, out_ref,
    tok, xs, n, qkv, at, mixed, act, pooled, wqkv, wout, wup, wdown, sems
):
    tokens, images, width = x_ref.shape
    pad = -(-tokens // 8) * 8
    rows = images * pad
    i = pl.program_id(0)
    weights = ((wqkv_hbm, wqkv), (wout_hbm, wout), (wup_hbm, wup), (wdown_hbm, wdown))

    def fetched(k):
        @pl.when(i == 0)
        def _():
            pltpu.make_async_copy(*weights[k], sems.at[k]).wait()

    @pl.when(i == 0)
    def _():
        for k in range(4):
            pltpu.make_async_copy(*weights[k], sems.at[k]).start()
        xs[...] = jnp.zeros_like(xs)
        qkv[rows:, :] = jnp.zeros((qkv.shape[0] - rows, 3 * width), bf16)

    count = tokens * images
    for j in range(width // 128):
        lanes = slice(j * 128, (j + 1) * 128)
        tok[j * count : (j + 1) * count, :] = x_ref[:, :, lanes].astype(f32).reshape(count, 128)
    for j in range(width // 128):
        for k in range(images):
            xs[k * pad : k * pad + tokens, j * 128 : (j + 1) * 128] = tok[pl.ds(j * count + k, tokens, stride=images), :]
    scaled, _ = stats(xs[...])
    n[...] = (scaled * g1[...][None] + s1[...][None]).astype(bf16)
    fetched(0)
    for c in range(3):
        cols = slice(c * width, (c + 1) * width)
        qkv[:rows, cols] = dot(n[...], wqkv[:, cols]).astype(bf16)

    group = 2 * pad
    hd = width // heads
    r_id = lax.broadcasted_iota(jnp.int32, (group, 2 * hd), 0)
    c_id = lax.broadcasted_iota(jnp.int32, (group, 2 * hd), 1)
    same = (r_id < pad) == (c_id < pad)
    inside = jnp.where(c_id < pad, c_id, c_id - pad) < tokens
    keep = same & inside
    first = lax.broadcasted_iota(jnp.int32, (group, 2 * hd), 1) < hd
    factor = hd ** (-0.5) * log2e

    def attend(g, carry):
        rs = pl.ds(pl.multiple_of(g * group, 16), group)
        ks = pl.ds(pl.multiple_of(g * group, 16), 2 * hd)
        for hp in range(heads // 2):
            lanes = slice(hp * 2 * hd, (hp + 1) * 2 * hd)
            q2 = qkv[rs, lanes]
            k2 = two_heads(qkv[ks, slice(width + lanes.start, width + lanes.stop)])
            v2 = two_heads(qkv[ks, slice(2 * width + lanes.start, 2 * width + lanes.stop)])
            s2 = dot_t(q2, k2) * factor
            es, inv = [], []
            for h in range(2):
                s = jnp.where(keep, s2[:, h * 2 * hd : (h + 1) * 2 * hd], -1e30)
                e = jnp.exp2(s - jnp.max(s, -1, keepdims=True))
                inv.append(1.0 / jnp.sum(e, -1, keepdims=True))
                es.append(e.astype(bf16))
            out = dot(jnp.concatenate(es, 1), v2)
            at[rs, lanes] = (out * jnp.where(first, inv[0], inv[1])).astype(bf16)
        return carry

    lax.fori_loop(0, rows // group, attend, 0)
    fetched(1)
    mixed[...] = xs[...] + dot(at[...], wout[...])
    row = lax.broadcasted_iota(jnp.int32, (pad, 1), 0)
    valid = (row < tokens).astype(f32)
    dst = pl.ds(pl.multiple_of(i * images, 8), images)
    m3 = mixed[...].reshape(images, pad, width)
    pooled[dst, :] = jnp.sum(m3 * valid[None], 1)
    scaled, _ = stats(mixed[...])
    normed = ((scaled * g2[...][None] + s2[...][None]).reshape(images, pad, width) * valid[None]).reshape(rows, width)
    n[...] = normed.astype(bf16)
    hidden = wup.shape[1]
    step = 768
    fetched(2)
    for c in range(0, hidden, step):
        a = gelu(dot(n[...], wup[:, c : c + step]))
        act[dst, c : c + step] = jnp.sum(a.reshape(images, pad, step), 1)

    fetched(3)

    @pl.when(i == pl.num_programs(0) - 1)
    def _():
        a = act[...] * (1.0 / tokens)
        hi = a.astype(bf16)
        lo = (a - hi.astype(f32)).astype(bf16)
        count = a.shape[0]
        both = dot(jnp.concatenate([hi, lo], 0), wdown[...])
        e = pooled[...] * (1.0 / tokens) + both[:count] + both[count:]
        out_ref[...] = (e * lax.rsqrt(jnp.sum(e * e, -1, keepdims=True) + epsilon)).astype(bf16)


def image_unit(x, g1, s1, wqkv, wout, g2, s2, wup, wdown, heads=12, images=8):
    count, tokens, width = x.shape
    hidden = wup.shape[1]
    pad = -(-tokens // 8) * 8
    rows = images * pad
    full = lambda a: pl.BlockSpec(a.shape, lambda i: (0,) * a.ndim, pipeline_mode=pl.Buffered(1))
    hbm = pl.BlockSpec(memory_space=pl.ANY)
    args = (jnp.transpose(x, (1, 0, 2)), g1, s1, wqkv, wout, g2, s2, wup, wdown)
    return pl.pallas_call(
        functools.partial(image_kernel, heads),
        name="image",
        grid=(count // images,),
        out_shape=jax.ShapeDtypeStruct((count, width), bf16),
        in_specs=[pl.BlockSpec((tokens, images, width), lambda i: (0, i, 0))]
        + [full(a) if a.ndim == 1 else hbm for a in args[1:]],
        out_specs=pl.BlockSpec((count, width), lambda i: (0, 0)),
        scratch_shapes=[
            pltpu.VMEM((width // 128 * tokens * images, 128), f32),
            pltpu.VMEM((rows, width), f32),
            pltpu.VMEM((rows, width), bf16),
            pltpu.VMEM((rows + 16, 3 * width), bf16),
            pltpu.VMEM((rows, width), bf16),
            pltpu.VMEM((rows, width), f32),
            pltpu.VMEM((count, hidden), f32),
            pltpu.VMEM((count, width), f32),
        ]
        + [pltpu.VMEM(w.shape, bf16) for w in (wqkv, wout, wup, wdown)]
        + [pltpu.SemaphoreType.DMA((4,))],
        compiler_params=pltpu.CompilerParams(vmem_limit_bytes=67043328),
    )(*args)

def dot_0(a, b):
    return lax.dot_general(a, b, (((0,), (0,)), ((), ())), preferred_element_type=f32)


def norm_back(grad_normed, scaled, inverse, gain):
    g = grad_normed * gain
    centre = jnp.mean(g, -1, keepdims=True)
    along = jnp.mean(g * scaled, -1, keepdims=True)
    return inverse * (g - centre - scaled * along)


def token_columns(mask_ref, length_ref, seq):
    captions = mask_ref.shape[1]
    rows = captions * seq
    row = lax.broadcasted_iota(jnp.int32, (rows, captions), 0)
    lane = lax.broadcasted_iota(jnp.int32, (rows, captions), 1)
    length = length_ref[...].astype(f32)
    own = row // seq == lane
    length_t = jnp.sum(jnp.where(own, length, 0.0), -1, keepdims=True)
    spread = dot_t(jnp.where(own, 1.0, 0.0).astype(bf16), mask_ref[...].astype(f32).astype(bf16))
    row = lax.broadcasted_iota(jnp.int32, (rows, seq), 0)
    lane = lax.broadcasted_iota(jnp.int32, (rows, seq), 1)
    mask_t = jnp.sum(jnp.where(row % seq == lane, spread, 0.0), -1, keepdims=True)
    place = (lax.broadcasted_iota(jnp.int32, (rows, 1), 0) % seq).astype(f32)
    weight = jnp.where(place < length_t, mask_t, 0.0)
    count = jnp.sum(weight.reshape(captions, seq, 1), 1)
    return length_t, weight, jnp.maximum(count, 1.0)


def text_attention(heads, seq, group, width, qkv, probs, at, cols):
    hd = width // heads
    r_id = lax.broadcasted_iota(jnp.int32, (group, group), 0)
    c_id = lax.broadcasted_iota(jnp.int32, (group, group), 1)
    same = r_id // seq == c_id // seq
    place = (c_id % seq).astype(f32)
    factor = hd ** (-0.5) * log2e

    def attend(g, carry):
        rs = pl.ds(pl.multiple_of(g * group, 16), group)
        keep = same & (place < cols[rs, 1:2])
        for hp in range(heads // 2):
            lanes = slice(hp * 2 * hd, (hp + 1) * 2 * hd)
            q2 = qkv[rs, lanes]
            k2 = two_heads(qkv[rs, slice(width + lanes.start, width + lanes.stop)])
            v2 = two_heads(qkv[rs, slice(2 * width + lanes.start, 2 * width + lanes.stop)])
            s2 = dot_t(q2, k2) * factor
            ps = []
            for h in range(2):
                s = jnp.where(keep, s2[:, h * group : (h + 1) * group], -1e30)
                e = jnp.exp2(s - jnp.max(s, -1, keepdims=True))
                p = e * (1.0 / jnp.sum(e, -1, keepdims=True))
                probs[rs, pl.ds((hp * 2 + h) * group, group)] = p
                ps.append(p.astype(bf16))
            at[rs, lanes] = dot(jnp.concatenate(ps, 1), v2).astype(bf16)
        return carry

    return attend


inv_root_2pi = 0.3989422804014327


def split_dot(a, w):
    hi = a.astype(bf16)
    lo = (a - hi.astype(f32)).astype(bf16)
    both = dot(jnp.concatenate([hi, lo], 0), w[...])
    return both[: a.shape[0]] + both[a.shape[0] :]


def text_attention_back(heads, group, width, qkv, probs, at):
    hd = width // heads
    scale = hd ** (-0.5)

    def attend(g, carry):
        rs = pl.ds(pl.multiple_of(g * group, 16), group)
        for hp in range(heads // 2):
            lanes = slice(hp * 2 * hd, (hp + 1) * 2 * hd)
            klanes = slice(width + lanes.start, width + lanes.stop)
            vlanes = slice(2 * width + lanes.start, 2 * width + lanes.stop)
            ga = at[rs, lanes]
            q2, k2, v2 = two_heads(qkv[rs, lanes]), two_heads(qkv[rs, klanes]), two_heads(qkv[rs, vlanes])
            dp2 = dot_t(ga, v2)
            ps, ds = [], []
            for h in range(2):
                p = probs[rs, pl.ds((hp * 2 + h) * group, group)]
                dp = dp2[:, h * group : (h + 1) * group]
                ds.append((p * (dp - jnp.sum(dp * p, -1, keepdims=True))).astype(bf16))
                ps.append(p.astype(bf16))
            dv = dot_0(jnp.concatenate(ps, 0), two_heads(ga))
            dq = dot(jnp.concatenate(ds, 1), k2)
            dk = dot_0(jnp.concatenate(ds, 0), q2)
            qkv[rs, lanes] = (dq * scale).astype(bf16)
            qkv[rs, klanes] = (dk * scale).astype(bf16)
            qkv[rs, vlanes] = dv.astype(bf16)
        return carry

    return attend


MESH = pl.DeviceIdType.MESH


COLORS = 3


def color_plans(cb):
    rest = [("c", b) for b in range(1, cb)]
    return [[("r", 1), ("c", 0)] + rest, [("c", 0), ("r", 1)] + rest, rest + [("r", 1), ("c", 0)]]


def log2(n):
    return n.bit_length() - 1


def text_step(
    shape, heads,
    unit_ref, mask_ref, length_ref, g1, s1, g2, s2, x_hbm, wqkv_hbm, wout_hbm, wup_hbm, wdown_hbm,
    gx_hbm, parts_hbm, vecs_ref, images_hbm,
    x_ref, wqkv, wout, wup, wdown, n1, qkv, probs, at, mixed, n2, slope, act, cols,
    images, rowsum, rowsum_c, rowsum_cs, rowsum_r, pooled_act, act_all, gpc_own, gpc_all,
    g_up, g_out, g_qkv, r_up, r_out, r_qkv, d_part, d_recv, d_recv2, final, extra, vec, vec_c, vec_cs, vec_r,
    load_sem, out_sem, ag_send, ag_recv, ps_send, ps_recv, a_send, a_recv, gp_send, gp_recv,
    c_send, c_recv, rs_send, rs_recv, d_send, d_recv_sem, f_send, f_recv, v_send, v_recv,
):
    R, C, captions, seq, group = shape
    rb, cb = log2(R), log2(C)
    r, c = lax.axis_index("row"), lax.axis_index("col")
    rbit = [lax.rem(lax.div(r, 1 << b), 2) for b in range(rb)]
    cbit = [lax.rem(lax.div(c, 1 << b), 2) for b in range(cb)]
    core, xh = rbit[0], rbit[1]
    rows, width = x_ref.shape
    hidden = wup.shape[1]
    half = width // 2
    sub = hidden // (4 * C)

    def flip_r(b):
        return (r + (1 - 2 * rbit[b]) * (1 << b), c)

    def flip_c(b):
        return (r, c + (1 - 2 * cbit[b]) * (1 << b))

    row_peers = [(lax.rem(r + d, R), c) for d in range(1, R)]
    col_peers = [(r, lax.rem(c + d, C)) for d in range(1, C)]

    def remote(src, dst, send, recv, to):
        return pltpu.make_async_remote_copy(
            src_ref=src, dst_ref=dst, send_sem=send, recv_sem=recv, device_id=to, device_id_type=MESH
        )

    sent = []

    def go(copy):
        copy.start()
        sent.append(copy)
        return copy

    barrier = pltpu.get_barrier_semaphore()
    for to in row_peers + col_peers:
        pl.semaphore_signal(barrier, inc=1, device_id=to, device_id_type=MESH)

    loads = []
    for k, (src, dst) in enumerate(
        ((x_hbm, x_ref), (wqkv_hbm, wqkv), (wout_hbm, wout), (wup_hbm, wup), (wdown_hbm, wdown))
    ):
        copy = pltpu.make_async_copy(src, dst, load_sem.at[k])
        copy.start()
        loads.append(copy)

    length_t, weight, count = token_columns(mask_ref, length_ref, seq)
    cols[:, 0:1] = weight
    cols[:, 1:2] = length_t
    loads[0].wait()
    pl.semaphore_wait(barrier, R + C - 2)

    mine = tuple(rbit[b] for b in reversed(range(rb))) + tuple(cbit[b] for b in reversed(range(cb)))
    part = captions // 2
    pairs = captions * R * C
    staged = len(images.shape) < 3 + rb + cb
    gather = images_hbm if staged else images
    for k in range(2):
        if staged:
            copy = pltpu.make_async_copy(unit_ref.at[pl.ds(k * part, part), :], gather.at[(k,) + mine], load_sem.at[5 + k])
            copy.start()
            loads.append(copy)
        else:
            images[(k,) + mine] = unit_ref[k * part : (k + 1) * part, :]
    if staged:
        loads[5].wait()
        loads[6].wait()

    def stage(i):
        if not staged:
            return images[...].reshape(pairs, width)
        lead = 3 + rb + cb - len(images.shape)
        where = tuple((i >> b) & 1 for b in reversed(range(lead)))
        copy = pltpu.make_async_copy(gather.at[where], images, load_sem.at[5])
        copy.start()
        copy.wait()
        return images[...].reshape(pairs >> lead, width)

    stages = pairs // math.prod(images.shape[:-1])
    order = [("c", b) for b in reversed(range(1, cb))]
    tail = [("r", b) for b in reversed(range(1, rb))]
    plans = (order + [("c", 0)] + tail + [("r", 0)], order + tail + [("c", 0)] + [("r", 0)])
    gathered = [set(), set()]
    pending = [None, None]
    phase = [0, 0]

    def gather_step():
        for k in range(2):
            if pending[k] is not None:
                pending[k].wait_recv()
                gathered[k].add(plans[k][phase[k] - 1])
                pending[k] = None
            if phase[k] < len(plans[k]):
                kind, b = plans[k][phase[k]]
                names = [("r", i) for i in reversed(range(rb))] + [("c", i) for i in reversed(range(cb))]
                where = tuple(slice(None) if nm in gathered[k] else v for nm, v in zip(names, mine))
                dst = gather.at[(k,) + where]
                src = unit_ref.at[pl.ds(k * part, part), :] if phase[k] == 0 else dst
                to = flip_r(b) if kind == "r" else flip_c(b)
                pending[k] = go(remote(src, dst, ag_send.at[k, phase[k]], ag_recv.at[k, phase[k]], to))
                phase[k] += 1

    gather_step()
    x = x_ref[...].astype(f32)
    scaled, _ = stats(x)
    n1[...] = (scaled * g1[...][None] + s1[...][None]).astype(bf16)
    loads[1].wait()
    for q in range(3):
        cut = slice(q * width, (q + 1) * width)
        qkv[:, cut] = dot(n1[...], wqkv[:, cut]).astype(bf16)
    gather_step()
    attend = text_attention(heads, seq, group, width, qkv, probs, at, cols)
    groups = rows // group
    lax.fori_loop(0, groups // 2, attend, 0)
    gather_step()
    lax.fori_loop(groups // 2, groups, attend, 0)
    gather_step()
    loads[2].wait()
    mixed[...] = x_ref[...].astype(f32) + dot(at[...], wout[...])
    scaled, _ = stats(mixed[...])
    n2[...] = (scaled * g2[...][None] + s2[...][None]).astype(bf16)
    weight = cols[:, 0:1]
    loads[3].wait()
    for f in range(0, hidden, width):
        cut = slice(f, f + width)
        h = dot(n2[...], wup[:, cut])
        phi = 0.5 + 0.5 * lax.erf(h * inv_root2)
        slope[:, cut] = (phi + h * (jnp.exp(-0.5 * h * h) * inv_root_2pi)).astype(bf16)
        act[:, cut] = jnp.sum((h * phi * weight).reshape(captions, seq, width), 1)
        if f == 2 * width:
            gather_step()
    loads[4].wait()
    pooled = jnp.sum((mixed[...] * weight).reshape(captions, seq, width), 1) + split_dot(act[...], wdown)
    pooled = pooled / count
    inverse = lax.rsqrt(jnp.sum(pooled * pooled, -1, keepdims=True) + epsilon)
    text_unit = (pooled * inverse).astype(bf16)
    span = hidden // C
    for k in range(C):
        pooled_act[k] = act[:, k * span : (k + 1) * span].astype(bf16)
    while pending[0] is not None or pending[1] is not None:
        gather_step()

    t = 2.0 * math.sqrt(width)
    sims = []
    for i in range(stages):
        every = stage(i)
        sims.append(dot_t(text_unit, every))
    e = jnp.exp2(jnp.concatenate(sims, 1) * (t * log2e))
    rowsum[...] = jnp.sum(e, 0, keepdims=True)
    first = [
        go(remote(rowsum, rowsum_c.at[d], ps_send.at[d], ps_recv.at[d], to)) for d, to in enumerate(col_peers)
    ]
    col_scale = 1.0 / jnp.sum(e, -1, keepdims=True)
    acts = []
    for d, to in enumerate(col_peers):
        acts.append(
            go(remote(pooled_act.at[lax.rem(c + d + 1, C)], act_all.at[d], a_send.at[d], a_recv.at[d], to))
        )
    act_all[C - 1] = pooled_act[c]
    total = rowsum[...]
    for d, copy in enumerate(first):
        copy.wait_recv()
        total += rowsum_c[d]
    rowsum_cs[...] = total
    second = [
        go(remote(rowsum_cs, rowsum_r.at[d], ps_send.at[C - 1 + d], ps_recv.at[C - 1 + d], to))
        for d, to in enumerate(row_peers)
    ]
    for d, copy in enumerate(second):
        copy.wait_recv()
        total += rowsum_r[d]
    grad_sim = (e * (1.0 / total + col_scale) * (0.5 / pairs)).astype(bf16)
    share = pairs // stages
    hits = sum(
        dot(grad_sim[:, i * share : (i + 1) * share], every if stages == 1 else stage(i)) for i in range(stages)
    )
    grad_unit = t * hits - (t / pairs) * unit_ref[...].astype(f32)
    along = jnp.sum(grad_unit * pooled, -1, keepdims=True)
    gpc = (inverse * grad_unit - pooled * (inverse * inverse * inverse * along)) / count
    gpc_r = gpc.astype(bf16)
    gpc_own[...] = gpc_r
    gps = [go(remote(gpc_own, gpc_all.at[d], gp_send.at[d], gp_recv.at[d], to)) for d, to in enumerate(col_peers)]
    gpc_all[C - 1] = gpc_r

    def emit(name, row, block):
        scatter = scatters[name]
        sub = scatter.sub
        for i in range(0, block.shape[0], sub):
            index = (row + i) // sub
            to = index // (2 * COLORS)
            bits = tuple((to >> b) & 1 for b in reversed(range(cb)))
            color, xbit = index % (2 * COLORS) // 2, index % 2
            for s in range(2):
                scatter.buf[(s, color, xbit) + bits] = block[i : i + sub, s * half : (s + 1) * half].astype(bf16)

    class Scatter:
        def __init__(self, index, buf, recvs, offset):
            self.index, self.buf, self.recvs, self.offset = index, buf, recvs, offset
            self.sub = buf.shape[-2]
            self.plans = color_plans(cb)
            self.phase = [0] * COLORS
            self.copies = [None] * COLORS
            self.kept = [None] * COLORS
            self.pieces = []

        def start(self, piece):
            bits = (piece // 2, piece % 2)
            n = len(self.pieces)
            assert n == piece
            self.pieces.append(
                go(
                    remote(
                        self.buf.at[(1 - core, slice(None), slice(None)) + bits], self.recvs[0].at[(slice(None), slice(None)) + bits],
                        c_send.at[self.index, piece], c_recv.at[self.index, piece], flip_r(0),
                    )
                )
            )

        def step(self, colors=range(3)):
            for copy in self.pieces:
                copy.wait_recv()
            self.pieces = []
            for k in colors:
                self.advance(k)

        def done(self):
            return min(self.phase) > len(self.plans[0])

        def advance(self, k):
            p = self.phase[k]
            plan = self.plans[k]
            self.phase[k] += 1
            if p == 0:
                before, here = self.buf.at[core, k], self.recvs[0].at[k]
            else:
                self.copies[k].wait_recv()
                before = self.recvs[0].at[(k,) + self.kept[k]] if p == 1 else self.recvs[p - 1][k].at[self.kept[k]]
                here = self.recvs[p][k]
            if p == len(plan):
                rows = slice(self.offset + k * self.sub, self.offset + (k + 1) * self.sub)
                final[core, xh, rows, :] = before[...] + here[...]
                return
            kind, b = plan[p]
            left = [("r", 1)] + [("c", i) for i in reversed(range(cb))]
            for gone in plan[:p]:
                left.remove(gone)
            axis = left.index((kind, b))
            bit = xh if kind == "r" else cbit[b]
            give = (slice(None),) * axis + (1 - bit,)
            keep = (slice(None),) * axis + (bit,)
            here[give] = before[give] + here[give]
            to = flip_r(1) if kind == "r" else flip_c(b)
            self.copies[k] = go(
                remote(
                    here.at[give], self.recvs[p + 1][k],
                    rs_send.at[self.index, k, p], rs_recv.at[self.index, k, p], to,
                )
            )
            here[keep] = before[keep] + here[keep]
            self.kept[k] = keep

    up_rows = COLORS * g_up.shape[-2]
    out_rows = COLORS * g_out.shape[-2]
    down_rows = 2 * sub
    up = Scatter(0, g_up, r_up, 0)
    out = Scatter(1, g_out, r_out, up_rows + down_rows)
    rest = Scatter(2, g_qkv, r_qkv, up_rows + down_rows + out_rows)
    scatters = {"up": up, "out": out, "qkv": rest}
    early, late = slice(0, up_rows + down_rows + out_rows), slice(up_rows + down_rows + out_rows, final.shape[2])

    class Finals:
        def __init__(self, index, rows):
            self.index, self.rows = index, rows

        def start(self):
            for b in range(2, rb):
                there = extra.at[b - 2, self.rows]
                swap = remote(final.at[core, xh, self.rows], there, f_send.at[self.index, b], f_recv.at[self.index, b], flip_r(b))
                swap.start()
                swap.wait()
                final[core, xh, self.rows, :] = final[core, xh, self.rows, :] + there[...]
            here = final.at[core, xh, self.rows]
            self.copy = go(remote(here, here, f_send.at[self.index, 0], f_recv.at[self.index, 0], flip_r(1)))

        def step(self):
            self.copy.wait_recv()
            here = final.at[core, :, self.rows]
            self.copy = go(remote(here, here, f_send.at[self.index, 1], f_recv.at[self.index, 1], flip_r(0)))

        def end(self):
            self.copy.wait_recv()

    for f in range(0, hidden, width):
        cut = slice(f, f + width)
        hh = dot_t(gpc_r, wdown[cut, :])
        spread = jnp.broadcast_to(hh[:, None, :], (captions, seq, width)).reshape(rows, width)
        slope[:, cut] = (spread * weight * slope[:, cut].astype(f32)).astype(bf16)
        emit("up", f, dot_0(slope[:, cut], n2[...]))
        up.start(f // width)
    gn2 = dot_t(slope[...], wup[...])
    up.step()
    scaled, inv2 = stats(mixed[...])
    vec[2:3, :] = jnp.sum(gn2 * scaled, 0, keepdims=True)
    vec[3:4, :] = jnp.sum(gn2, 0, keepdims=True)
    spread = jnp.broadcast_to(gpc[:, None, :], (captions, seq, width)).reshape(rows, width) * weight
    mixed[...] = spread + norm_back(gn2, scaled, inv2, g2[...][None])
    n2[...] = mixed[...].astype(bf16)
    emit("out", 0, dot_0(n2[...], at[...]))
    for piece in range(4):
        out.start(piece)
    at[...] = dot_t(n2[...], wout[...]).astype(bf16)
    attend_back = text_attention_back(heads, group, width, qkv, probs, at)
    lax.fori_loop(0, groups // 2, attend_back, 0)
    up.step()
    out.step()

    for copy in acts + gps:
        copy.wait_recv()
    down = dot_0(act_all[...].reshape(C * captions, span), gpc_all[...].reshape(C * captions, width))
    for j in range(4):
        for s in range(2):
            d_part[s, j // 2, j % 2] = down[j * sub : (j + 1) * sub, s * half : (s + 1) * half].astype(bf16)
    d0 = go(remote(d_part.at[1 - core], d_recv, d_send.at[0], d_recv_sem.at[0], flip_r(0)))

    lax.fori_loop(groups // 2, groups, attend_back, 0)
    up.step(range(2))
    pieces = 0
    for q in range(3):
        emit("qkv", q * width, dot_0(qkv[:, q * width : (q + 1) * width], n1[...]))
        while pieces < 4 * (q + 1) // 3:
            rest.start(pieces)
            pieces += 1
    up.step(range(2, 3))
    out.step()
    d0.wait_recv()
    d_recv[:, 1 - xh] = d_part[core, :, 1 - xh] + d_recv[:, 1 - xh]
    d1 = go(remote(d_recv.at[:, 1 - xh], d_recv2, d_send.at[1], d_recv_sem.at[1], flip_r(1)))
    d_recv[:, xh] = d_part[core, :, xh] + d_recv[:, xh]
    rest.step()
    gn1 = dot_t(qkv[...], wqkv[...])
    up.step()
    scaled, inv1 = stats(x_ref[...].astype(f32))
    vec[0:1, :] = jnp.sum(gn1 * scaled, 0, keepdims=True)
    vec[1:2, :] = jnp.sum(gn1, 0, keepdims=True)
    vfirst = [go(remote(vec, vec_c.at[d], v_send.at[d], v_recv.at[d], to)) for d, to in enumerate(col_peers)]
    out.step()
    mixed[...] = mixed[...] + norm_back(gn1, scaled, inv1, g1[...][None])
    gx_out = pltpu.make_async_copy(mixed, gx_hbm, out_sem.at[0])
    gx_out.start()
    d1.wait_recv()
    for k in range(2):
        final[core, xh, up_rows + k * sub : up_rows + (k + 1) * sub, :] = d_recv[k, xh] + d_recv2[k]
    rest.step()
    while not up.done():
        up.step()
        if not out.done():
            out.step()
    while not out.done():
        out.step()
    first_finals, last_finals = Finals(0, early), Finals(1, late)
    first_finals.start()
    vtotal = vec[...]
    for d, copy in enumerate(vfirst):
        copy.wait_recv()
        vtotal += vec_c[d]
    vec_cs[...] = vtotal
    vsecond = [
        go(remote(vec_cs, vec_r.at[d], v_send.at[C - 1 + d], v_recv.at[C - 1 + d], to)) for d, to in enumerate(row_peers)
    ]
    rest.step()
    first_finals.step()
    while not rest.done():
        rest.step()
    last_finals.start()
    for d, copy in enumerate(vsecond):
        copy.wait_recv()
        vtotal += vec_r[d]
    vecs_ref[...] = vtotal
    first_finals.end()
    last_finals.step()
    last_finals.end()
    parts_out = pltpu.make_async_copy(final, parts_hbm, out_sem.at[1])
    parts_out.start()
    for copy in sent:
        copy.wait_send()
    gx_out.wait()
    parts_out.wait()


def text_call(R, C, unit, tokens, mask, length, g1, s1, wqkv, wout, g2, s2, wup, wdown, heads=12, group=128):
    captions, seq, width = tokens.shape
    rows, hidden = captions * seq, wup.shape[1]
    rb, cb = log2(R), log2(C)
    half, sub, span = width // 2, hidden // (4 * C), hidden // C
    V, S, D = pltpu.VMEM, jax.ShapeDtypeStruct, pltpu.SemaphoreType.DMA
    pairs = captions * R * C
    bits_c = (2,) * cb

    dims, tail = 1 + rb + cb, (captions // 2, width)
    lead = max(log2(pairs // 1024), 0)
    held_dims, staged_dims = dims - lead, dims if lead else 0

    subs = [hidden // (2 * COLORS * C), width // (2 * COLORS * C), 3 * width // (2 * COLORS * C)]

    def recvs(rows):
        phases = len(color_plans(cb)[0]) + 1
        return [V((COLORS, 2) + bits_c + (rows, half), bf16)] + [
            [V((2,) * (1 + cb - p) + (rows, half), bf16) for _ in range(COLORS)] for p in range(1, phases)
        ]

    total = COLORS * sum(subs) + 2 * sub
    vm = pl.BlockSpec(memory_space=pltpu.VMEM)
    hbm = pl.BlockSpec(memory_space=pl.ANY)
    out = pl.pallas_call(
        functools.partial(text_step, (R, C, captions, seq, group), heads),
        name="text",
        in_specs=[vm] * 7 + [hbm] * 5,
        out_specs=(hbm, hbm, vm, hbm),
        out_shape=(S((rows, width), f32), S((2, 2, total, half), bf16), S((4, width), f32), S((2,) * staged_dims + tail, bf16)),
        scratch_shapes=[
            V((rows, width), bf16), V(wqkv.shape, bf16), V(wout.shape, bf16), V(wup.shape, bf16), V(wdown.shape, bf16),
            V((rows, width), bf16), V((rows, 3 * width), bf16), V((rows, heads * group), f32), V((rows, width), bf16),
            V((rows, width), f32), V((rows, width), bf16), V((rows, hidden), bf16), V((captions, hidden), f32), V((rows, 128), f32),
            V((2,) * held_dims + tail, bf16),
            V((1, pairs), f32), V((C - 1, 1, pairs), f32), V((1, pairs), f32), V((R - 1, 1, pairs), f32),
            V((C, captions, span), bf16), V((C, captions, span), bf16), V((captions, width), bf16), V((C, captions, width), bf16),
            *[V((2, COLORS, 2) + bits_c + (n, half), bf16) for n in subs], *[recvs(n) for n in subs],
            V((2, 2, 2, sub, half), bf16), V((2, 2, sub, half), bf16), V((2, sub, half), bf16),
            V((2, 2, total, half), bf16), V((max(rb - 2, 1), total, half), bf16),
            V((4, width), f32), V((C - 1, 4, width), f32), V((4, width), f32), V((R - 1, 4, width), f32),
            D((7,)), D((2,)), D((2, rb + cb)), D((2, rb + cb)), D((R + C - 2,)), D((R + C - 2,)),
            D((C - 1,)), D((C - 1,)), D((C - 1,)), D((C - 1,)),
            D((3, 4)), D((3, 4)), D((3, COLORS, cb + 1)), D((3, COLORS, cb + 1)), D((2,)), D((2,)), D((2, max(rb, 2))), D((2, max(rb, 2))), D((R + C - 2,)), D((R + C - 2,)),
        ],
        compiler_params=pltpu.CompilerParams(collective_id=0, has_side_effects=True, vmem_limit_bytes=67043328),
    )(unit, mask.T, length[None], g1, s1, g2, s2, tokens.reshape(rows, width), wqkv, wout, wup, wdown)
    return out[:3]


def finish_kernel(
    col_size, parts, vecs, shift, gx_in, gx_out, up_out, out_out, qkv_out, down_out, v0, v1, v2, v3,
    gx, up, out, qkv, down, sems
):
    load = pltpu.make_async_copy(gx_in, gx, sems.at[0])
    load.start()
    stores = []

    def store(src, dst):
        copy = pltpu.make_async_copy(src, dst, sems.at[1 + len(stores)])
        copy.start()
        stores.append(copy)

    def blocks(lo, colors, sub):
        for j in range(2 * colors):
            rows = slice(lo + j // 2 * sub, lo + (j // 2 + 1) * sub)
            yield j * sub, jnp.concatenate([parts[0, j % 2, rows, :], parts[1, j % 2, rows, :]], -1).astype(f32)

    def fill(ref, lo, colors):
        sub = ref.shape[0] // (2 * colors)
        for at_row, block in blocks(lo, colors, sub):
            ref[at_row : at_row + sub, :] = block

    hidden_share = down.shape[0]
    fill(down, hidden_share // 2, 2)
    store(down, down_out)
    fill(qkv, hidden_share + out.shape[0] // 2, COLORS)
    store(qkv, qkv_out)
    fill(out, hidden_share, COLORS)
    store(out, out_out)
    load.wait()
    store(gx, gx_out)
    up[...] = jnp.concatenate([block for _, block in blocks(0, COLORS, hidden_share // (2 * COLORS))], 0).T
    store(up, up_out)
    width = vecs.shape[1]
    share = width // col_size
    lane = lax.broadcasted_iota(jnp.int32, (width, share), 1)
    row = lax.broadcasted_iota(jnp.int32, (width, share), 0)
    pick = jnp.where(row == lane + shift[0], 1.0, 0.0)
    own = jnp.dot(vecs[...], pick, precision=lax.Precision.HIGHEST, preferred_element_type=f32)
    for k, v in enumerate((v0, v1, v2, v3)):
        v[...] = own[k : k + 1, :]
    for copy in stores:
        copy.wait()


def finish_call(C, hidden, gx, parts, vecs):
    width = 2 * parts.shape[-1]
    share, hidden_share = width // C, hidden // C
    S, V = jax.ShapeDtypeStruct, pltpu.VMEM
    shift = (lax.axis_index("col") * share).astype(jnp.int32)[None]
    vm = pl.BlockSpec(memory_space=pltpu.VMEM)
    hbm = pl.BlockSpec(memory_space=pl.ANY)
    shapes = [gx.shape, (width, hidden_share), (share, width), (3 * share, width), (hidden_share, width)]
    return pl.pallas_call(
        functools.partial(finish_kernel, C),
        name="finish",
        in_specs=[vm, vm, pl.BlockSpec(memory_space=pltpu.SMEM), hbm],
        out_specs=(hbm,) * 5 + (vm,) * 4,
        out_shape=tuple(S(s, f32) for s in shapes) + (S((1, share), f32),) * 4,
        scratch_shapes=[V(s, f32) for s in shapes] + [pltpu.SemaphoreType.DMA((6,))],
    )(parts, vecs, shift, gx)


def on_device(
    image_tokens, caption_tokens, caption_mask, caption_length,
    image_gain1, image_shift1, image_qkv, image_out, image_gain2, image_shift2, image_up, image_down,
    text_gain1, text_shift1, text_qkv, text_out, text_gain2, text_shift2, text_up, text_down,
):
    R, C = lax.axis_size("row"), lax.axis_size("col")
    unit = image_unit(
        image_tokens, image_gain1, image_shift1, image_qkv, image_out,
        image_gain2, image_shift2, image_up, image_down,
    )
    grad_tokens, parts, vecs = text_call(
        R, C, unit, caption_tokens, caption_mask, caption_length, text_gain1, text_shift1, text_qkv, text_out,
        text_gain2, text_shift2, text_up, text_down,
    )
    grad_tokens, up, out, qkv, down, gain1, shift1, gain2, shift2 = finish_call(C, text_up.shape[1], grad_tokens, parts, vecs)
    return (
        grad_tokens.reshape(caption_tokens.shape), gain1[0], shift1[0], qkv.T, out.T, gain2[0], shift2[0], up, down,
    )


def solution(mesh):
    pair = P(("row", "col"))
    return jax.shard_map(
        on_device,
        mesh=mesh,
        in_specs=(pair,) * 4 + (P(),) * 16,
        out_specs=(pair, P("col"), P("col"), P(None, "col"), P(None, "col"), P("col"), P("col"), P(None, "col"), P("col")),
        check_vma=False,
    )
```

```python
import math, functools
import jax, jax.numpy as jnp
from jax import lax
from jax.experimental import pallas as pl
from jax.experimental.pallas import tpu as pltpu
from jax.sharding import PartitionSpec as P

epsilon = 1e-06
log2e = 1.4426950408889634
inv_root2 = 0.7071067811865476
f32 = jnp.float32
bf16 = jnp.bfloat16


def dot(a, b):
    return jnp.dot(a, b, preferred_element_type=f32)


def dot_t(a, b):
    return lax.dot_general(a, b, (((1,), (1,)), ((), ())), preferred_element_type=f32)


def stats(x):
    centred = x - jnp.mean(x, -1, keepdims=True)
    inverse = lax.rsqrt(jnp.mean(centred * centred, -1, keepdims=True) + epsilon)
    return centred * inverse, inverse


def two_heads(v):
    first = lax.broadcasted_iota(jnp.int32, v.shape, 1) < v.shape[1] // 2
    zero = jnp.zeros_like(v)
    return jnp.concatenate([jnp.where(first, v, zero), jnp.where(first, zero, v)], 0)


def gelu(v):
    u = 0.5 * v
    return u * lax.erf(v * inv_root2) + u


def image_kernel(
    heads, x_ref, g1, s1, wqkv_hbm, wout_hbm, g2, s2, wup_hbm, wdown_hbm, out_ref,
    tok, xs, n, qkv, at, mixed, act, pooled, wqkv, wout, wup, wdown, sems
):
    tokens, images, width = x_ref.shape
    pad = -(-tokens // 8) * 8
    rows = images * pad
    i = pl.program_id(0)
    weights = ((wqkv_hbm, wqkv), (wout_hbm, wout), (wup_hbm, wup), (wdown_hbm, wdown))

    def fetched(k):
        @pl.when(i == 0)
        def _():
            pltpu.make_async_copy(*weights[k], sems.at[k]).wait()

    @pl.when(i == 0)
    def _():
        for k in range(4):
            pltpu.make_async_copy(*weights[k], sems.at[k]).start()
        xs[...] = jnp.zeros_like(xs)
        qkv[rows:, :] = jnp.zeros((qkv.shape[0] - rows, 3 * width), bf16)

    count = tokens * images
    for j in range(width // 128):
        lanes = slice(j * 128, (j + 1) * 128)
        tok[j * count : (j + 1) * count, :] = x_ref[:, :, lanes].astype(f32).reshape(count, 128)
    for j in range(width // 128):
        for k in range(images):
            xs[k * pad : k * pad + tokens, j * 128 : (j + 1) * 128] = tok[pl.ds(j * count + k, tokens, stride=images), :]
    scaled, _ = stats(xs[...])
    n[...] = (scaled * g1[...][None] + s1[...][None]).astype(bf16)
    fetched(0)
    for c in range(3):
        cols = slice(c * width, (c + 1) * width)
        qkv[:rows, cols] = dot(n[...], wqkv[:, cols]).astype(bf16)

    group = 2 * pad
    hd = width // heads
    r_id = lax.broadcasted_iota(jnp.int32, (group, 2 * hd), 0)
    c_id = lax.broadcasted_iota(jnp.int32, (group, 2 * hd), 1)
    same = (r_id < pad) == (c_id < pad)
    inside = jnp.where(c_id < pad, c_id, c_id - pad) < tokens
    keep = same & inside
    first = lax.broadcasted_iota(jnp.int32, (group, 2 * hd), 1) < hd
    factor = hd ** (-0.5) * log2e

    def attend(g, carry):
        rs = pl.ds(pl.multiple_of(g * group, 16), group)
        ks = pl.ds(pl.multiple_of(g * group, 16), 2 * hd)
        for hp in range(heads // 2):
            lanes = slice(hp * 2 * hd, (hp + 1) * 2 * hd)
            q2 = qkv[rs, lanes]
            k2 = two_heads(qkv[ks, slice(width + lanes.start, width + lanes.stop)])
            v2 = two_heads(qkv[ks, slice(2 * width + lanes.start, 2 * width + lanes.stop)])
            s2 = dot_t(q2, k2) * factor
            es, inv = [], []
            for h in range(2):
                s = jnp.where(keep, s2[:, h * 2 * hd : (h + 1) * 2 * hd], -1e30)
                e = jnp.exp2(s - jnp.max(s, -1, keepdims=True))
                inv.append(1.0 / jnp.sum(e, -1, keepdims=True))
                es.append(e.astype(bf16))
            out = dot(jnp.concatenate(es, 1), v2)
            at[rs, lanes] = (out * jnp.where(first, inv[0], inv[1])).astype(bf16)
        return carry

    lax.fori_loop(0, rows // group, attend, 0)
    fetched(1)
    mixed[...] = xs[...] + dot(at[...], wout[...])
    row = lax.broadcasted_iota(jnp.int32, (pad, 1), 0)
    valid = (row < tokens).astype(f32)
    dst = pl.ds(pl.multiple_of(i * images, 8), images)
    m3 = mixed[...].reshape(images, pad, width)
    pooled[dst, :] = jnp.sum(m3 * valid[None], 1)
    scaled, _ = stats(mixed[...])
    normed = ((scaled * g2[...][None] + s2[...][None]).reshape(images, pad, width) * valid[None]).reshape(rows, width)
    n[...] = normed.astype(bf16)
    hidden = wup.shape[1]
    step = 768
    fetched(2)
    for c in range(0, hidden, step):
        a = gelu(dot(n[...], wup[:, c : c + step]))
        act[dst, c : c + step] = jnp.sum(a.reshape(images, pad, step), 1)

    fetched(3)

    @pl.when(i == pl.num_programs(0) - 1)
    def _():
        a = act[...] * (1.0 / tokens)
        hi = a.astype(bf16)
        lo = (a - hi.astype(f32)).astype(bf16)
        count = a.shape[0]
        both = dot(jnp.concatenate([hi, lo], 0), wdown[...])
        e = pooled[...] * (1.0 / tokens) + both[:count] + both[count:]
        out_ref[...] = (e * lax.rsqrt(jnp.sum(e * e, -1, keepdims=True) + epsilon)).astype(bf16)


def image_unit(x, g1, s1, wqkv, wout, g2, s2, wup, wdown, heads=12, images=8):
    count, tokens, width = x.shape
    hidden = wup.shape[1]
    pad = -(-tokens // 8) * 8
    rows = images * pad
    full = lambda a: pl.BlockSpec(a.shape, lambda i: (0,) * a.ndim, pipeline_mode=pl.Buffered(1))
    hbm = pl.BlockSpec(memory_space=pl.ANY)
    args = (jnp.transpose(x, (1, 0, 2)), g1, s1, wqkv, wout, g2, s2, wup, wdown)
    return pl.pallas_call(
        functools.partial(image_kernel, heads),
        name="image",
        grid=(count // images,),
        out_shape=jax.ShapeDtypeStruct((count, width), bf16),
        in_specs=[pl.BlockSpec((tokens, images, width), lambda i: (0, i, 0))]
        + [full(a) if a.ndim == 1 else hbm for a in args[1:]],
        out_specs=pl.BlockSpec((count, width), lambda i: (0, 0)),
        scratch_shapes=[
            pltpu.VMEM((width // 128 * tokens * images, 128), f32),
            pltpu.VMEM((rows, width), f32),
            pltpu.VMEM((rows, width), bf16),
            pltpu.VMEM((rows + 16, 3 * width), bf16),
            pltpu.VMEM((rows, width), bf16),
            pltpu.VMEM((rows, width), f32),
            pltpu.VMEM((count, hidden), f32),
            pltpu.VMEM((count, width), f32),
        ]
        + [pltpu.VMEM(w.shape, bf16) for w in (wqkv, wout, wup, wdown)]
        + [pltpu.SemaphoreType.DMA((4,))],
        compiler_params=pltpu.CompilerParams(vmem_limit_bytes=67043328),
    )(*args)

def dot_0(a, b):
    return lax.dot_general(a, b, (((0,), (0,)), ((), ())), preferred_element_type=f32)


def norm_back(grad_normed, scaled, inverse, gain):
    g = grad_normed * gain
    centre = jnp.mean(g, -1, keepdims=True)
    along = jnp.mean(g * scaled, -1, keepdims=True)
    return inverse * (g - centre - scaled * along)


def token_columns(mask_ref, length_ref, seq):
    captions = mask_ref.shape[1]
    rows = captions * seq
    row = lax.broadcasted_iota(jnp.int32, (rows, captions), 0)
    lane = lax.broadcasted_iota(jnp.int32, (rows, captions), 1)
    length = length_ref[...].astype(f32)
    own = row // seq == lane
    length_t = jnp.sum(jnp.where(own, length, 0.0), -1, keepdims=True)
    spread = dot_t(jnp.where(own, 1.0, 0.0).astype(bf16), mask_ref[...].astype(f32).astype(bf16))
    row = lax.broadcasted_iota(jnp.int32, (rows, seq), 0)
    lane = lax.broadcasted_iota(jnp.int32, (rows, seq), 1)
    mask_t = jnp.sum(jnp.where(row % seq == lane, spread, 0.0), -1, keepdims=True)
    place = (lax.broadcasted_iota(jnp.int32, (rows, 1), 0) % seq).astype(f32)
    weight = jnp.where(place < length_t, mask_t, 0.0)
    count = jnp.sum(weight.reshape(captions, seq, 1), 1)
    return length_t, weight, jnp.maximum(count, 1.0)


def text_attention(heads, seq, group, width, qkv, probs, at, cols):
    hd = width // heads
    r_id = lax.broadcasted_iota(jnp.int32, (group, group), 0)
    c_id = lax.broadcasted_iota(jnp.int32, (group, group), 1)
    same = r_id // seq == c_id // seq
    place = (c_id % seq).astype(f32)
    factor = hd ** (-0.5) * log2e

    def attend(g, carry):
        rs = pl.ds(pl.multiple_of(g * group, 16), group)
        keep = same & (place < cols[rs, 1:2])
        for hp in range(heads // 2):
            lanes = slice(hp * 2 * hd, (hp + 1) * 2 * hd)
            q2 = qkv[rs, lanes]
            k2 = two_heads(qkv[rs, slice(width + lanes.start, width + lanes.stop)])
            v2 = two_heads(qkv[rs, slice(2 * width + lanes.start, 2 * width + lanes.stop)])
            s2 = dot_t(q2, k2) * factor
            ps = []
            for h in range(2):
                s = jnp.where(keep, s2[:, h * group : (h + 1) * group], -1e30)
                e = jnp.exp2(s - jnp.max(s, -1, keepdims=True))
                p = e * (1.0 / jnp.sum(e, -1, keepdims=True))
                probs[rs, pl.ds((hp * 2 + h) * group, group)] = p
                ps.append(p.astype(bf16))
            at[rs, lanes] = dot(jnp.concatenate(ps, 1), v2).astype(bf16)
        return carry

    return attend


inv_root_2pi = 0.3989422804014327


def split_dot(a, w):
    hi = a.astype(bf16)
    lo = (a - hi.astype(f32)).astype(bf16)
    both = dot(jnp.concatenate([hi, lo], 0), w[...])
    return both[: a.shape[0]] + both[a.shape[0] :]


def text_attention_back(heads, group, width, qkv, probs, at):
    hd = width // heads
    scale = hd ** (-0.5)

    def attend(g, carry):
        rs = pl.ds(pl.multiple_of(g * group, 16), group)
        for hp in range(heads // 2):
            lanes = slice(hp * 2 * hd, (hp + 1) * 2 * hd)
            klanes = slice(width + lanes.start, width + lanes.stop)
            vlanes = slice(2 * width + lanes.start, 2 * width + lanes.stop)
            ga = at[rs, lanes]
            q2, k2, v2 = two_heads(qkv[rs, lanes]), two_heads(qkv[rs, klanes]), two_heads(qkv[rs, vlanes])
            dp2 = dot_t(ga, v2)
            ps, ds = [], []
            for h in range(2):
                p = probs[rs, pl.ds((hp * 2 + h) * group, group)]
                dp = dp2[:, h * group : (h + 1) * group]
                ds.append((p * (dp - jnp.sum(dp * p, -1, keepdims=True))).astype(bf16))
                ps.append(p.astype(bf16))
            dv = dot_0(jnp.concatenate(ps, 0), two_heads(ga))
            dq = dot(jnp.concatenate(ds, 1), k2)
            dk = dot_0(jnp.concatenate(ds, 0), q2)
            qkv[rs, lanes] = (dq * scale).astype(bf16)
            qkv[rs, klanes] = (dk * scale).astype(bf16)
            qkv[rs, vlanes] = dv.astype(bf16)
        return carry

    return attend


MESH = pl.DeviceIdType.MESH


COLORS = 3


def color_plans(cb):
    rest = [("c", b) for b in range(1, cb)]
    return [[("r", 1), ("c", 0)] + rest, [("c", 0), ("r", 1)] + rest, rest + [("c", 0), ("r", 1)]]


def log2(n):
    return n.bit_length() - 1


def text_step(
    shape, heads,
    unit_ref, mask_ref, length_ref, g1, s1, g2, s2, x_hbm, wqkv_hbm, wout_hbm, wup_hbm, wdown_hbm,
    gx_hbm, parts_hbm, vecs_ref, images_hbm,
    x_ref, wqkv, wout, wup, wdown, n1, qkv, probs, at, mixed, n2, slope, act, cols,
    images, rowsum, rowsum_c, rowsum_cs, rowsum_r, pooled_act, act_all, gpc_own, gpc_all,
    g_up, g_out, g_qkv, r_up, r_out, r_qkv, d_part, d_recv, d_recv2, final, extra, vec, vec_c, vec_cs, vec_r,
    load_sem, out_sem, ag_send, ag_recv, ps_send, ps_recv, a_send, a_recv, gp_send, gp_recv,
    c_send, c_recv, rs_send, rs_recv, d_send, d_recv_sem, f_send, f_recv, v_send, v_recv,
):
    R, C, captions, seq, group = shape
    rb, cb = log2(R), log2(C)
    r, c = lax.axis_index("row"), lax.axis_index("col")
    rbit = [lax.rem(lax.div(r, 1 << b), 2) for b in range(rb)]
    cbit = [lax.rem(lax.div(c, 1 << b), 2) for b in range(cb)]
    core, xh = rbit[0], rbit[1]
    rows, width = x_ref.shape
    hidden = wup.shape[1]
    half = width // 2
    sub = hidden // (4 * C)

    def flip_r(b):
        return (r + (1 - 2 * rbit[b]) * (1 << b), c)

    def flip_c(b):
        return (r, c + (1 - 2 * cbit[b]) * (1 << b))

    row_peers = [(lax.rem(r + d, R), c) for d in range(1, R)]
    col_peers = [(r, lax.rem(c + d, C)) for d in range(1, C)]

    def remote(src, dst, send, recv, to):
        return pltpu.make_async_remote_copy(
            src_ref=src, dst_ref=dst, send_sem=send, recv_sem=recv, device_id=to, device_id_type=MESH
        )

    sent = []

    def go(copy):
        copy.start()
        sent.append(copy)
        return copy

    barrier = pltpu.get_barrier_semaphore()
    for to in row_peers + col_peers:
        pl.semaphore_signal(barrier, inc=1, device_id=to, device_id_type=MESH)

    loads = []
    for k, (src, dst) in enumerate(
        ((x_hbm, x_ref), (wqkv_hbm, wqkv), (wout_hbm, wout), (wup_hbm, wup), (wdown_hbm, wdown))
    ):
        copy = pltpu.make_async_copy(src, dst, load_sem.at[k])
        copy.start()
        loads.append(copy)

    length_t, weight, count = token_columns(mask_ref, length_ref, seq)
    cols[:, 0:1] = weight
    cols[:, 1:2] = length_t
    loads[0].wait()
    pl.semaphore_wait(barrier, R + C - 2)

    mine = tuple(rbit[b] for b in reversed(range(rb))) + tuple(cbit[b] for b in reversed(range(cb)))
    part = captions // 2
    pairs = captions * R * C
    staged = len(images.shape) < 3 + rb + cb
    gather = images_hbm if staged else images
    for k in range(2):
        if staged:
            copy = pltpu.make_async_copy(unit_ref.at[pl.ds(k * part, part), :], gather.at[(k,) + mine], load_sem.at[5 + k])
            copy.start()
            loads.append(copy)
        else:
            images[(k,) + mine] = unit_ref[k * part : (k + 1) * part, :]
    if staged:
        loads[5].wait()
        loads[6].wait()

    def stage(i):
        if not staged:
            return images[...].reshape(pairs, width)
        lead = 3 + rb + cb - len(images.shape)
        where = tuple((i >> b) & 1 for b in reversed(range(lead)))
        copy = pltpu.make_async_copy(gather.at[where], images, load_sem.at[5])
        copy.start()
        copy.wait()
        return images[...].reshape(pairs >> lead, width)

    stages = pairs // math.prod(images.shape[:-1])
    order = [("c", b) for b in reversed(range(1, cb))]
    tail = [("r", b) for b in reversed(range(1, rb))]
    plans = (order + [("c", 0)] + tail + [("r", 0)], order + tail + [("c", 0)] + [("r", 0)])
    gathered = [set(), set()]
    pending = [None, None]
    phase = [0, 0]

    def gather_step():
        for k in range(2):
            if pending[k] is not None:
                pending[k].wait_recv()
                gathered[k].add(plans[k][phase[k] - 1])
                pending[k] = None
            if phase[k] < len(plans[k]):
                kind, b = plans[k][phase[k]]
                names = [("r", i) for i in reversed(range(rb))] + [("c", i) for i in reversed(range(cb))]
                where = tuple(slice(None) if nm in gathered[k] else v for nm, v in zip(names, mine))
                dst = gather.at[(k,) + where]
                src = unit_ref.at[pl.ds(k * part, part), :] if phase[k] == 0 else dst
                to = flip_r(b) if kind == "r" else flip_c(b)
                pending[k] = go(remote(src, dst, ag_send.at[k, phase[k]], ag_recv.at[k, phase[k]], to))
                phase[k] += 1

    gather_step()
    x = x_ref[...].astype(f32)
    scaled, _ = stats(x)
    n1[...] = (scaled * g1[...][None] + s1[...][None]).astype(bf16)
    loads[1].wait()
    for q in range(3):
        cut = slice(q * width, (q + 1) * width)
        qkv[:, cut] = dot(n1[...], wqkv[:, cut]).astype(bf16)
    gather_step()
    attend = text_attention(heads, seq, group, width, qkv, probs, at, cols)
    groups = rows // group
    lax.fori_loop(0, groups, attend, 0)
    gather_step()
    loads[2].wait()
    mixed[...] = x_ref[...].astype(f32) + dot(at[...], wout[...])
    scaled, _ = stats(mixed[...])
    n2[...] = (scaled * g2[...][None] + s2[...][None]).astype(bf16)
    weight = cols[:, 0:1]
    loads[3].wait()
    gather_step()

    def up_block(f, carry):
        cut = pl.ds(pl.multiple_of(f * width, 128), width)
        h = dot(n2[...], wup[:, cut])
        phi = 0.5 + 0.5 * lax.erf(h * inv_root2)
        slope[:, cut] = (phi + h * (jnp.exp(-0.5 * h * h) * inv_root_2pi)).astype(bf16)
        act[:, cut] = jnp.sum((h * phi * cols[:, 0:1]).reshape(captions, seq, width), 1)
        return carry

    lax.fori_loop(0, hidden // width, up_block, 0)
    gather_step()
    loads[4].wait()
    pooled = jnp.sum((mixed[...] * weight).reshape(captions, seq, width), 1) + split_dot(act[...], wdown)
    pooled = pooled / count
    inverse = lax.rsqrt(jnp.sum(pooled * pooled, -1, keepdims=True) + epsilon)
    text_unit = (pooled * inverse).astype(bf16)
    span = hidden // C
    for k in range(C):
        pooled_act[k] = act[:, k * span : (k + 1) * span].astype(bf16)
    while pending[0] is not None or pending[1] is not None:
        gather_step()

    t = 2.0 * math.sqrt(width)
    sims = []
    for i in range(stages):
        every = stage(i)
        sims.append(dot_t(text_unit, every))
    e = jnp.exp2(jnp.concatenate(sims, 1) * (t * log2e))
    rowsum[...] = jnp.sum(e, 0, keepdims=True)
    first = [
        go(remote(rowsum, rowsum_c.at[d], ps_send.at[d], ps_recv.at[d], to)) for d, to in enumerate(col_peers)
    ]
    col_scale = 1.0 / jnp.sum(e, -1, keepdims=True)
    acts = []
    for d, to in enumerate(col_peers):
        acts.append(
            go(remote(pooled_act.at[lax.rem(c + d + 1, C)], act_all.at[d], a_send.at[d], a_recv.at[d], to))
        )
    act_all[C - 1] = pooled_act[c]
    total = rowsum[...]
    for d, copy in enumerate(first):
        copy.wait_recv()
        total += rowsum_c[d]
    rowsum_cs[...] = total
    second = [
        go(remote(rowsum_cs, rowsum_r.at[d], ps_send.at[C - 1 + d], ps_recv.at[C - 1 + d], to))
        for d, to in enumerate(row_peers)
    ]
    for d, copy in enumerate(second):
        copy.wait_recv()
        total += rowsum_r[d]
    grad_sim = (e * (1.0 / total + col_scale) * (0.5 / pairs)).astype(bf16)
    share = pairs // stages
    hits = sum(
        dot(grad_sim[:, i * share : (i + 1) * share], every if stages == 1 else stage(i)) for i in range(stages)
    )
    grad_unit = t * hits - (t / pairs) * unit_ref[...].astype(f32)
    along = jnp.sum(grad_unit * pooled, -1, keepdims=True)
    gpc = (inverse * grad_unit - pooled * (inverse * inverse * inverse * along)) / count
    gpc_r = gpc.astype(bf16)
    gpc_own[...] = gpc_r
    gps = [go(remote(gpc_own, gpc_all.at[d], gp_send.at[d], gp_recv.at[d], to)) for d, to in enumerate(col_peers)]
    gpc_all[C - 1] = gpc_r

    def emit(name, row, block, lead=()):
        scatter = scatters[name]
        sub = scatter.sub
        for i in range(0, block.shape[0], sub):
            index = (row + i) // sub
            to = index // (2 * COLORS)
            bits = lead + tuple((to >> b) & 1 for b in reversed(range(cb - len(lead))))
            color, xbit = index % (2 * COLORS) // 2, index % 2
            for s in range(2):
                scatter.buf[(s, color, xbit) + bits] = block[i : i + sub, s * half : (s + 1) * half].astype(bf16)

    class Scatter:
        def __init__(self, index, buf, recvs, offset):
            self.index, self.buf, self.recvs, self.offset = index, buf, recvs, offset
            self.sub = buf.shape[-2]
            self.plans = color_plans(cb)
            self.phase = [0] * COLORS
            self.copies = [None] * COLORS
            self.kept = [None] * COLORS
            self.pieces = []

        def start(self, piece):
            self.copy(piece).start()
            if isinstance(piece, int):
                self.started(piece)

        def started(self, piece):
            self.pieces.append(self.copy(piece))
            sent.append(self.pieces[-1])

        def copy(self, piece):
            bits = (piece // 2, piece % 2) if isinstance(piece, int) else (lax.div(piece, 2), lax.rem(piece, 2))
            return remote(
                self.buf.at[(1 - core, slice(None), slice(None)) + bits], self.recvs[0].at[(slice(None), slice(None)) + bits],
                c_send.at[self.index, piece], c_recv.at[self.index, piece], flip_r(0),
            )

        def step(self, colors=range(3)):
            for copy in self.pieces:
                copy.wait_recv()
            self.pieces = []
            for k in colors:
                self.advance(k)

        def done(self):
            return min(self.phase) > len(self.plans[0])

        def advance(self, k):
            p = self.phase[k]
            plan = self.plans[k]
            self.phase[k] += 1
            if p == 0:
                before, here = self.buf.at[core, k], self.recvs[0].at[k]
            else:
                self.copies[k].wait_recv()
                before = self.recvs[0].at[(k,) + self.kept[k]] if p == 1 else self.recvs[p - 1][k].at[self.kept[k]]
                here = self.recvs[p][k]
            if p == len(plan):
                rows = slice(self.offset + k * self.sub, self.offset + (k + 1) * self.sub)
                final[core, xh, rows, :] = before[...] + here[...]
                return
            kind, b = plan[p]
            left = [("r", 1)] + [("c", i) for i in reversed(range(cb))]
            for gone in plan[:p]:
                left.remove(gone)
            axis = left.index((kind, b))
            bit = xh if kind == "r" else cbit[b]
            give = (slice(None),) * axis + (1 - bit,)
            keep = (slice(None),) * axis + (bit,)
            here[give] = before[give] + here[give]
            to = flip_r(1) if kind == "r" else flip_c(b)
            self.copies[k] = go(
                remote(
                    here.at[give], self.recvs[p + 1][k],
                    rs_send.at[self.index, k, p], rs_recv.at[self.index, k, p], to,
                )
            )
            here[keep] = before[keep] + here[keep]
            self.kept[k] = keep

    up_rows = COLORS * g_up.shape[-2]
    out_rows = COLORS * g_out.shape[-2]
    down_rows = 2 * sub
    up = Scatter(0, g_up, r_up, 0)
    out = Scatter(1, g_out, r_out, up_rows + down_rows)
    rest = Scatter(2, g_qkv, r_qkv, up_rows + down_rows + out_rows)
    scatters = {"up": up, "out": out, "qkv": rest}
    early, late = slice(0, up_rows + down_rows + out_rows), slice(up_rows + down_rows + out_rows, final.shape[2])

    class Finals:
        def __init__(self, index, rows):
            self.index, self.rows = index, rows

        def start(self):
            for b in range(2, rb):
                there = extra.at[b - 2, self.rows]
                swap = remote(final.at[core, xh, self.rows], there, f_send.at[self.index, b], f_recv.at[self.index, b], flip_r(b))
                swap.start()
                swap.wait()
                final[core, xh, self.rows, :] = final[core, xh, self.rows, :] + there[...]
            here = final.at[core, xh, self.rows]
            self.copy = go(remote(here, here, f_send.at[self.index, 0], f_recv.at[self.index, 0], flip_r(1)))

        def step(self):
            self.copy.wait_recv()
            here = final.at[core, :, self.rows]
            self.copy = go(remote(here, here, f_send.at[self.index, 1], f_recv.at[self.index, 1], flip_r(0)))

        def end(self):
            self.copy.wait_recv()

    def up_back(f, carry):
        cut = pl.ds(pl.multiple_of(f * width, 128), width)
        hh = dot_t(gpc_own[...], wdown[cut, :])
        spread = jnp.broadcast_to(hh[:, None, :], (captions, seq, width)).reshape(rows, width)
        slope[:, cut] = (spread * cols[:, 0:1] * slope[:, cut].astype(f32)).astype(bf16)
        emit("up", 0, dot_0(slope[:, cut], n2[...]), (lax.div(f, 2), lax.rem(f, 2)))
        up.start(f)
        return carry

    lax.fori_loop(0, 4, up_back, 0)
    for piece in range(4):
        up.started(piece)
    gn2 = dot_t(slope[...], wup[...])
    up.step()
    scaled, inv2 = stats(mixed[...])
    vec[2:3, :] = jnp.sum(gn2 * scaled, 0, keepdims=True)
    vec[3:4, :] = jnp.sum(gn2, 0, keepdims=True)
    spread = jnp.broadcast_to(gpc[:, None, :], (captions, seq, width)).reshape(rows, width) * weight
    mixed[...] = spread + norm_back(gn2, scaled, inv2, g2[...][None])
    n2[...] = mixed[...].astype(bf16)
    emit("out", 0, dot_0(n2[...], at[...]))
    for piece in range(4):
        out.start(piece)
    at[...] = dot_t(n2[...], wout[...]).astype(bf16)
    attend_back = text_attention_back(heads, group, width, qkv, probs, at)
    lax.fori_loop(0, groups // 2, attend_back, 0)
    up.step()
    out.step()

    for copy in acts + gps:
        copy.wait_recv()
    down = dot_0(act_all[...].reshape(C * captions, span), gpc_all[...].reshape(C * captions, width))
    for j in range(4):
        for s in range(2):
            d_part[s, j // 2, j % 2] = down[j * sub : (j + 1) * sub, s * half : (s + 1) * half].astype(bf16)
    d0 = go(remote(d_part.at[1 - core], d_recv, d_send.at[0], d_recv_sem.at[0], flip_r(0)))

    lax.fori_loop(groups // 2, groups, attend_back, 0)
    up.step(range(2))
    pieces = 0
    for q in range(3):
        emit("qkv", q * width, dot_0(qkv[:, q * width : (q + 1) * width], n1[...]))
        while pieces < 4 * (q + 1) // 3:
            rest.start(pieces)
            pieces += 1
    up.step(range(2, 3))
    out.step()
    d0.wait_recv()
    d_recv[:, 1 - xh] = d_part[core, :, 1 - xh] + d_recv[:, 1 - xh]
    d1 = go(remote(d_recv.at[:, 1 - xh], d_recv2, d_send.at[1], d_recv_sem.at[1], flip_r(1)))
    d_recv[:, xh] = d_part[core, :, xh] + d_recv[:, xh]
    rest.step()
    gn1 = dot_t(qkv[...], wqkv[...])
    up.step()
    scaled, inv1 = stats(x_ref[...].astype(f32))
    vec[0:1, :] = jnp.sum(gn1 * scaled, 0, keepdims=True)
    vec[1:2, :] = jnp.sum(gn1, 0, keepdims=True)
    vfirst = [go(remote(vec, vec_c.at[d], v_send.at[d], v_recv.at[d], to)) for d, to in enumerate(col_peers)]
    out.step()
    mixed[...] = mixed[...] + norm_back(gn1, scaled, inv1, g1[...][None])
    gx_out = pltpu.make_async_copy(mixed, gx_hbm, out_sem.at[0])
    gx_out.start()
    d1.wait_recv()
    for k in range(2):
        final[core, xh, up_rows + k * sub : up_rows + (k + 1) * sub, :] = d_recv[k, xh] + d_recv2[k]
    rest.step()
    while not up.done():
        up.step()
        if not out.done():
            out.step()
    while not out.done():
        out.step()
    first_finals, last_finals = Finals(0, early), Finals(1, late)
    first_finals.start()
    vtotal = vec[...]
    for d, copy in enumerate(vfirst):
        copy.wait_recv()
        vtotal += vec_c[d]
    vec_cs[...] = vtotal
    vsecond = [
        go(remote(vec_cs, vec_r.at[d], v_send.at[C - 1 + d], v_recv.at[C - 1 + d], to)) for d, to in enumerate(row_peers)
    ]
    rest.step()
    first_finals.step()
    while not rest.done():
        rest.step()
    last_finals.start()
    for d, copy in enumerate(vsecond):
        copy.wait_recv()
        vtotal += vec_r[d]
    vecs_ref[...] = vtotal
    first_finals.end()
    last_finals.step()
    last_finals.end()
    parts_out = pltpu.make_async_copy(final, parts_hbm, out_sem.at[1])
    parts_out.start()
    for copy in sent:
        copy.wait_send()
    gx_out.wait()
    parts_out.wait()


def text_call(R, C, unit, tokens, mask, length, g1, s1, wqkv, wout, g2, s2, wup, wdown, heads=12, group=128):
    captions, seq, width = tokens.shape
    rows, hidden = captions * seq, wup.shape[1]
    rb, cb = log2(R), log2(C)
    half, sub, span = width // 2, hidden // (4 * C), hidden // C
    V, S, D = pltpu.VMEM, jax.ShapeDtypeStruct, pltpu.SemaphoreType.DMA
    pairs = captions * R * C
    bits_c = (2,) * cb

    dims, tail = 1 + rb + cb, (captions // 2, width)
    lead = max(log2(pairs // 1024), 0)
    held_dims, staged_dims = dims - lead, dims if lead else 0

    subs = [hidden // (2 * COLORS * C), width // (2 * COLORS * C), 3 * width // (2 * COLORS * C)]

    def recvs(rows):
        phases = len(color_plans(cb)[0]) + 1
        return [V((COLORS, 2) + bits_c + (rows, half), bf16)] + [
            [V((2,) * (1 + cb - p) + (rows, half), bf16) for _ in range(COLORS)] for p in range(1, phases)
        ]

    total = COLORS * sum(subs) + 2 * sub
    vm = pl.BlockSpec(memory_space=pltpu.VMEM)
    hbm = pl.BlockSpec(memory_space=pl.ANY)
    out = pl.pallas_call(
        functools.partial(text_step, (R, C, captions, seq, group), heads),
        name="text",
        in_specs=[vm] * 7 + [hbm] * 5,
        out_specs=(hbm, hbm, vm, hbm),
        out_shape=(S((rows, width), f32), S((2, 2, total, half), bf16), S((4, width), f32), S((2,) * staged_dims + tail, bf16)),
        scratch_shapes=[
            V((rows, width), bf16), V(wqkv.shape, bf16), V(wout.shape, bf16), V(wup.shape, bf16), V(wdown.shape, bf16),
            V((rows, width), bf16), V((rows, 3 * width), bf16), V((rows, heads * group), f32), V((rows, width), bf16),
            V((rows, width), f32), V((rows, width), bf16), V((rows, hidden), bf16), V((captions, hidden), f32), V((rows, 128), f32),
            V((2,) * held_dims + tail, bf16),
            V((1, pairs), f32), V((C - 1, 1, pairs), f32), V((1, pairs), f32), V((R - 1, 1, pairs), f32),
            V((C, captions, span), bf16), V((C, captions, span), bf16), V((captions, width), bf16), V((C, captions, width), bf16),
            *[V((2, COLORS, 2) + bits_c + (n, half), bf16) for n in subs], *[recvs(n) for n in subs],
            V((2, 2, 2, sub, half), bf16), V((2, 2, sub, half), bf16), V((2, sub, half), bf16),
            V((2, 2, total, half), bf16), V((max(rb - 2, 1), total, half), bf16),
            V((4, width), f32), V((C - 1, 4, width), f32), V((4, width), f32), V((R - 1, 4, width), f32),
            D((7,)), D((2,)), D((2, rb + cb)), D((2, rb + cb)), D((R + C - 2,)), D((R + C - 2,)),
            D((C - 1,)), D((C - 1,)), D((C - 1,)), D((C - 1,)),
            D((3, 4)), D((3, 4)), D((3, COLORS, cb + 1)), D((3, COLORS, cb + 1)), D((2,)), D((2,)), D((2, max(rb, 2))), D((2, max(rb, 2))), D((R + C - 2,)), D((R + C - 2,)),
        ],
        compiler_params=pltpu.CompilerParams(collective_id=0, has_side_effects=True, vmem_limit_bytes=67043328),
    )(unit, mask.T, length[None], g1, s1, g2, s2, tokens.reshape(rows, width), wqkv, wout, wup, wdown)
    return out[:3]


def finish_kernel(
    col_size, parts, vecs, shift, gx_in, gx_out, up_out, out_out, qkv_out, down_out, v0, v1, v2, v3,
    gx, up, out, qkv, down, sems
):
    load = pltpu.make_async_copy(gx_in, gx, sems.at[0])
    load.start()
    stores = []

    def store(src, dst):
        copy = pltpu.make_async_copy(src, dst, sems.at[1 + len(stores)])
        copy.start()
        stores.append(copy)

    def blocks(lo, colors, sub):
        for j in range(2 * colors):
            rows = slice(lo + j // 2 * sub, lo + (j // 2 + 1) * sub)
            yield j * sub, jnp.concatenate([parts[0, j % 2, rows, :], parts[1, j % 2, rows, :]], -1).astype(f32)

    def fill(ref, lo, colors):
        sub = ref.shape[0] // (2 * colors)
        for at_row, block in blocks(lo, colors, sub):
            ref[at_row : at_row + sub, :] = block

    hidden_share = down.shape[0]
    fill(down, hidden_share // 2, 2)
    store(down, down_out)
    fill(qkv, hidden_share + out.shape[0] // 2, COLORS)
    store(qkv, qkv_out)
    fill(out, hidden_share, COLORS)
    store(out, out_out)
    load.wait()
    store(gx, gx_out)
    up[...] = jnp.concatenate([block for _, block in blocks(0, COLORS, hidden_share // (2 * COLORS))], 0).T
    store(up, up_out)
    width = vecs.shape[1]
    share = width // col_size
    lane = lax.broadcasted_iota(jnp.int32, (width, share), 1)
    row = lax.broadcasted_iota(jnp.int32, (width, share), 0)
    pick = jnp.where(row == lane + shift[0], 1.0, 0.0)
    own = jnp.dot(vecs[...], pick, precision=lax.Precision.HIGHEST, preferred_element_type=f32)
    for k, v in enumerate((v0, v1, v2, v3)):
        v[...] = own[k : k + 1, :]
    for copy in stores:
        copy.wait()


def finish_call(C, hidden, gx, parts, vecs):
    width = 2 * parts.shape[-1]
    share, hidden_share = width // C, hidden // C
    S, V = jax.ShapeDtypeStruct, pltpu.VMEM
    shift = (lax.axis_index("col") * share).astype(jnp.int32)[None]
    vm = pl.BlockSpec(memory_space=pltpu.VMEM)
    hbm = pl.BlockSpec(memory_space=pl.ANY)
    shapes = [gx.shape, (width, hidden_share), (share, width), (3 * share, width), (hidden_share, width)]
    return pl.pallas_call(
        functools.partial(finish_kernel, C),
        name="finish",
        in_specs=[vm, vm, pl.BlockSpec(memory_space=pltpu.SMEM), hbm],
        out_specs=(hbm,) * 5 + (vm,) * 4,
        out_shape=tuple(S(s, f32) for s in shapes) + (S((1, share), f32),) * 4,
        scratch_shapes=[V(s, f32) for s in shapes] + [pltpu.SemaphoreType.DMA((6,))],
    )(parts, vecs, shift, gx)


def on_device(
    image_tokens, caption_tokens, caption_mask, caption_length,
    image_gain1, image_shift1, image_qkv, image_out, image_gain2, image_shift2, image_up, image_down,
    text_gain1, text_shift1, text_qkv, text_out, text_gain2, text_shift2, text_up, text_down,
):
    R, C = lax.axis_size("row"), lax.axis_size("col")
    unit = image_unit(
        image_tokens, image_gain1, image_shift1, image_qkv, image_out,
        image_gain2, image_shift2, image_up, image_down,
    )
    grad_tokens, parts, vecs = text_call(
        R, C, unit, caption_tokens, caption_mask, caption_length, text_gain1, text_shift1, text_qkv, text_out,
        text_gain2, text_shift2, text_up, text_down,
    )
    grad_tokens, up, out, qkv, down, gain1, shift1, gain2, shift2 = finish_call(C, text_up.shape[1], grad_tokens, parts, vecs)
    return (
        grad_tokens.reshape(caption_tokens.shape), gain1[0], shift1[0], qkv.T, out.T, gain2[0], shift2[0], up, down,
    )


def solution(mesh):
    pair = P(("row", "col"))
    return jax.shard_map(
        on_device,
        mesh=mesh,
        in_specs=(pair,) * 4 + (P(),) * 16,
        out_specs=(pair, P("col"), P("col"), P(None, "col"), P(None, "col"), P("col"), P("col"), P(None, "col"), P("col")),
        check_vma=False,
    )
```

```python
import math, functools
import jax, jax.numpy as jnp
from jax import lax
from jax.experimental import pallas as pl
from jax.experimental.pallas import tpu as pltpu
from jax.sharding import PartitionSpec as P

epsilon = 1e-06
log2e = 1.4426950408889634
inv_root2 = 0.7071067811865476
f32 = jnp.float32
bf16 = jnp.bfloat16


def dot(a, b):
    return jnp.dot(a, b, preferred_element_type=f32)


def dot_t(a, b):
    return lax.dot_general(a, b, (((1,), (1,)), ((), ())), preferred_element_type=f32)


def stats(x):
    centred = x - jnp.mean(x, -1, keepdims=True)
    inverse = lax.rsqrt(jnp.mean(centred * centred, -1, keepdims=True) + epsilon)
    return centred * inverse, inverse


def two_heads(v):
    first = lax.broadcasted_iota(jnp.int32, v.shape, 1) < v.shape[1] // 2
    zero = jnp.zeros_like(v)
    return jnp.concatenate([jnp.where(first, v, zero), jnp.where(first, zero, v)], 0)


def gelu(v):
    u = 0.5 * v
    return u * lax.erf(v * inv_root2) + u


def image_kernel(
    heads, x_ref, g1, s1, wqkv_hbm, wout_hbm, g2, s2, wup_hbm, wdown_hbm, out_ref,
    tok, xs, n, qkv, at, mixed, act, pooled, wqkv, wout, wup, wdown, sems
):
    tokens, images, width = x_ref.shape
    pad = -(-tokens // 8) * 8
    rows = images * pad
    i = pl.program_id(0)
    weights = ((wqkv_hbm, wqkv), (wout_hbm, wout), (wup_hbm, wup), (wdown_hbm, wdown))

    def fetched(k):
        @pl.when(i == 0)
        def _():
            pltpu.make_async_copy(*weights[k], sems.at[k]).wait()
            for later in range(1, 4 if k == 0 else 0):
                pltpu.make_async_copy(*weights[later], sems.at[later]).start()

    @pl.when(i == 0)
    def _():
        pltpu.make_async_copy(*weights[0], sems.at[0]).start()
        xs[...] = jnp.zeros_like(xs)
        qkv[rows:, :] = jnp.zeros((qkv.shape[0] - rows, 3 * width), bf16)

    count = tokens * images
    for j in range(width // 128):
        lanes = slice(j * 128, (j + 1) * 128)
        tok[j * count : (j + 1) * count, :] = x_ref[:, :, lanes].astype(f32).reshape(count, 128)
    for j in range(width // 128):
        for k in range(images):
            xs[k * pad : k * pad + tokens, j * 128 : (j + 1) * 128] = tok[pl.ds(j * count + k, tokens, stride=images), :]
    scaled, _ = stats(xs[...])
    n[...] = (scaled * g1[...][None] + s1[...][None]).astype(bf16)
    fetched(0)
    for c in range(3):
        cols = slice(c * width, (c + 1) * width)
        qkv[:rows, cols] = dot(n[...], wqkv[:, cols]).astype(bf16)

    group = 2 * pad
    hd = width // heads
    r_id = lax.broadcasted_iota(jnp.int32, (group, 2 * hd), 0)
    c_id = lax.broadcasted_iota(jnp.int32, (group, 2 * hd), 1)
    same = (r_id < pad) == (c_id < pad)
    inside = jnp.where(c_id < pad, c_id, c_id - pad) < tokens
    keep = same & inside
    ones = two_heads(jnp.ones((2 * hd, 2 * hd), bf16))
    factor = hd ** (-0.5) * log2e

    def attend(g, carry):
        rs = pl.ds(pl.multiple_of(g * group, 16), group)
        ks = pl.ds(pl.multiple_of(g * group, 16), 2 * hd)
        def scores(hp):
            k2 = two_heads(qkv[ks, width + hp * 2 * hd : width + (hp + 1) * 2 * hd])
            return dot_t(qkv[rs, hp * 2 * hd : (hp + 1) * 2 * hd], k2)

        def values(hp, es):
            v2 = two_heads(qkv[ks, 2 * width + hp * 2 * hd : 2 * width + (hp + 1) * 2 * hd])
            out = dot(es, jnp.concatenate([v2, ones], 1))
            at[rs, hp * 2 * hd : (hp + 1) * 2 * hd] = (out[:, : 2 * hd] / out[:, 2 * hd :]).astype(bf16)

        after, before = scores(0), None
        for hp in range(heads // 2):
            s2 = after
            if hp + 1 < heads // 2:
                after = scores(hp + 1)
            es = []
            for h in range(2):
                s = jnp.where(keep, s2[:, h * 2 * hd : (h + 1) * 2 * hd] * factor, -1e30)
                es.append(jnp.exp2(s - jnp.max(s, -1, keepdims=True)).astype(bf16))
            if before is not None:
                values(hp - 1, before)
            before = jnp.concatenate(es, 1)
        values(heads // 2 - 1, before)
        return carry

    lax.fori_loop(0, rows // group, attend, 0)
    fetched(1)
    mixed[...] = xs[...] + dot(at[...], wout[...])
    row = lax.broadcasted_iota(jnp.int32, (pad, 1), 0)
    valid = (row < tokens).astype(f32)
    dst = pl.ds(pl.multiple_of(i * images, 8), images)
    m3 = mixed[...].reshape(images, pad, width)
    pooled[dst, :] = jnp.sum(m3 * valid[None], 1)
    scaled, _ = stats(mixed[...])
    normed = ((scaled * g2[...][None] + s2[...][None]).reshape(images, pad, width) * valid[None]).reshape(rows, width)
    n[...] = normed.astype(bf16)
    hidden = wup.shape[1]
    step = 768
    fetched(2)
    for c in range(0, hidden, step):
        a = gelu(dot(n[...], wup[:, c : c + step]))
        act[dst, c : c + step] = jnp.sum(a.reshape(images, pad, step), 1)

    fetched(3)

    @pl.when(i == pl.num_programs(0) - 1)
    def _():
        a = act[...] * (1.0 / tokens)
        hi = a.astype(bf16)
        lo = (a - hi.astype(f32)).astype(bf16)
        count = a.shape[0]
        both = dot(jnp.concatenate([hi, lo], 0), wdown[...])
        e = pooled[...] * (1.0 / tokens) + both[:count] + both[count:]
        out_ref[...] = (e * lax.rsqrt(jnp.sum(e * e, -1, keepdims=True) + epsilon)).astype(bf16)


def image_unit(x, g1, s1, wqkv, wout, g2, s2, wup, wdown, heads=12, images=8):
    count, tokens, width = x.shape
    hidden = wup.shape[1]
    pad = -(-tokens // 8) * 8
    rows = images * pad
    full = lambda a: pl.BlockSpec(a.shape, lambda i: (0,) * a.ndim, pipeline_mode=pl.Buffered(1))
    hbm = pl.BlockSpec(memory_space=pl.ANY)
    args = (jnp.transpose(x, (1, 0, 2)), g1, s1, wqkv, wout, g2, s2, wup, wdown)
    return pl.pallas_call(
        functools.partial(image_kernel, heads),
        name="image",
        grid=(count // images,),
        out_shape=jax.ShapeDtypeStruct((count, width), bf16),
        in_specs=[pl.BlockSpec((tokens, images, width), lambda i: (0, i, 0))]
        + [full(a) if a.ndim == 1 else hbm for a in args[1:]],
        out_specs=pl.BlockSpec((count, width), lambda i: (0, 0)),
        scratch_shapes=[
            pltpu.VMEM((width // 128 * tokens * images, 128), f32),
            pltpu.VMEM((rows, width), f32),
            pltpu.VMEM((rows, width), bf16),
            pltpu.VMEM((rows + 16, 3 * width), bf16),
            pltpu.VMEM((rows, width), bf16),
            pltpu.VMEM((rows, width), f32),
            pltpu.VMEM((count, hidden), f32),
            pltpu.VMEM((count, width), f32),
        ]
        + [pltpu.VMEM(w.shape, bf16) for w in (wqkv, wout, wup, wdown)]
        + [pltpu.SemaphoreType.DMA((4,))],
        compiler_params=pltpu.CompilerParams(vmem_limit_bytes=67043328),
    )(*args)

def dot_0(a, b):
    return lax.dot_general(a, b, (((0,), (0,)), ((), ())), preferred_element_type=f32)


def norm_back(grad_normed, scaled, inverse, gain):
    g = grad_normed * gain
    centre = jnp.mean(g, -1, keepdims=True)
    along = jnp.mean(g * scaled, -1, keepdims=True)
    return inverse * (g - centre - scaled * along)


def token_columns(mask_ref, length_ref, seq):
    captions = mask_ref.shape[1]
    rows = captions * seq
    row = lax.broadcasted_iota(jnp.int32, (rows, captions), 0)
    lane = lax.broadcasted_iota(jnp.int32, (rows, captions), 1)
    length = length_ref[...].astype(f32)
    own = row // seq == lane
    length_t = jnp.sum(jnp.where(own, length, 0.0), -1, keepdims=True)
    spread = dot_t(jnp.where(own, 1.0, 0.0).astype(bf16), mask_ref[...].astype(f32).astype(bf16))
    row = lax.broadcasted_iota(jnp.int32, (rows, seq), 0)
    lane = lax.broadcasted_iota(jnp.int32, (rows, seq), 1)
    mask_t = jnp.sum(jnp.where(row % seq == lane, spread, 0.0), -1, keepdims=True)
    place = (lax.broadcasted_iota(jnp.int32, (rows, 1), 0) % seq).astype(f32)
    weight = jnp.where(place < length_t, mask_t, 0.0)
    count = jnp.sum(weight.reshape(captions, seq, 1), 1)
    return length_t, weight, jnp.maximum(count, 1.0)


def text_attention(heads, seq, group, width, qkv, probs, at, cols):
    hd = width // heads
    r_id = lax.broadcasted_iota(jnp.int32, (group, group), 0)
    c_id = lax.broadcasted_iota(jnp.int32, (group, group), 1)
    same = r_id // seq == c_id // seq
    place = (c_id % seq).astype(f32)
    factor = hd ** (-0.5) * log2e

    def attend(g, carry):
        rs = pl.ds(pl.multiple_of(g * group, 16), group)
        keep = same & (place < cols[rs, 1:2])

        def scores(hp):
            k2 = two_heads(qkv[rs, width + hp * 2 * hd : width + (hp + 1) * 2 * hd])
            return dot_t(qkv[rs, hp * 2 * hd : (hp + 1) * 2 * hd], k2)

        def values(hp, ps):
            v2 = two_heads(qkv[rs, 2 * width + hp * 2 * hd : 2 * width + (hp + 1) * 2 * hd])
            at[rs, hp * 2 * hd : (hp + 1) * 2 * hd] = dot(ps, v2).astype(bf16)

        after, before = scores(0), None
        for hp in range(heads // 2):
            s2 = after
            if hp + 1 < heads // 2:
                after = scores(hp + 1)
            ps = []
            for h in range(2):
                s = jnp.where(keep, s2[:, h * group : (h + 1) * group] * factor, -1e30)
                e = jnp.exp2(s - jnp.max(s, -1, keepdims=True))
                p = e * (1.0 / jnp.sum(e, -1, keepdims=True))
                probs[rs, pl.ds((hp * 2 + h) * group, group)] = p
                ps.append(p.astype(bf16))
            if before is not None:
                values(hp - 1, before)
            before = jnp.concatenate(ps, 1)
        values(heads // 2 - 1, before)
        return carry

    return attend


inv_root_2pi = 0.3989422804014327


def split_dot(a, w):
    hi = a.astype(bf16)
    lo = (a - hi.astype(f32)).astype(bf16)
    both = dot(jnp.concatenate([hi, lo], 0), w[...])
    return both[: a.shape[0]] + both[a.shape[0] :]


def text_attention_back(heads, group, width, qkv, probs, at):
    hd = width // heads
    scale = hd ** (-0.5)

    def attend(g, carry):
        rs = pl.ds(pl.multiple_of(g * group, 16), group)
        for hp in range(heads // 2):
            lanes = slice(hp * 2 * hd, (hp + 1) * 2 * hd)
            klanes = slice(width + lanes.start, width + lanes.stop)
            vlanes = slice(2 * width + lanes.start, 2 * width + lanes.stop)
            ga = at[rs, lanes]
            q2, k2, v2 = two_heads(qkv[rs, lanes]), two_heads(qkv[rs, klanes]), two_heads(qkv[rs, vlanes])
            dp2 = dot_t(ga, v2)
            ps, ds = [], []
            for h in range(2):
                p = probs[rs, pl.ds((hp * 2 + h) * group, group)]
                dp = dp2[:, h * group : (h + 1) * group]
                ds.append((p * (dp - jnp.sum(dp * p, -1, keepdims=True))).astype(bf16))
                ps.append(p.astype(bf16))
            dv = dot_0(jnp.concatenate(ps, 0), two_heads(ga))
            dq = dot(jnp.concatenate(ds, 1), k2)
            dk = dot_0(jnp.concatenate(ds, 0), q2)
            qkv[rs, lanes] = (dq * scale).astype(bf16)
            qkv[rs, klanes] = (dk * scale).astype(bf16)
            qkv[rs, vlanes] = dv.astype(bf16)
        return carry

    return attend


MESH = pl.DeviceIdType.MESH


COLORS = 3


def color_plans(cb):
    rest = [("c", b) for b in range(1, cb)]
    return [[("r", 1), ("c", 0)] + rest, [("c", 0), ("r", 1)] + rest, rest + [("c", 0), ("r", 1)]]


def log2(n):
    return n.bit_length() - 1


def text_step(
    shape, heads,
    unit_ref, mask_ref, length_ref, g1, s1, g2, s2, x_hbm, wqkv_hbm, wout_hbm, wup_hbm, wdown_hbm,
    gx_hbm, parts_hbm, vecs_ref, images_hbm,
    x_ref, wqkv, wout, wup, wdown, n1, qkv, probs, at, mixed, n2, slope, act, cols,
    images, rowsum, rowsum_c, rowsum_cs, rowsum_r, pooled_act, act_all, gpc_own, gpc_all,
    g_up, g_out, g_qkv, r_up, r_out, r_qkv, d_part, d_recv, d_recv2, final, extra, vec, vec_c, vec_cs, vec_r,
    load_sem, out_sem, ag_send, ag_recv, ps_send, ps_recv, a_send, a_recv, gp_send, gp_recv,
    c_send, c_recv, rs_send, rs_recv, d_send, d_recv_sem, f_send, f_recv, v_send, v_recv,
):
    R, C, captions, seq, group = shape
    rb, cb = log2(R), log2(C)
    r, c = lax.axis_index("row"), lax.axis_index("col")
    rbit = [lax.rem(lax.div(r, 1 << b), 2) for b in range(rb)]
    cbit = [lax.rem(lax.div(c, 1 << b), 2) for b in range(cb)]
    core, xh = rbit[0], rbit[1]
    rows, width = x_ref.shape
    hidden = wup.shape[1]
    half = width // 2
    sub = hidden // (4 * C)

    def flip_r(b):
        return (r + (1 - 2 * rbit[b]) * (1 << b), c)

    def flip_c(b):
        return (r, c + (1 - 2 * cbit[b]) * (1 << b))

    row_peers = [(lax.rem(r + d, R), c) for d in range(1, R)]
    col_peers = [(r, lax.rem(c + d, C)) for d in range(1, C)]

    def remote(src, dst, send, recv, to):
        return pltpu.make_async_remote_copy(
            src_ref=src, dst_ref=dst, send_sem=send, recv_sem=recv, device_id=to, device_id_type=MESH
        )

    sent = []

    def go(copy):
        copy.start()
        sent.append(copy)
        return copy

    barrier = pltpu.get_barrier_semaphore()
    for to in row_peers + col_peers:
        pl.semaphore_signal(barrier, inc=1, device_id=to, device_id_type=MESH)

    loads = []
    for k, (src, dst) in enumerate(
        ((x_hbm, x_ref), (wqkv_hbm, wqkv), (wout_hbm, wout), (wup_hbm, wup), (wdown_hbm, wdown))
    ):
        copy = pltpu.make_async_copy(src, dst, load_sem.at[k])
        if k < 2:
            copy.start()
        loads.append(copy)

    length_t, weight, count = token_columns(mask_ref, length_ref, seq)
    cols[:, 0:1] = weight
    cols[:, 1:2] = length_t
    loads[0].wait()
    pl.semaphore_wait(barrier, R + C - 2)

    mine = tuple(rbit[b] for b in reversed(range(rb))) + tuple(cbit[b] for b in reversed(range(cb)))
    part = captions // 2
    pairs = captions * R * C
    staged = len(images.shape) < 3 + rb + cb
    gather = images_hbm if staged else images
    for k in range(2):
        if staged:
            copy = pltpu.make_async_copy(unit_ref.at[pl.ds(k * part, part), :], gather.at[(k,) + mine], load_sem.at[5 + k])
            copy.start()
            loads.append(copy)
        else:
            images[(k,) + mine] = unit_ref[k * part : (k + 1) * part, :]
    if staged:
        loads[5].wait()
        loads[6].wait()

    def stage(i):
        if not staged:
            return images[...].reshape(pairs, width)
        lead = 3 + rb + cb - len(images.shape)
        where = tuple((i >> b) & 1 for b in reversed(range(lead)))
        copy = pltpu.make_async_copy(gather.at[where], images, load_sem.at[5])
        copy.start()
        copy.wait()
        return images[...].reshape(pairs >> lead, width)

    stages = pairs // math.prod(images.shape[:-1])
    order = [("c", b) for b in reversed(range(1, cb))]
    tail = [("r", b) for b in reversed(range(1, rb))]
    plans = (order + [("c", 0)] + tail + [("r", 0)], order + tail + [("c", 0)] + [("r", 0)])
    gathered = [set(), set()]
    pending = [None, None]
    phase = [0, 0]

    def gather_step():
        for k in range(2):
            if pending[k] is not None:
                pending[k].wait_recv()
                gathered[k].add(plans[k][phase[k] - 1])
                pending[k] = None
            if phase[k] < len(plans[k]):
                kind, b = plans[k][phase[k]]
                names = [("r", i) for i in reversed(range(rb))] + [("c", i) for i in reversed(range(cb))]
                where = tuple(slice(None) if nm in gathered[k] else v for nm, v in zip(names, mine))
                dst = gather.at[(k,) + where]
                src = unit_ref.at[pl.ds(k * part, part), :] if phase[k] == 0 else dst
                to = flip_r(b) if kind == "r" else flip_c(b)
                pending[k] = go(remote(src, dst, ag_send.at[k, phase[k]], ag_recv.at[k, phase[k]], to))
                phase[k] += 1

    gather_step()
    x = x_ref[...].astype(f32)
    scaled, _ = stats(x)
    n1[...] = (scaled * g1[...][None] + s1[...][None]).astype(bf16)
    loads[1].wait()
    for copy in loads[2:5]:
        copy.start()
    for q in range(3):
        cut = slice(q * width, (q + 1) * width)
        qkv[:, cut] = dot(n1[...], wqkv[:, cut]).astype(bf16)
    gather_step()
    attend = text_attention(heads, seq, group, width, qkv, probs, at, cols)
    groups = rows // group
    lax.fori_loop(0, groups, attend, 0)
    gather_step()
    loads[2].wait()
    mixed[...] = x_ref[...].astype(f32) + dot(at[...], wout[...])
    scaled, _ = stats(mixed[...])
    n2[...] = (scaled * g2[...][None] + s2[...][None]).astype(bf16)
    weight = cols[:, 0:1]
    loads[3].wait()
    gather_step()

    def up_block(f, carry):
        cut = pl.ds(pl.multiple_of(f * width, 128), width)
        h = dot(n2[...], wup[:, cut])
        phi = 0.5 + 0.5 * lax.erf(h * inv_root2)
        slope[:, cut] = (phi + h * (jnp.exp(-0.5 * h * h) * inv_root_2pi)).astype(bf16)
        act[:, cut] = jnp.sum((h * phi * cols[:, 0:1]).reshape(captions, seq, width), 1)
        return carry

    lax.fori_loop(0, hidden // width, up_block, 0)
    gather_step()
    loads[4].wait()
    pooled = jnp.sum((mixed[...] * weight).reshape(captions, seq, width), 1) + split_dot(act[...], wdown)
    pooled = pooled / count
    inverse = lax.rsqrt(jnp.sum(pooled * pooled, -1, keepdims=True) + epsilon)
    text_unit = (pooled * inverse).astype(bf16)
    span = hidden // C
    for k in range(C):
        pooled_act[k] = act[:, k * span : (k + 1) * span].astype(bf16)
    while pending[0] is not None or pending[1] is not None:
        gather_step()

    t = 2.0 * math.sqrt(width)
    sims = []
    for i in range(stages):
        every = stage(i)
        sims.append(dot_t(text_unit, every))
    e = jnp.exp2(jnp.concatenate(sims, 1) * (t * log2e))
    rowsum[...] = jnp.sum(e, 0, keepdims=True)
    first = [
        go(remote(rowsum, rowsum_c.at[d], ps_send.at[d], ps_recv.at[d], to)) for d, to in enumerate(col_peers)
    ]
    col_scale = 1.0 / jnp.sum(e, -1, keepdims=True)
    acts = []
    for d, to in enumerate(col_peers):
        acts.append(
            go(remote(pooled_act.at[lax.rem(c + d + 1, C)], act_all.at[d], a_send.at[d], a_recv.at[d], to))
        )
    act_all[C - 1] = pooled_act[c]
    total = rowsum[...]
    for d, copy in enumerate(first):
        copy.wait_recv()
        total += rowsum_c[d]
    rowsum_cs[...] = total
    second = [
        go(remote(rowsum_cs, rowsum_r.at[d], ps_send.at[C - 1 + d], ps_recv.at[C - 1 + d], to))
        for d, to in enumerate(row_peers)
    ]
    for d, copy in enumerate(second):
        copy.wait_recv()
        total += rowsum_r[d]
    grad_sim = (e * (1.0 / total + col_scale) * (0.5 / pairs)).astype(bf16)
    share = pairs // stages
    hits = sum(
        dot(grad_sim[:, i * share : (i + 1) * share], every if stages == 1 else stage(i)) for i in range(stages)
    )
    grad_unit = t * hits - (t / pairs) * unit_ref[...].astype(f32)
    along = jnp.sum(grad_unit * pooled, -1, keepdims=True)
    gpc = (inverse * grad_unit - pooled * (inverse * inverse * inverse * along)) / count
    gpc_r = gpc.astype(bf16)
    gpc_own[...] = gpc_r
    gps = [go(remote(gpc_own, gpc_all.at[d], gp_send.at[d], gp_recv.at[d], to)) for d, to in enumerate(col_peers)]
    gpc_all[C - 1] = gpc_r

    def emit(name, row, block, lead=()):
        scatter = scatters[name]
        sub = scatter.sub
        for i in range(0, block.shape[0], sub):
            index = (row + i) // sub
            to = index // (2 * COLORS)
            bits = lead + tuple((to >> b) & 1 for b in reversed(range(cb - len(lead))))
            color, xbit = index % (2 * COLORS) // 2, index % 2
            for s in range(2):
                scatter.buf[(s, color, xbit) + bits] = block[i : i + sub, s * half : (s + 1) * half].astype(bf16)

    class Scatter:
        def __init__(self, index, buf, recvs, offset):
            self.index, self.buf, self.recvs, self.offset = index, buf, recvs, offset
            self.sub = buf.shape[-2]
            self.plans = color_plans(cb)
            self.phase = [0] * COLORS
            self.copies = [None] * COLORS
            self.kept = [None] * COLORS
            self.pieces = []
            self.finals = None

        def rows(self, k):
            return slice(self.offset + k * self.sub, self.offset + (k + 1) * self.sub)

        def start(self, piece):
            self.copy(piece).start()
            if isinstance(piece, int):
                self.started(piece)

        def started(self, piece):
            self.pieces.append(self.copy(piece))
            sent.append(self.pieces[-1])

        def copy(self, piece):
            bits = (piece // 2, piece % 2) if isinstance(piece, int) else (lax.div(piece, 2), lax.rem(piece, 2))
            return remote(
                self.buf.at[(1 - core, slice(None), slice(None)) + bits], self.recvs[0].at[(slice(None), slice(None)) + bits],
                c_send.at[self.index, piece], c_recv.at[self.index, piece], flip_r(0),
            )

        def step(self, colors=range(3)):
            for copy in self.pieces:
                copy.wait_recv()
            self.pieces = []
            for k in colors:
                self.advance(k)

        def done(self):
            return min(self.phase) > len(self.plans[0])

        def advance(self, k):
            p = self.phase[k]
            plan = self.plans[k]
            self.phase[k] += 1
            if p == 0:
                before, here = self.buf.at[core, k], self.recvs[0].at[k]
            else:
                self.copies[k].wait_recv()
                before = self.recvs[0].at[(k,) + self.kept[k]] if p == 1 else self.recvs[p - 1][k].at[self.kept[k]]
                here = self.recvs[p][k]
            if p == len(plan):
                rows = self.rows(k)
                final[core, xh, rows, :] = before[...] + here[...]
                if self.finals:
                    self.finals[k].start()
                return
            kind, b = plan[p]
            left = [("r", 1)] + [("c", i) for i in reversed(range(cb))]
            for gone in plan[:p]:
                left.remove(gone)
            axis = left.index((kind, b))
            bit = xh if kind == "r" else cbit[b]
            give = (slice(None),) * axis + (1 - bit,)
            keep = (slice(None),) * axis + (bit,)
            here[give] = before[give] + here[give]
            to = flip_r(1) if kind == "r" else flip_c(b)
            self.copies[k] = go(
                remote(
                    here.at[give], self.recvs[p + 1][k],
                    rs_send.at[self.index, k, p], rs_recv.at[self.index, k, p], to,
                )
            )
            here[keep] = before[keep] + here[keep]
            self.kept[k] = keep

    up_rows = COLORS * g_up.shape[-2]
    out_rows = COLORS * g_out.shape[-2]
    down_rows = 2 * sub
    up = Scatter(0, g_up, r_up, 0)
    out = Scatter(1, g_out, r_out, up_rows + down_rows)
    rest = Scatter(2, g_qkv, r_qkv, up_rows + down_rows + out_rows)
    scatters = {"up": up, "out": out, "qkv": rest}
    early = slice(0, up_rows + down_rows + out_rows)

    class Finals:
        def __init__(self, index, rows):
            self.index, self.rows = index, rows

        def start(self):
            for b in range(2, rb):
                there = extra.at[b - 2, self.rows]
                swap = remote(final.at[core, xh, self.rows], there, f_send.at[self.index, b], f_recv.at[self.index, b], flip_r(b))
                swap.start()
                swap.wait()
                final[core, xh, self.rows, :] = final[core, xh, self.rows, :] + there[...]
            here = final.at[core, xh, self.rows]
            self.copy = go(remote(here, here, f_send.at[self.index, 0], f_recv.at[self.index, 0], flip_r(1)))

        def step(self):
            self.copy.wait_recv()
            here = final.at[core, :, self.rows]
            self.copy = go(remote(here, here, f_send.at[self.index, 1], f_recv.at[self.index, 1], flip_r(0)))

        def end(self):
            self.copy.wait_recv()

    first_finals, rest.finals = Finals(0, early), [Finals(1 + k, rest.rows(k)) for k in range(COLORS)]

    def up_back(f, carry):
        cut = pl.ds(pl.multiple_of(f * width, 128), width)
        hh = dot_t(gpc_own[...], wdown[cut, :])
        spread = jnp.broadcast_to(hh[:, None, :], (captions, seq, width)).reshape(rows, width)
        slope[:, cut] = (spread * cols[:, 0:1] * slope[:, cut].astype(f32)).astype(bf16)
        emit("up", 0, dot_0(slope[:, cut], n2[...]), (lax.div(f, 2), lax.rem(f, 2)))
        up.start(f)
        return carry

    lax.fori_loop(0, 4, up_back, 0)
    for piece in range(4):
        up.started(piece)
    gn2 = dot_t(slope[...], wup[...])
    up.step()
    scaled, inv2 = stats(mixed[...])
    vec[2:3, :] = jnp.sum(gn2 * scaled, 0, keepdims=True)
    vec[3:4, :] = jnp.sum(gn2, 0, keepdims=True)
    spread = jnp.broadcast_to(gpc[:, None, :], (captions, seq, width)).reshape(rows, width) * weight
    mixed[...] = spread + norm_back(gn2, scaled, inv2, g2[...][None])
    n2[...] = mixed[...].astype(bf16)
    emit("out", 0, dot_0(n2[...], at[...]))
    for piece in range(4):
        out.start(piece)
    at[...] = dot_t(n2[...], wout[...]).astype(bf16)
    attend_back = text_attention_back(heads, group, width, qkv, probs, at)
    lax.fori_loop(0, groups // 2, attend_back, 0)
    up.step()
    out.step()

    for copy in acts + gps:
        copy.wait_recv()
    down = dot_0(act_all[...].reshape(C * captions, span), gpc_all[...].reshape(C * captions, width))
    for j in range(4):
        for s in range(2):
            d_part[s, j // 2, j % 2] = down[j * sub : (j + 1) * sub, s * half : (s + 1) * half].astype(bf16)
    d0 = go(remote(d_part.at[1 - core], d_recv, d_send.at[0], d_recv_sem.at[0], flip_r(0)))

    lax.fori_loop(groups // 2, groups, attend_back, 0)
    up.step(range(2))
    pieces = 0
    for q in range(3):
        emit("qkv", q * width, dot_0(qkv[:, q * width : (q + 1) * width], n1[...]))
        while pieces < 4 * (q + 1) // 3:
            rest.start(pieces)
            pieces += 1
    up.step(range(2, 3))
    out.step()
    d0.wait_recv()
    d_recv[:, 1 - xh] = d_part[core, :, 1 - xh] + d_recv[:, 1 - xh]
    d1 = go(remote(d_recv.at[:, 1 - xh], d_recv2, d_send.at[1], d_recv_sem.at[1], flip_r(1)))
    d_recv[:, xh] = d_part[core, :, xh] + d_recv[:, xh]
    rest.step()
    gn1 = dot_t(qkv[...], wqkv[...])
    up.step()
    scaled, inv1 = stats(x_ref[...].astype(f32))
    vec[0:1, :] = jnp.sum(gn1 * scaled, 0, keepdims=True)
    vec[1:2, :] = jnp.sum(gn1, 0, keepdims=True)
    vfirst = [go(remote(vec, vec_c.at[d], v_send.at[d], v_recv.at[d], to)) for d, to in enumerate(col_peers)]
    out.step()
    mixed[...] = mixed[...] + norm_back(gn1, scaled, inv1, g1[...][None])
    gx_out = pltpu.make_async_copy(mixed, gx_hbm, out_sem.at[0])
    gx_out.start()
    d1.wait_recv()
    for k in range(2):
        final[core, xh, up_rows + k * sub : up_rows + (k + 1) * sub, :] = d_recv[k, xh] + d_recv2[k]
    rest.step()
    while not up.done():
        up.step()
        if not out.done():
            out.step()
    while not out.done():
        out.step()
    first_finals.start()
    vtotal = vec[...]
    for d, copy in enumerate(vfirst):
        copy.wait_recv()
        vtotal += vec_c[d]
    vec_cs[...] = vtotal
    vsecond = [
        go(remote(vec_cs, vec_r.at[d], v_send.at[C - 1 + d], v_recv.at[C - 1 + d], to)) for d, to in enumerate(row_peers)
    ]
    rest.step()
    first_finals.step()
    while not rest.done():
        rest.step()
    for last in rest.finals:
        last.step()
    for d, copy in enumerate(vsecond):
        copy.wait_recv()
        vtotal += vec_r[d]
    vecs_ref[...] = vtotal
    first_finals.end()
    for last in rest.finals:
        last.end()
    parts_out = pltpu.make_async_copy(final, parts_hbm, out_sem.at[1])
    parts_out.start()
    for copy in sent:
        copy.wait_send()
    gx_out.wait()
    parts_out.wait()


def text_call(R, C, unit, tokens, mask, length, g1, s1, wqkv, wout, g2, s2, wup, wdown, heads=12, group=128):
    captions, seq, width = tokens.shape
    rows, hidden = captions * seq, wup.shape[1]
    rb, cb = log2(R), log2(C)
    half, sub, span = width // 2, hidden // (4 * C), hidden // C
    V, S, D = pltpu.VMEM, jax.ShapeDtypeStruct, pltpu.SemaphoreType.DMA
    pairs = captions * R * C
    bits_c = (2,) * cb

    dims, tail = 1 + rb + cb, (captions // 2, width)
    lead = max(log2(pairs // 1024), 0)
    held_dims, staged_dims = dims - lead, dims if lead else 0

    subs = [hidden // (2 * COLORS * C), width // (2 * COLORS * C), 3 * width // (2 * COLORS * C)]

    def recvs(rows):
        phases = len(color_plans(cb)[0]) + 1
        return [V((COLORS, 2) + bits_c + (rows, half), bf16)] + [
            [V((2,) * (1 + cb - p) + (rows, half), bf16) for _ in range(COLORS)] for p in range(1, phases)
        ]

    total = COLORS * sum(subs) + 2 * sub
    vm = pl.BlockSpec(memory_space=pltpu.VMEM)
    hbm = pl.BlockSpec(memory_space=pl.ANY)
    out = pl.pallas_call(
        functools.partial(text_step, (R, C, captions, seq, group), heads),
        name="text",
        in_specs=[vm] * 7 + [hbm] * 5,
        out_specs=(hbm, hbm, vm, hbm),
        out_shape=(S((rows, width), f32), S((2, 2, total, half), bf16), S((4, width), f32), S((2,) * staged_dims + tail, bf16)),
        scratch_shapes=[
            V((rows, width), bf16), V(wqkv.shape, bf16), V(wout.shape, bf16), V(wup.shape, bf16), V(wdown.shape, bf16),
            V((rows, width), bf16), V((rows, 3 * width), bf16), V((rows, heads * group), f32), V((rows, width), bf16),
            V((rows, width), f32), V((rows, width), bf16), V((rows, hidden), bf16), V((captions, hidden), f32), V((rows, 128), f32),
            V((2,) * held_dims + tail, bf16),
            V((1, pairs), f32), V((C - 1, 1, pairs), f32), V((1, pairs), f32), V((R - 1, 1, pairs), f32),
            V((C, captions, span), bf16), V((C, captions, span), bf16), V((captions, width), bf16), V((C, captions, width), bf16),
            *[V((2, COLORS, 2) + bits_c + (n, half), bf16) for n in subs], *[recvs(n) for n in subs],
            V((2, 2, 2, sub, half), bf16), V((2, 2, sub, half), bf16), V((2, sub, half), bf16),
            V((2, 2, total, half), bf16), V((max(rb - 2, 1), total, half), bf16),
            V((4, width), f32), V((C - 1, 4, width), f32), V((4, width), f32), V((R - 1, 4, width), f32),
            D((7,)), D((2,)), D((2, rb + cb)), D((2, rb + cb)), D((R + C - 2,)), D((R + C - 2,)),
            D((C - 1,)), D((C - 1,)), D((C - 1,)), D((C - 1,)),
            D((3, 4)), D((3, 4)), D((3, COLORS, cb + 1)), D((3, COLORS, cb + 1)), D((2,)), D((2,)), D((1 + COLORS, max(rb, 2))), D((1 + COLORS, max(rb, 2))), D((R + C - 2,)), D((R + C - 2,)),
        ],
        compiler_params=pltpu.CompilerParams(collective_id=0, has_side_effects=True, vmem_limit_bytes=67043328),
    )(unit, mask.T, length[None], g1, s1, g2, s2, tokens.reshape(rows, width), wqkv, wout, wup, wdown)
    return out[:3]


def finish_kernel(
    col_size, parts, vecs, shift, gx_in, gx_out, up_out, out_out, qkv_out, down_out, v0, v1, v2, v3,
    gx, up, out, qkv, down, sems
):
    load = pltpu.make_async_copy(gx_in, gx, sems.at[0])
    load.start()
    stores = []

    def store(src, dst):
        copy = pltpu.make_async_copy(src, dst, sems.at[1 + len(stores)])
        copy.start()
        stores.append(copy)

    def blocks(lo, colors, sub):
        for j in range(2 * colors):
            rows = slice(lo + j // 2 * sub, lo + (j // 2 + 1) * sub)
            yield j * sub, jnp.concatenate([parts[0, j % 2, rows, :], parts[1, j % 2, rows, :]], -1).astype(f32)

    def fill(ref, lo, colors):
        sub = ref.shape[0] // (2 * colors)
        for at_row, block in blocks(lo, colors, sub):
            ref[at_row : at_row + sub, :] = block

    hidden_share = down.shape[0]
    fill(down, hidden_share // 2, 2)
    store(down, down_out)
    fill(qkv, hidden_share + out.shape[0] // 2, COLORS)
    store(qkv, qkv_out)
    fill(out, hidden_share, COLORS)
    store(out, out_out)
    load.wait()
    store(gx, gx_out)
    up[...] = jnp.concatenate([block for _, block in blocks(0, COLORS, hidden_share // (2 * COLORS))], 0).T
    store(up, up_out)
    width = vecs.shape[1]
    share = width // col_size
    lane = lax.broadcasted_iota(jnp.int32, (width, share), 1)
    row = lax.broadcasted_iota(jnp.int32, (width, share), 0)
    pick = jnp.where(row == lane + shift[0], 1.0, 0.0)
    own = jnp.dot(vecs[...], pick, precision=lax.Precision.HIGHEST, preferred_element_type=f32)
    for k, v in enumerate((v0, v1, v2, v3)):
        v[...] = own[k : k + 1, :]
    for copy in stores:
        copy.wait()


def finish_call(C, hidden, gx, parts, vecs):
    width = 2 * parts.shape[-1]
    share, hidden_share = width // C, hidden // C
    S, V = jax.ShapeDtypeStruct, pltpu.VMEM
    shift = (lax.axis_index("col") * share).astype(jnp.int32)[None]
    vm = pl.BlockSpec(memory_space=pltpu.VMEM)
    hbm = pl.BlockSpec(memory_space=pl.ANY)
    shapes = [gx.shape, (width, hidden_share), (share, width), (3 * share, width), (hidden_share, width)]
    return pl.pallas_call(
        functools.partial(finish_kernel, C),
        name="finish",
        in_specs=[vm, vm, pl.BlockSpec(memory_space=pltpu.SMEM), hbm],
        out_specs=(hbm,) * 5 + (vm,) * 4,
        out_shape=tuple(S(s, f32) for s in shapes) + (S((1, share), f32),) * 4,
        scratch_shapes=[V(s, f32) for s in shapes] + [pltpu.SemaphoreType.DMA((6,))],
    )(parts, vecs, shift, gx)


def on_device(
    image_tokens, caption_tokens, caption_mask, caption_length,
    image_gain1, image_shift1, image_qkv, image_out, image_gain2, image_shift2, image_up, image_down,
    text_gain1, text_shift1, text_qkv, text_out, text_gain2, text_shift2, text_up, text_down,
):
    R, C = lax.axis_size("row"), lax.axis_size("col")
    unit = image_unit(
        image_tokens, image_gain1, image_shift1, image_qkv, image_out,
        image_gain2, image_shift2, image_up, image_down,
    )
    grad_tokens, parts, vecs = text_call(
        R, C, unit, caption_tokens, caption_mask, caption_length, text_gain1, text_shift1, text_qkv, text_out,
        text_gain2, text_shift2, text_up, text_down,
    )
    grad_tokens, up, out, qkv, down, gain1, shift1, gain2, shift2 = finish_call(C, text_up.shape[1], grad_tokens, parts, vecs)
    return (
        grad_tokens.reshape(caption_tokens.shape), gain1[0], shift1[0], qkv.T, out.T, gain2[0], shift2[0], up, down,
    )


def solution(mesh):
    pair = P(("row", "col"))
    return jax.shard_map(
        on_device,
        mesh=mesh,
        in_specs=(pair,) * 4 + (P(),) * 16,
        out_specs=(pair, P("col"), P("col"), P(None, "col"), P(None, "col"), P("col"), P("col"), P(None, "col"), P("col")),
        check_vma=False,
    )
```

```python
import math, functools
import jax, jax.numpy as jnp
from jax import lax
from jax.experimental import pallas as pl
from jax.experimental.pallas import tpu as pltpu
from jax.sharding import PartitionSpec as P

epsilon = 1e-06
log2e = 1.4426950408889634
inv_root2 = 0.7071067811865476
f32 = jnp.float32
bf16 = jnp.bfloat16


def dot(a, b):
    return jnp.dot(a, b, preferred_element_type=f32)


def dot_t(a, b):
    return lax.dot_general(a, b, (((1,), (1,)), ((), ())), preferred_element_type=f32)


def stats(x):
    centred = x - jnp.mean(x, -1, keepdims=True)
    inverse = lax.rsqrt(jnp.mean(centred * centred, -1, keepdims=True) + epsilon)
    return centred * inverse, inverse


def two_heads(v):
    first = lax.broadcasted_iota(jnp.int32, v.shape, 1) < v.shape[1] // 2
    zero = jnp.zeros_like(v)
    return jnp.concatenate([jnp.where(first, v, zero), jnp.where(first, zero, v)], 0)


def gelu(v):
    u = 0.5 * v
    return u * lax.erf(v * inv_root2) + u


def image_kernel(
    heads, x_ref, g1, s1, wqkv_hbm, wout_hbm, g2, s2, wup_hbm, wdown_hbm, out_ref,
    tok, xs, n, qkv, at, mixed, act, pooled, wqkv, wout, wup, wdown, sems
):
    tokens, images, width = x_ref.shape
    pad = -(-tokens // 8) * 8
    rows = images * pad
    i = pl.program_id(0)
    weights = ((wqkv_hbm, wqkv), (wout_hbm, wout), (wup_hbm, wup), (wdown_hbm, wdown))

    def fetched(k):
        @pl.when(i == 0)
        def _():
            pltpu.make_async_copy(*weights[k], sems.at[k]).wait()
            for later in range(1, 4 if k == 0 else 0):
                pltpu.make_async_copy(*weights[later], sems.at[later]).start()

    @pl.when(i == 0)
    def _():
        pltpu.make_async_copy(*weights[0], sems.at[0]).start()
        xs[...] = jnp.zeros_like(xs)
        qkv[rows:, :] = jnp.zeros((qkv.shape[0] - rows, 3 * width), bf16)

    count = tokens * images
    for j in range(width // 128):
        lanes = slice(j * 128, (j + 1) * 128)
        tok[j * count : (j + 1) * count, :] = x_ref[:, :, lanes].astype(f32).reshape(count, 128)
    for j in range(width // 128):
        for k in range(images):
            xs[k * pad : k * pad + tokens, j * 128 : (j + 1) * 128] = tok[pl.ds(j * count + k, tokens, stride=images), :]
    scaled, _ = stats(xs[...])
    n[...] = (scaled * g1[...][None] + s1[...][None]).astype(bf16)
    fetched(0)
    for c in range(3):
        cols = slice(c * width, (c + 1) * width)
        qkv[:rows, cols] = dot(n[...], wqkv[:, cols]).astype(bf16)

    group = 2 * pad
    hd = width // heads
    r_id = lax.broadcasted_iota(jnp.int32, (group, 2 * hd), 0)
    c_id = lax.broadcasted_iota(jnp.int32, (group, 2 * hd), 1)
    same = (r_id < pad) == (c_id < pad)
    inside = jnp.where(c_id < pad, c_id, c_id - pad) < tokens
    keep = same & inside
    ones = two_heads(jnp.ones((2 * hd, 2 * hd), bf16))
    factor = hd ** (-0.5) * log2e

    def attend(g, carry):
        rs = pl.ds(pl.multiple_of(g * group, 16), group)
        ks = pl.ds(pl.multiple_of(g * group, 16), 2 * hd)
        def scores(hp):
            k2 = two_heads(qkv[ks, width + hp * 2 * hd : width + (hp + 1) * 2 * hd])
            return dot_t(qkv[rs, hp * 2 * hd : (hp + 1) * 2 * hd], k2)

        def values(hp, es):
            v2 = two_heads(qkv[ks, 2 * width + hp * 2 * hd : 2 * width + (hp + 1) * 2 * hd])
            out = dot(es, jnp.concatenate([v2, ones], 1))
            at[rs, hp * 2 * hd : (hp + 1) * 2 * hd] = (out[:, : 2 * hd] / out[:, 2 * hd :]).astype(bf16)

        after, before = scores(0), None
        for hp in range(heads // 2):
            s2 = after
            if hp + 1 < heads // 2:
                after = scores(hp + 1)
            es = []
            for h in range(2):
                s = jnp.where(keep, s2[:, h * 2 * hd : (h + 1) * 2 * hd] * factor, -1e30)
                es.append(jnp.exp2(s - jnp.max(s, -1, keepdims=True)).astype(bf16))
            if before is not None:
                values(hp - 1, before)
            before = jnp.concatenate(es, 1)
        values(heads // 2 - 1, before)
        return carry

    lax.fori_loop(0, rows // group, attend, 0)
    fetched(1)
    mixed[...] = xs[...] + dot(at[...], wout[...])
    row = lax.broadcasted_iota(jnp.int32, (pad, 1), 0)
    valid = (row < tokens).astype(f32)
    dst = pl.ds(pl.multiple_of(i * images, 8), images)
    m3 = mixed[...].reshape(images, pad, width)
    pooled[dst, :] = jnp.sum(m3 * valid[None], 1)
    scaled, _ = stats(mixed[...])
    normed = ((scaled * g2[...][None] + s2[...][None]).reshape(images, pad, width) * valid[None]).reshape(rows, width)
    n[...] = normed.astype(bf16)
    hidden = wup.shape[1]
    step = 768
    fetched(2)
    for c in range(0, hidden, step):
        a = gelu(dot(n[...], wup[:, c : c + step]))
        act[dst, c : c + step] = jnp.sum(a.reshape(images, pad, step), 1)

    fetched(3)

    @pl.when(i == pl.num_programs(0) - 1)
    def _():
        a = act[...] * (1.0 / tokens)
        hi = a.astype(bf16)
        lo = (a - hi.astype(f32)).astype(bf16)
        count = a.shape[0]
        both = dot(jnp.concatenate([hi, lo], 0), wdown[...])
        e = pooled[...] * (1.0 / tokens) + both[:count] + both[count:]
        out_ref[...] = (e * lax.rsqrt(jnp.sum(e * e, -1, keepdims=True) + epsilon)).astype(bf16)


def image_unit(x, g1, s1, wqkv, wout, g2, s2, wup, wdown, heads=12, images=8):
    count, tokens, width = x.shape
    hidden = wup.shape[1]
    pad = -(-tokens // 8) * 8
    rows = images * pad
    full = lambda a: pl.BlockSpec(a.shape, lambda i: (0,) * a.ndim, pipeline_mode=pl.Buffered(1))
    hbm = pl.BlockSpec(memory_space=pl.ANY)
    args = (jnp.transpose(x, (1, 0, 2)), g1, s1, wqkv, wout, g2, s2, wup, wdown)
    return pl.pallas_call(
        functools.partial(image_kernel, heads),
        name="image",
        grid=(count // images,),
        out_shape=jax.ShapeDtypeStruct((count, width), bf16),
        in_specs=[pl.BlockSpec((tokens, images, width), lambda i: (0, i, 0))]
        + [full(a) if a.ndim == 1 else hbm for a in args[1:]],
        out_specs=pl.BlockSpec((count, width), lambda i: (0, 0)),
        scratch_shapes=[
            pltpu.VMEM((width // 128 * tokens * images, 128), f32),
            pltpu.VMEM((rows, width), f32),
            pltpu.VMEM((rows, width), bf16),
            pltpu.VMEM((rows + 16, 3 * width), bf16),
            pltpu.VMEM((rows, width), bf16),
            pltpu.VMEM((rows, width), f32),
            pltpu.VMEM((count, hidden), f32),
            pltpu.VMEM((count, width), f32),
        ]
        + [pltpu.VMEM(w.shape, bf16) for w in (wqkv, wout, wup, wdown)]
        + [pltpu.SemaphoreType.DMA((4,))],
        compiler_params=pltpu.CompilerParams(vmem_limit_bytes=67043328),
    )(*args)

def dot_0(a, b):
    return lax.dot_general(a, b, (((0,), (0,)), ((), ())), preferred_element_type=f32)


def norm_back(grad_normed, scaled, inverse, gain):
    g = grad_normed * gain
    centre = jnp.mean(g, -1, keepdims=True)
    along = jnp.mean(g * scaled, -1, keepdims=True)
    return inverse * (g - centre - scaled * along)


def token_columns(mask_ref, length_ref, seq):
    captions = mask_ref.shape[1]
    rows = captions * seq
    row = lax.broadcasted_iota(jnp.int32, (rows, captions), 0)
    lane = lax.broadcasted_iota(jnp.int32, (rows, captions), 1)
    length = length_ref[...].astype(f32)
    own = row // seq == lane
    length_t = jnp.sum(jnp.where(own, length, 0.0), -1, keepdims=True)
    spread = dot_t(jnp.where(own, 1.0, 0.0).astype(bf16), mask_ref[...].astype(f32).astype(bf16))
    row = lax.broadcasted_iota(jnp.int32, (rows, seq), 0)
    lane = lax.broadcasted_iota(jnp.int32, (rows, seq), 1)
    mask_t = jnp.sum(jnp.where(row % seq == lane, spread, 0.0), -1, keepdims=True)
    place = (lax.broadcasted_iota(jnp.int32, (rows, 1), 0) % seq).astype(f32)
    weight = jnp.where(place < length_t, mask_t, 0.0)
    count = jnp.sum(weight.reshape(captions, seq, 1), 1)
    return length_t, weight, jnp.maximum(count, 1.0)


def text_attention(heads, seq, group, width, qkv, probs, at, cols):
    hd = width // heads
    r_id = lax.broadcasted_iota(jnp.int32, (group, group), 0)
    c_id = lax.broadcasted_iota(jnp.int32, (group, group), 1)
    same = r_id // seq == c_id // seq
    place = (c_id % seq).astype(f32)
    factor = hd ** (-0.5) * log2e

    def attend(g, carry):
        rs = pl.ds(pl.multiple_of(g * group, 16), group)
        keep = same & (place < cols[rs, 1:2])

        def scores(hp):
            k2 = two_heads(qkv[rs, width + hp * 2 * hd : width + (hp + 1) * 2 * hd])
            return dot_t(qkv[rs, hp * 2 * hd : (hp + 1) * 2 * hd], k2)

        def values(hp, ps):
            v2 = two_heads(qkv[rs, 2 * width + hp * 2 * hd : 2 * width + (hp + 1) * 2 * hd])
            at[rs, hp * 2 * hd : (hp + 1) * 2 * hd] = dot(ps, v2).astype(bf16)

        after, before = scores(0), None
        for hp in range(heads // 2):
            s2 = after
            if hp + 1 < heads // 2:
                after = scores(hp + 1)
            ps = []
            for h in range(2):
                s = jnp.where(keep, s2[:, h * group : (h + 1) * group] * factor, -1e30)
                e = jnp.exp2(s - jnp.max(s, -1, keepdims=True))
                p = e * (1.0 / jnp.sum(e, -1, keepdims=True))
                probs[rs, pl.ds((hp * 2 + h) * group, group)] = p
                ps.append(p.astype(bf16))
            if before is not None:
                values(hp - 1, before)
            before = jnp.concatenate(ps, 1)
        values(heads // 2 - 1, before)
        return carry

    return attend


inv_root_2pi = 0.3989422804014327


def split_dot(a, w):
    hi = a.astype(bf16)
    lo = (a - hi.astype(f32)).astype(bf16)
    both = dot(jnp.concatenate([hi, lo], 0), w[...])
    return both[: a.shape[0]] + both[a.shape[0] :]


def text_attention_back(heads, group, width, qkv, probs, at):
    hd = width // heads
    scale = hd ** (-0.5)

    def attend(g, carry):
        rs = pl.ds(pl.multiple_of(g * group, 16), group)
        for hp in range(heads // 2):
            lanes = slice(hp * 2 * hd, (hp + 1) * 2 * hd)
            klanes = slice(width + lanes.start, width + lanes.stop)
            vlanes = slice(2 * width + lanes.start, 2 * width + lanes.stop)
            ga = at[rs, lanes]
            q2, k2, v2 = two_heads(qkv[rs, lanes]), two_heads(qkv[rs, klanes]), two_heads(qkv[rs, vlanes])
            dp2 = dot_t(ga, v2)
            ps, ds = [], []
            for h in range(2):
                p = probs[rs, pl.ds((hp * 2 + h) * group, group)]
                dp = dp2[:, h * group : (h + 1) * group]
                ds.append((p * (dp - jnp.sum(dp * p, -1, keepdims=True))).astype(bf16))
                ps.append(p.astype(bf16))
            dv = dot_0(jnp.concatenate(ps, 0), two_heads(ga))
            dq = dot(jnp.concatenate(ds, 1), k2)
            dk = dot_0(jnp.concatenate(ds, 0), q2)
            qkv[rs, lanes] = (dq * scale).astype(bf16)
            qkv[rs, klanes] = (dk * scale).astype(bf16)
            qkv[rs, vlanes] = dv.astype(bf16)
        return carry

    return attend


MESH = pl.DeviceIdType.MESH


COLORS = 3


def color_plans(cb):
    rest = [("c", b) for b in range(1, cb)]
    return [[("r", 1), ("c", 0)] + rest, [("c", 0), ("r", 1)] + rest, rest + [("c", 0), ("r", 1)]]


def log2(n):
    return n.bit_length() - 1


def text_step(
    shape, heads,
    unit_ref, mask_ref, length_ref, g1, s1, g2, s2, x_hbm, wqkv_hbm, wout_hbm, wup_hbm, wdown_hbm,
    gx_hbm, parts_hbm, vecs_ref, images_hbm,
    x_ref, wqkv, wout, wup, wdown, n1, qkv, probs, at, mixed, n2, slope, act, cols,
    images, rowsum, rowsum_c, rowsum_cs, rowsum_r, pooled_act, act_all, gpc_own, gpc_all,
    g_up, g_out, g_qkv, r_up, r_out, r_qkv, d_part, d_recv, d_recv2, final, extra, vec, vec_c, vec_cs, vec_r,
    load_sem, out_sem, ag_send, ag_recv, ps_send, ps_recv, a_send, a_recv, gp_send, gp_recv,
    c_send, c_recv, rs_send, rs_recv, d_send, d_recv_sem, f_send, f_recv, v_send, v_recv,
):
    R, C, captions, seq, group = shape
    rb, cb = log2(R), log2(C)
    r, c = lax.axis_index("row"), lax.axis_index("col")
    rbit = [lax.rem(lax.div(r, 1 << b), 2) for b in range(rb)]
    cbit = [lax.rem(lax.div(c, 1 << b), 2) for b in range(cb)]
    core, xh = rbit[0], rbit[1]
    rows, width = x_ref.shape
    hidden = wup.shape[1]
    half = width // 2
    sub = hidden // (4 * C)

    def flip_r(b):
        return (r + (1 - 2 * rbit[b]) * (1 << b), c)

    def flip_c(b):
        return (r, c + (1 - 2 * cbit[b]) * (1 << b))

    row_peers = [(lax.rem(r + d, R), c) for d in range(1, R)]
    col_peers = [(r, lax.rem(c + d, C)) for d in range(1, C)]

    def remote(src, dst, send, recv, to):
        return pltpu.make_async_remote_copy(
            src_ref=src, dst_ref=dst, send_sem=send, recv_sem=recv, device_id=to, device_id_type=MESH
        )

    sent = []

    def go(copy):
        copy.start()
        sent.append(copy)
        return copy

    barrier = pltpu.get_barrier_semaphore()
    for to in row_peers + col_peers:
        pl.semaphore_signal(barrier, inc=1, device_id=to, device_id_type=MESH)

    loads = []
    for k, (src, dst) in enumerate(
        ((x_hbm, x_ref), (wqkv_hbm, wqkv), (wout_hbm, wout), (wup_hbm, wup), (wdown_hbm, wdown))
    ):
        copy = pltpu.make_async_copy(src, dst, load_sem.at[k])
        if k < 2:
            copy.start()
        loads.append(copy)

    length_t, weight, count = token_columns(mask_ref, length_ref, seq)
    cols[:, 0:1] = weight
    cols[:, 1:2] = length_t
    loads[0].wait()
    pl.semaphore_wait(barrier, R + C - 2)

    mine = tuple(rbit[b] for b in reversed(range(rb))) + tuple(cbit[b] for b in reversed(range(cb)))
    part = captions // 2
    pairs = captions * R * C
    staged = len(images.shape) < 3 + rb + cb
    gather = images_hbm if staged else images
    for k in range(2):
        if staged:
            copy = pltpu.make_async_copy(unit_ref.at[pl.ds(k * part, part), :], gather.at[(k,) + mine], load_sem.at[5 + k])
            copy.start()
            loads.append(copy)
        else:
            images[(k,) + mine] = unit_ref[k * part : (k + 1) * part, :]
    if staged:
        loads[5].wait()
        loads[6].wait()

    def stage(i):
        if not staged:
            return images[...].reshape(pairs, width)
        lead = 3 + rb + cb - len(images.shape)
        where = tuple((i >> b) & 1 for b in reversed(range(lead)))
        copy = pltpu.make_async_copy(gather.at[where], images, load_sem.at[5])
        copy.start()
        copy.wait()
        return images[...].reshape(pairs >> lead, width)

    stages = pairs // math.prod(images.shape[:-1])
    order = [("c", b) for b in reversed(range(1, cb))]
    tail = [("r", b) for b in reversed(range(1, rb))]
    plans = (order + [("c", 0)] + tail + [("r", 0)], order + tail + [("c", 0)] + [("r", 0)])
    gathered = [set(), set()]
    pending = [None, None]
    phase = [0, 0]

    def gather_step():
        for k in range(2):
            if pending[k] is not None:
                pending[k].wait_recv()
                gathered[k].add(plans[k][phase[k] - 1])
                pending[k] = None
            if phase[k] < len(plans[k]):
                kind, b = plans[k][phase[k]]
                names = [("r", i) for i in reversed(range(rb))] + [("c", i) for i in reversed(range(cb))]
                where = tuple(slice(None) if nm in gathered[k] else v for nm, v in zip(names, mine))
                dst = gather.at[(k,) + where]
                src = unit_ref.at[pl.ds(k * part, part), :] if phase[k] == 0 else dst
                to = flip_r(b) if kind == "r" else flip_c(b)
                pending[k] = go(remote(src, dst, ag_send.at[k, phase[k]], ag_recv.at[k, phase[k]], to))
                phase[k] += 1

    gather_step()
    x = x_ref[...].astype(f32)
    scaled, _ = stats(x)
    n1[...] = (scaled * g1[...][None] + s1[...][None]).astype(bf16)
    loads[1].wait()
    for copy in loads[2:5]:
        copy.start()
    for q in range(3):
        cut = slice(q * width, (q + 1) * width)
        qkv[:, cut] = dot(n1[...], wqkv[:, cut]).astype(bf16)
    gather_step()
    attend = text_attention(heads, seq, group, width, qkv, probs, at, cols)
    groups = rows // group
    lax.fori_loop(0, groups, attend, 0)
    gather_step()
    loads[2].wait()
    mixed[...] = x_ref[...].astype(f32) + dot(at[...], wout[...])
    scaled, _ = stats(mixed[...])
    n2[...] = (scaled * g2[...][None] + s2[...][None]).astype(bf16)
    weight = cols[:, 0:1]
    loads[3].wait()
    gather_step()

    def up_block(f, carry):
        cut = pl.ds(pl.multiple_of(f * width, 128), width)
        h = dot(n2[...], wup[:, cut])
        phi = 0.5 + 0.5 * lax.erf(h * inv_root2)
        slope[:, cut] = (phi + h * (jnp.exp(-0.5 * h * h) * inv_root_2pi)).astype(bf16)
        act[:, cut] = jnp.sum((h * phi * cols[:, 0:1]).reshape(captions, seq, width), 1)
        return carry

    lax.fori_loop(0, hidden // width, up_block, 0)
    gather_step()
    loads[4].wait()
    pooled = jnp.sum((mixed[...] * weight).reshape(captions, seq, width), 1) + split_dot(act[...], wdown)
    pooled = pooled / count
    inverse = lax.rsqrt(jnp.sum(pooled * pooled, -1, keepdims=True) + epsilon)
    text_unit = (pooled * inverse).astype(bf16)
    span = hidden // C
    for k in range(C):
        pooled_act[k] = act[:, k * span : (k + 1) * span].astype(bf16)
    while pending[0] is not None or pending[1] is not None:
        gather_step()

    t = 2.0 * math.sqrt(width)
    sims = []
    for i in range(stages):
        every = stage(i)
        sims.append(dot_t(text_unit, every))
    e = jnp.exp2(jnp.concatenate(sims, 1) * (t * log2e))
    rowsum[...] = jnp.sum(e, 0, keepdims=True)
    first = [
        go(remote(rowsum, rowsum_c.at[d], ps_send.at[d], ps_recv.at[d], to)) for d, to in enumerate(col_peers)
    ]
    col_scale = 1.0 / jnp.sum(e, -1, keepdims=True)
    acts = []
    for d, to in enumerate(col_peers):
        acts.append(
            go(remote(pooled_act.at[lax.rem(c + d + 1, C)], act_all.at[d], a_send.at[d], a_recv.at[d], to))
        )
    act_all[C - 1] = pooled_act[c]
    total = rowsum[...]
    for d, copy in enumerate(first):
        copy.wait_recv()
        total += rowsum_c[d]
    rowsum_cs[...] = total
    second = [
        go(remote(rowsum_cs, rowsum_r.at[d], ps_send.at[C - 1 + d], ps_recv.at[C - 1 + d], to))
        for d, to in enumerate(row_peers)
    ]
    for d, copy in enumerate(second):
        copy.wait_recv()
        total += rowsum_r[d]
    grad_sim = (e * (1.0 / total + col_scale) * (0.5 / pairs)).astype(bf16)
    share = pairs // stages
    hits = sum(
        dot(grad_sim[:, i * share : (i + 1) * share], every if stages == 1 else stage(i)) for i in range(stages)
    )
    grad_unit = t * hits - (t / pairs) * unit_ref[...].astype(f32)
    along = jnp.sum(grad_unit * pooled, -1, keepdims=True)
    gpc = (inverse * grad_unit - pooled * (inverse * inverse * inverse * along)) / count
    gpc_r = gpc.astype(bf16)
    gpc_own[...] = gpc_r
    gps = [go(remote(gpc_own, gpc_all.at[d], gp_send.at[d], gp_recv.at[d], to)) for d, to in enumerate(col_peers)]
    gpc_all[C - 1] = gpc_r

    def emit(name, row, block, lead=()):
        scatter = scatters[name]
        sub = scatter.sub
        for i in range(0, block.shape[0], sub):
            index = (row + i) // sub
            to = index // (2 * COLORS)
            bits = lead + tuple((to >> b) & 1 for b in reversed(range(cb - len(lead))))
            color, xbit = index % (2 * COLORS) // 2, index % 2
            for s in range(2):
                scatter.buf[(s, color, xbit) + bits] = block[i : i + sub, s * half : (s + 1) * half].astype(bf16)

    class Scatter:
        def __init__(self, index, buf, recvs, offset):
            self.index, self.buf, self.recvs, self.offset = index, buf, recvs, offset
            self.sub = buf.shape[-2]
            self.plans = color_plans(cb)
            self.phase = [0] * COLORS
            self.copies = [None] * COLORS
            self.kept = [None] * COLORS
            self.pieces = []
            self.finals = None

        def rows(self, k):
            return slice(self.offset + k * self.sub, self.offset + (k + 1) * self.sub)

        def start(self, piece):
            self.copy(piece).start()
            if isinstance(piece, int):
                self.started(piece)

        def started(self, piece):
            self.pieces.append(self.copy(piece))
            sent.append(self.pieces[-1])

        def copy(self, piece):
            bits = (piece // 2, piece % 2) if isinstance(piece, int) else (lax.div(piece, 2), lax.rem(piece, 2))
            return remote(
                self.buf.at[(1 - core, slice(None), slice(None)) + bits], self.recvs[0].at[(slice(None), slice(None)) + bits],
                c_send.at[self.index, piece], c_recv.at[self.index, piece], flip_r(0),
            )

        def step(self, colors=range(3)):
            for copy in self.pieces:
                copy.wait_recv()
            self.pieces = []
            for k in colors:
                self.advance(k)

        def done(self):
            return min(self.phase) > len(self.plans[0])

        def advance(self, k):
            p = self.phase[k]
            plan = self.plans[k]
            self.phase[k] += 1
            if p == 0:
                before, here = self.buf.at[core, k], self.recvs[0].at[k]
            else:
                self.copies[k].wait_recv()
                before = self.recvs[0].at[(k,) + self.kept[k]] if p == 1 else self.recvs[p - 1][k].at[self.kept[k]]
                here = self.recvs[p][k]
            if p == len(plan):
                rows = self.rows(k)
                final[core, xh, rows, :] = before[...] + here[...]
                if self.finals:
                    self.finals[k].start()
                return
            kind, b = plan[p]
            left = [("r", 1)] + [("c", i) for i in reversed(range(cb))]
            for gone in plan[:p]:
                left.remove(gone)
            axis = left.index((kind, b))
            bit = xh if kind == "r" else cbit[b]
            give = (slice(None),) * axis + (1 - bit,)
            keep = (slice(None),) * axis + (bit,)
            here[give] = before[give] + here[give]
            to = flip_r(1) if kind == "r" else flip_c(b)
            self.copies[k] = go(
                remote(
                    here.at[give], self.recvs[p + 1][k],
                    rs_send.at[self.index, k, p], rs_recv.at[self.index, k, p], to,
                )
            )
            here[keep] = before[keep] + here[keep]
            self.kept[k] = keep

    up_rows = COLORS * g_up.shape[-2]
    out_rows = COLORS * g_out.shape[-2]
    down_rows = 2 * sub
    up = Scatter(0, g_up, r_up, 0)
    out = Scatter(1, g_out, r_out, up_rows + down_rows)
    rest = Scatter(2, g_qkv, r_qkv, up_rows + down_rows + out_rows)
    scatters = {"up": up, "out": out, "qkv": rest}
    early = slice(up_rows, up_rows + down_rows + out_rows)

    class Finals:
        def __init__(self, index, rows):
            self.index, self.rows = index, rows

        def start(self):
            for b in range(2, rb):
                there = extra.at[b - 2, self.rows]
                swap = remote(final.at[core, xh, self.rows], there, f_send.at[self.index, b], f_recv.at[self.index, b], flip_r(b))
                swap.start()
                swap.wait()
                final[core, xh, self.rows, :] = final[core, xh, self.rows, :] + there[...]
            here = final.at[core, xh, self.rows]
            self.copy = go(remote(here, here, f_send.at[self.index, 0], f_recv.at[self.index, 0], flip_r(1)))

        def step(self):
            self.copy.wait_recv()
            here = final.at[core, :, self.rows]
            self.copy = go(remote(here, here, f_send.at[self.index, 1], f_recv.at[self.index, 1], flip_r(0)))

        def end(self):
            self.copy.wait_recv()

    first_finals, rest.finals = Finals(0, early), [Finals(1 + k, rest.rows(k)) for k in range(COLORS)]
    up.finals = [Finals(1 + COLORS + k, up.rows(k)) for k in range(COLORS)]

    def up_back(f, carry):
        cut = pl.ds(pl.multiple_of(f * width, 128), width)
        hh = dot_t(gpc_own[...], wdown[cut, :])
        spread = jnp.broadcast_to(hh[:, None, :], (captions, seq, width)).reshape(rows, width)
        slope[:, cut] = (spread * cols[:, 0:1] * slope[:, cut].astype(f32)).astype(bf16)
        emit("up", 0, dot_0(slope[:, cut], n2[...]), (lax.div(f, 2), lax.rem(f, 2)))
        up.start(f)
        return carry

    lax.fori_loop(0, 4, up_back, 0)
    for piece in range(4):
        up.started(piece)
    gn2 = dot_t(slope[...], wup[...])
    up.step()
    scaled, inv2 = stats(mixed[...])
    vec[2:3, :] = jnp.sum(gn2 * scaled, 0, keepdims=True)
    vec[3:4, :] = jnp.sum(gn2, 0, keepdims=True)
    spread = jnp.broadcast_to(gpc[:, None, :], (captions, seq, width)).reshape(rows, width) * weight
    mixed[...] = spread + norm_back(gn2, scaled, inv2, g2[...][None])
    n2[...] = mixed[...].astype(bf16)
    emit("out", 0, dot_0(n2[...], at[...]))
    for piece in range(4):
        out.start(piece)
    at[...] = dot_t(n2[...], wout[...]).astype(bf16)
    attend_back = text_attention_back(heads, group, width, qkv, probs, at)
    lax.fori_loop(0, groups // 2, attend_back, 0)
    up.step()
    out.step()

    for copy in acts + gps:
        copy.wait_recv()
    down = dot_0(act_all[...].reshape(C * captions, span), gpc_all[...].reshape(C * captions, width))
    for j in range(4):
        for s in range(2):
            d_part[s, j // 2, j % 2] = down[j * sub : (j + 1) * sub, s * half : (s + 1) * half].astype(bf16)
    d0 = go(remote(d_part.at[1 - core], d_recv, d_send.at[0], d_recv_sem.at[0], flip_r(0)))

    lax.fori_loop(groups // 2, groups, attend_back, 0)
    up.step(range(2))
    pieces = 0
    for q in range(3):
        emit("qkv", q * width, dot_0(qkv[:, q * width : (q + 1) * width], n1[...]))
        while pieces < 4 * (q + 1) // 3:
            rest.start(pieces)
            pieces += 1
    up.step(range(2, 3))
    out.step()
    d0.wait_recv()
    d_recv[:, 1 - xh] = d_part[core, :, 1 - xh] + d_recv[:, 1 - xh]
    d1 = go(remote(d_recv.at[:, 1 - xh], d_recv2, d_send.at[1], d_recv_sem.at[1], flip_r(1)))
    d_recv[:, xh] = d_part[core, :, xh] + d_recv[:, xh]
    rest.step()
    gn1 = dot_t(qkv[...], wqkv[...])
    up.step()
    scaled, inv1 = stats(x_ref[...].astype(f32))
    vec[0:1, :] = jnp.sum(gn1 * scaled, 0, keepdims=True)
    vec[1:2, :] = jnp.sum(gn1, 0, keepdims=True)
    vfirst = [go(remote(vec, vec_c.at[d], v_send.at[d], v_recv.at[d], to)) for d, to in enumerate(col_peers)]
    out.step()
    mixed[...] = mixed[...] + norm_back(gn1, scaled, inv1, g1[...][None])
    gx_out = pltpu.make_async_copy(mixed, gx_hbm, out_sem.at[0])
    gx_out.start()
    d1.wait_recv()
    for k in range(2):
        final[core, xh, up_rows + k * sub : up_rows + (k + 1) * sub, :] = d_recv[k, xh] + d_recv2[k]
    rest.step()
    while not up.done():
        up.step()
        if not out.done():
            out.step()
    while not out.done():
        out.step()
    first_finals.start()
    vtotal = vec[...]
    for d, copy in enumerate(vfirst):
        copy.wait_recv()
        vtotal += vec_c[d]
    vec_cs[...] = vtotal
    vsecond = [
        go(remote(vec_cs, vec_r.at[d], v_send.at[C - 1 + d], v_recv.at[C - 1 + d], to)) for d, to in enumerate(row_peers)
    ]
    rest.step()
    for some in up.finals + [first_finals]:
        some.step()
    while not rest.done():
        rest.step()
    for last in rest.finals:
        last.step()
    for d, copy in enumerate(vsecond):
        copy.wait_recv()
        vtotal += vec_r[d]
    vecs_ref[...] = vtotal
    for some in up.finals + [first_finals]:
        some.end()
    for last in rest.finals:
        last.end()
    parts_out = pltpu.make_async_copy(final, parts_hbm, out_sem.at[1])
    parts_out.start()
    for copy in sent:
        copy.wait_send()
    gx_out.wait()
    parts_out.wait()


def text_call(R, C, unit, tokens, mask, length, g1, s1, wqkv, wout, g2, s2, wup, wdown, heads=12, group=128):
    captions, seq, width = tokens.shape
    rows, hidden = captions * seq, wup.shape[1]
    rb, cb = log2(R), log2(C)
    half, sub, span = width // 2, hidden // (4 * C), hidden // C
    V, S, D = pltpu.VMEM, jax.ShapeDtypeStruct, pltpu.SemaphoreType.DMA
    pairs = captions * R * C
    bits_c = (2,) * cb

    dims, tail = 1 + rb + cb, (captions // 2, width)
    lead = max(log2(pairs // 1024), 0)
    held_dims, staged_dims = dims - lead, dims if lead else 0

    subs = [hidden // (2 * COLORS * C), width // (2 * COLORS * C), 3 * width // (2 * COLORS * C)]

    def recvs(rows):
        phases = len(color_plans(cb)[0]) + 1
        return [V((COLORS, 2) + bits_c + (rows, half), bf16)] + [
            [V((2,) * (1 + cb - p) + (rows, half), bf16) for _ in range(COLORS)] for p in range(1, phases)
        ]

    total = COLORS * sum(subs) + 2 * sub
    vm = pl.BlockSpec(memory_space=pltpu.VMEM)
    hbm = pl.BlockSpec(memory_space=pl.ANY)
    out = pl.pallas_call(
        functools.partial(text_step, (R, C, captions, seq, group), heads),
        name="text",
        in_specs=[vm] * 7 + [hbm] * 5,
        out_specs=(hbm, hbm, vm, hbm),
        out_shape=(S((rows, width), f32), S((2, 2, total, half), bf16), S((4, width), f32), S((2,) * staged_dims + tail, bf16)),
        scratch_shapes=[
            V((rows, width), bf16), V(wqkv.shape, bf16), V(wout.shape, bf16), V(wup.shape, bf16), V(wdown.shape, bf16),
            V((rows, width), bf16), V((rows, 3 * width), bf16), V((rows, heads * group), f32), V((rows, width), bf16),
            V((rows, width), f32), V((rows, width), bf16), V((rows, hidden), bf16), V((captions, hidden), f32), V((rows, 128), f32),
            V((2,) * held_dims + tail, bf16),
            V((1, pairs), f32), V((C - 1, 1, pairs), f32), V((1, pairs), f32), V((R - 1, 1, pairs), f32),
            V((C, captions, span), bf16), V((C, captions, span), bf16), V((captions, width), bf16), V((C, captions, width), bf16),
            *[V((2, COLORS, 2) + bits_c + (n, half), bf16) for n in subs], *[recvs(n) for n in subs],
            V((2, 2, 2, sub, half), bf16), V((2, 2, sub, half), bf16), V((2, sub, half), bf16),
            V((2, 2, total, half), bf16), V((max(rb - 2, 1), total, half), bf16),
            V((4, width), f32), V((C - 1, 4, width), f32), V((4, width), f32), V((R - 1, 4, width), f32),
            D((7,)), D((2,)), D((2, rb + cb)), D((2, rb + cb)), D((R + C - 2,)), D((R + C - 2,)),
            D((C - 1,)), D((C - 1,)), D((C - 1,)), D((C - 1,)),
            D((3, 4)), D((3, 4)), D((3, COLORS, cb + 1)), D((3, COLORS, cb + 1)), D((2,)), D((2,)), D((1 + 2 * COLORS, max(rb, 2))), D((1 + 2 * COLORS, max(rb, 2))), D((R + C - 2,)), D((R + C - 2,)),
        ],
        compiler_params=pltpu.CompilerParams(collective_id=0, has_side_effects=True, vmem_limit_bytes=67043328),
    )(unit, mask.T, length[None], g1, s1, g2, s2, tokens.reshape(rows, width), wqkv, wout, wup, wdown)
    return out[:3]


def finish_kernel(
    col_size, parts, vecs, shift, gx_in, gx_out, up_out, out_out, qkv_out, down_out, v0, v1, v2, v3,
    gx, up, out, qkv, down, sems
):
    load = pltpu.make_async_copy(gx_in, gx, sems.at[0])
    load.start()
    stores = []

    def store(src, dst):
        copy = pltpu.make_async_copy(src, dst, sems.at[1 + len(stores)])
        copy.start()
        stores.append(copy)

    def blocks(lo, colors, sub):
        for j in range(2 * colors):
            rows = slice(lo + j // 2 * sub, lo + (j // 2 + 1) * sub)
            yield j * sub, jnp.concatenate([parts[0, j % 2, rows, :], parts[1, j % 2, rows, :]], -1).astype(f32)

    def fill(ref, lo, colors):
        sub = ref.shape[0] // (2 * colors)
        for at_row, block in blocks(lo, colors, sub):
            ref[at_row : at_row + sub, :] = block

    hidden_share = down.shape[0]
    fill(down, hidden_share // 2, 2)
    store(down, down_out)
    fill(qkv, hidden_share + out.shape[0] // 2, COLORS)
    store(qkv, qkv_out)
    fill(out, hidden_share, COLORS)
    store(out, out_out)
    load.wait()
    store(gx, gx_out)
    up[...] = jnp.concatenate([block for _, block in blocks(0, COLORS, hidden_share // (2 * COLORS))], 0).T
    store(up, up_out)
    width = vecs.shape[1]
    share = width // col_size
    lane = lax.broadcasted_iota(jnp.int32, (width, share), 1)
    row = lax.broadcasted_iota(jnp.int32, (width, share), 0)
    pick = jnp.where(row == lane + shift[0], 1.0, 0.0)
    own = jnp.dot(vecs[...], pick, precision=lax.Precision.HIGHEST, preferred_element_type=f32)
    for k, v in enumerate((v0, v1, v2, v3)):
        v[...] = own[k : k + 1, :]
    for copy in stores:
        copy.wait()


def finish_call(C, hidden, gx, parts, vecs):
    width = 2 * parts.shape[-1]
    share, hidden_share = width // C, hidden // C
    S, V = jax.ShapeDtypeStruct, pltpu.VMEM
    shift = (lax.axis_index("col") * share).astype(jnp.int32)[None]
    vm = pl.BlockSpec(memory_space=pltpu.VMEM)
    hbm = pl.BlockSpec(memory_space=pl.ANY)
    shapes = [gx.shape, (width, hidden_share), (share, width), (3 * share, width), (hidden_share, width)]
    return pl.pallas_call(
        functools.partial(finish_kernel, C),
        name="finish",
        in_specs=[vm, vm, pl.BlockSpec(memory_space=pltpu.SMEM), hbm],
        out_specs=(hbm,) * 5 + (vm,) * 4,
        out_shape=tuple(S(s, f32) for s in shapes) + (S((1, share), f32),) * 4,
        scratch_shapes=[V(s, f32) for s in shapes] + [pltpu.SemaphoreType.DMA((6,))],
    )(parts, vecs, shift, gx)


def on_device(
    image_tokens, caption_tokens, caption_mask, caption_length,
    image_gain1, image_shift1, image_qkv, image_out, image_gain2, image_shift2, image_up, image_down,
    text_gain1, text_shift1, text_qkv, text_out, text_gain2, text_shift2, text_up, text_down,
):
    R, C = lax.axis_size("row"), lax.axis_size("col")
    unit = image_unit(
        image_tokens, image_gain1, image_shift1, image_qkv, image_out,
        image_gain2, image_shift2, image_up, image_down,
    )
    grad_tokens, parts, vecs = text_call(
        R, C, unit, caption_tokens, caption_mask, caption_length, text_gain1, text_shift1, text_qkv, text_out,
        text_gain2, text_shift2, text_up, text_down,
    )
    grad_tokens, up, out, qkv, down, gain1, shift1, gain2, shift2 = finish_call(C, text_up.shape[1], grad_tokens, parts, vecs)
    return (
        grad_tokens.reshape(caption_tokens.shape), gain1[0], shift1[0], qkv.T, out.T, gain2[0], shift2[0], up, down,
    )


def solution(mesh):
    pair = P(("row", "col"))
    return jax.shard_map(
        on_device,
        mesh=mesh,
        in_specs=(pair,) * 4 + (P(),) * 16,
        out_specs=(pair, P("col"), P("col"), P(None, "col"), P(None, "col"), P("col"), P("col"), P(None, "col"), P("col")),
        check_vma=False,
    )
```

```python
import math, functools
import jax, jax.numpy as jnp
from jax import lax
from jax.experimental import pallas as pl
from jax.experimental.pallas import tpu as pltpu
from jax.sharding import PartitionSpec as P

epsilon = 1e-06
log2e = 1.4426950408889634
inv_root2 = 0.7071067811865476
f32 = jnp.float32
bf16 = jnp.bfloat16


def dot(a, b):
    return jnp.dot(a, b, preferred_element_type=f32)


def dot_t(a, b):
    return lax.dot_general(a, b, (((1,), (1,)), ((), ())), preferred_element_type=f32)


def stats(x):
    centred = x - jnp.mean(x, -1, keepdims=True)
    inverse = lax.rsqrt(jnp.mean(centred * centred, -1, keepdims=True) + epsilon)
    return centred * inverse, inverse


def two_heads(v):
    first = lax.broadcasted_iota(jnp.int32, v.shape, 1) < v.shape[1] // 2
    zero = jnp.zeros_like(v)
    return jnp.concatenate([jnp.where(first, v, zero), jnp.where(first, zero, v)], 0)


def gelu(v):
    u = 0.5 * v
    return u * lax.erf(v * inv_root2) + u


def image_kernel(
    heads, x_ref, g1, s1, wqkv_hbm, wout_hbm, g2, s2, wup_hbm, wdown_hbm, out_ref,
    tok, xs, n, qkv, at, mixed, act, pooled, wqkv, wout, wup, wdown, sems
):
    tokens, images, width = x_ref.shape
    pad = -(-tokens // 8) * 8
    rows = images * pad
    i = pl.program_id(0)
    weights = ((wqkv_hbm, wqkv), (wout_hbm, wout), (wup_hbm, wup), (wdown_hbm, wdown))

    def fetched(k):
        @pl.when(i == 0)
        def _():
            pltpu.make_async_copy(*weights[k], sems.at[k]).wait()
            for later in range(1, 4 if k == 0 else 0):
                pltpu.make_async_copy(*weights[later], sems.at[later]).start()

    @pl.when(i == 0)
    def _():
        pltpu.make_async_copy(*weights[0], sems.at[0]).start()
        xs[...] = jnp.zeros_like(xs)
        qkv[rows:, :] = jnp.zeros((qkv.shape[0] - rows, 3 * width), bf16)

    count = tokens * images
    for j in range(width // 128):
        lanes = slice(j * 128, (j + 1) * 128)
        tok[j * count : (j + 1) * count, :] = x_ref[:, :, lanes].astype(f32).reshape(count, 128)
    for j in range(width // 128):
        for k in range(images):
            xs[k * pad : k * pad + tokens, j * 128 : (j + 1) * 128] = tok[pl.ds(j * count + k, tokens, stride=images), :]
    scaled, _ = stats(xs[...])
    n[...] = (scaled * g1[...][None] + s1[...][None]).astype(bf16)
    fetched(0)
    for c in range(3):
        cols = slice(c * width, (c + 1) * width)
        qkv[:rows, cols] = dot(n[...], wqkv[:, cols]).astype(bf16)

    group = 2 * pad
    hd = width // heads
    r_id = lax.broadcasted_iota(jnp.int32, (group, 2 * hd), 0)
    c_id = lax.broadcasted_iota(jnp.int32, (group, 2 * hd), 1)
    same = (r_id < pad) == (c_id < pad)
    inside = jnp.where(c_id < pad, c_id, c_id - pad) < tokens
    keep = same & inside
    ones = two_heads(jnp.ones((2 * hd, 2 * hd), bf16))
    factor = hd ** (-0.5) * log2e

    def attend(g, carry):
        rs = pl.ds(pl.multiple_of(g * group, 16), group)
        ks = pl.ds(pl.multiple_of(g * group, 16), 2 * hd)
        def scores(hp):
            k2 = two_heads(qkv[ks, width + hp * 2 * hd : width + (hp + 1) * 2 * hd])
            return dot_t(qkv[rs, hp * 2 * hd : (hp + 1) * 2 * hd], k2)

        def values(hp, es):
            v2 = two_heads(qkv[ks, 2 * width + hp * 2 * hd : 2 * width + (hp + 1) * 2 * hd])
            out = dot(es, jnp.concatenate([v2, ones], 1))
            at[rs, hp * 2 * hd : (hp + 1) * 2 * hd] = (out[:, : 2 * hd] / out[:, 2 * hd :]).astype(bf16)

        after, before = scores(0), None
        for hp in range(heads // 2):
            s2 = after
            if hp + 1 < heads // 2:
                after = scores(hp + 1)
            es = []
            for h in range(2):
                s = jnp.where(keep, s2[:, h * 2 * hd : (h + 1) * 2 * hd] * factor, -1e30)
                es.append(jnp.exp2(s - jnp.max(s, -1, keepdims=True)).astype(bf16))
            if before is not None:
                values(hp - 1, before)
            before = jnp.concatenate(es, 1)
        values(heads // 2 - 1, before)
        return carry

    lax.fori_loop(0, rows // group, attend, 0)
    fetched(1)
    mixed[...] = xs[...] + dot(at[...], wout[...])
    row = lax.broadcasted_iota(jnp.int32, (pad, 1), 0)
    valid = (row < tokens).astype(f32)
    dst = pl.ds(pl.multiple_of(i * images, 8), images)
    m3 = mixed[...].reshape(images, pad, width)
    pooled[dst, :] = jnp.sum(m3 * valid[None], 1)
    scaled, _ = stats(mixed[...])
    normed = ((scaled * g2[...][None] + s2[...][None]).reshape(images, pad, width) * valid[None]).reshape(rows, width)
    n[...] = normed.astype(bf16)
    hidden = wup.shape[1]
    step = 768
    fetched(2)
    for c in range(0, hidden, step):
        a = gelu(dot(n[...], wup[:, c : c + step]))
        act[dst, c : c + step] = jnp.sum(a.reshape(images, pad, step), 1)

    fetched(3)

    @pl.when(i == pl.num_programs(0) - 1)
    def _():
        a = act[...] * (1.0 / tokens)
        hi = a.astype(bf16)
        lo = (a - hi.astype(f32)).astype(bf16)
        count = a.shape[0]
        both = dot(jnp.concatenate([hi, lo], 0), wdown[...])
        e = pooled[...] * (1.0 / tokens) + both[:count] + both[count:]
        out_ref[...] = (e * lax.rsqrt(jnp.sum(e * e, -1, keepdims=True) + epsilon)).astype(bf16)


def image_unit(x, g1, s1, wqkv, wout, g2, s2, wup, wdown, heads=12, images=8):
    count, tokens, width = x.shape
    hidden = wup.shape[1]
    pad = -(-tokens // 8) * 8
    rows = images * pad
    full = lambda a: pl.BlockSpec(a.shape, lambda i: (0,) * a.ndim, pipeline_mode=pl.Buffered(1))
    hbm = pl.BlockSpec(memory_space=pl.ANY)
    args = (jnp.transpose(x, (1, 0, 2)), g1, s1, wqkv, wout, g2, s2, wup, wdown)
    return pl.pallas_call(
        functools.partial(image_kernel, heads),
        name="image",
        grid=(count // images,),
        out_shape=jax.ShapeDtypeStruct((count, width), bf16),
        in_specs=[pl.BlockSpec((tokens, images, width), lambda i: (0, i, 0))]
        + [full(a) if a.ndim == 1 else hbm for a in args[1:]],
        out_specs=pl.BlockSpec((count, width), lambda i: (0, 0)),
        scratch_shapes=[
            pltpu.VMEM((width // 128 * tokens * images, 128), f32),
            pltpu.VMEM((rows, width), f32),
            pltpu.VMEM((rows, width), bf16),
            pltpu.VMEM((rows + 16, 3 * width), bf16),
            pltpu.VMEM((rows, width), bf16),
            pltpu.VMEM((rows, width), f32),
            pltpu.VMEM((count, hidden), f32),
            pltpu.VMEM((count, width), f32),
        ]
        + [pltpu.VMEM(w.shape, bf16) for w in (wqkv, wout, wup, wdown)]
        + [pltpu.SemaphoreType.DMA((4,))],
        compiler_params=pltpu.CompilerParams(vmem_limit_bytes=67043328),
    )(*args)

def dot_0(a, b):
    return lax.dot_general(a, b, (((0,), (0,)), ((), ())), preferred_element_type=f32)


def norm_back(grad_normed, scaled, inverse, gain):
    g = grad_normed * gain
    centre = jnp.mean(g, -1, keepdims=True)
    along = jnp.mean(g * scaled, -1, keepdims=True)
    return inverse * (g - centre - scaled * along)


def token_columns(mask_ref, length_ref, seq):
    captions = mask_ref.shape[1]
    rows = captions * seq
    row = lax.broadcasted_iota(jnp.int32, (rows, captions), 0)
    lane = lax.broadcasted_iota(jnp.int32, (rows, captions), 1)
    length = length_ref[...].astype(f32)
    own = row // seq == lane
    length_t = jnp.sum(jnp.where(own, length, 0.0), -1, keepdims=True)
    spread = dot_t(jnp.where(own, 1.0, 0.0).astype(bf16), mask_ref[...].astype(f32).astype(bf16))
    row = lax.broadcasted_iota(jnp.int32, (rows, seq), 0)
    lane = lax.broadcasted_iota(jnp.int32, (rows, seq), 1)
    mask_t = jnp.sum(jnp.where(row % seq == lane, spread, 0.0), -1, keepdims=True)
    place = (lax.broadcasted_iota(jnp.int32, (rows, 1), 0) % seq).astype(f32)
    weight = jnp.where(place < length_t, mask_t, 0.0)
    count = jnp.sum(weight.reshape(captions, seq, 1), 1)
    return length_t, weight, jnp.maximum(count, 1.0)


def text_attention(heads, seq, group, width, qkv, probs, at, cols):
    hd = width // heads
    r_id = lax.broadcasted_iota(jnp.int32, (group, group), 0)
    c_id = lax.broadcasted_iota(jnp.int32, (group, group), 1)
    same = r_id // seq == c_id // seq
    place = (c_id % seq).astype(f32)
    factor = hd ** (-0.5) * log2e

    def attend(g, carry):
        rs = pl.ds(pl.multiple_of(g * group, 16), group)
        keep = same & (place < cols[rs, 1:2])

        def scores(hp):
            k2 = two_heads(qkv[rs, width + hp * 2 * hd : width + (hp + 1) * 2 * hd])
            return dot_t(qkv[rs, hp * 2 * hd : (hp + 1) * 2 * hd], k2)

        def values(hp, ps):
            v2 = two_heads(qkv[rs, 2 * width + hp * 2 * hd : 2 * width + (hp + 1) * 2 * hd])
            at[rs, hp * 2 * hd : (hp + 1) * 2 * hd] = dot(ps, v2).astype(bf16)

        after, before = scores(0), None
        for hp in range(heads // 2):
            s2 = after
            if hp + 1 < heads // 2:
                after = scores(hp + 1)
            ps = []
            for h in range(2):
                s = jnp.where(keep, s2[:, h * group : (h + 1) * group] * factor, -1e30)
                e = jnp.exp2(s - jnp.max(s, -1, keepdims=True))
                p = e * (1.0 / jnp.sum(e, -1, keepdims=True))
                probs[rs, pl.ds((hp * 2 + h) * group, group)] = p
                ps.append(p.astype(bf16))
            if before is not None:
                values(hp - 1, before)
            before = jnp.concatenate(ps, 1)
        values(heads // 2 - 1, before)
        return carry

    return attend


inv_root_2pi = 0.3989422804014327


def split_dot(a, w):
    hi = a.astype(bf16)
    lo = (a - hi.astype(f32)).astype(bf16)
    both = dot(jnp.concatenate([hi, lo], 0), w[...])
    return both[: a.shape[0]] + both[a.shape[0] :]


def text_attention_back(heads, group, width, qkv, probs, at):
    hd = width // heads
    scale = hd ** (-0.5)

    def attend(g, carry):
        rs = pl.ds(pl.multiple_of(g * group, 16), group)
        for hp in range(heads // 2):
            lanes = slice(hp * 2 * hd, (hp + 1) * 2 * hd)
            klanes = slice(width + lanes.start, width + lanes.stop)
            vlanes = slice(2 * width + lanes.start, 2 * width + lanes.stop)
            ga = at[rs, lanes]
            q2, k2, v2 = two_heads(qkv[rs, lanes]), two_heads(qkv[rs, klanes]), two_heads(qkv[rs, vlanes])
            dp2 = dot_t(ga, v2)
            ps, ds = [], []
            for h in range(2):
                p = probs[rs, pl.ds((hp * 2 + h) * group, group)]
                dp = dp2[:, h * group : (h + 1) * group]
                ds.append((p * (dp - jnp.sum(dp * p, -1, keepdims=True))).astype(bf16))
                ps.append(p.astype(bf16))
            dv = dot_0(jnp.concatenate(ps, 0), two_heads(ga))
            dq = dot(jnp.concatenate(ds, 1), k2)
            dk = dot_0(jnp.concatenate(ds, 0), q2)
            qkv[rs, lanes] = (dq * scale).astype(bf16)
            qkv[rs, klanes] = (dk * scale).astype(bf16)
            qkv[rs, vlanes] = dv.astype(bf16)
        return carry

    return attend


MESH = pl.DeviceIdType.MESH


COLORS = 3


def color_plans(cb):
    rest = [("c", b) for b in range(1, cb)]
    return [[("r", 1), ("c", 0)] + rest, [("c", 0), ("r", 1)] + rest, rest + [("c", 0), ("r", 1)]]


def log2(n):
    return n.bit_length() - 1


def text_step(
    shape, heads,
    unit_ref, mask_ref, length_ref, g1, s1, g2, s2, x_hbm, wqkv_hbm, wout_hbm, wup_hbm, wdown_hbm,
    gx_hbm, parts_hbm, vecs_ref, images_hbm,
    x_ref, wqkv, wout, wup, wdown, n1, qkv, probs, at, mixed, n2, slope, act, cols,
    images, rowsum, rowsum_c, rowsum_cs, rowsum_r, pooled_act, act_all, gpc_own, gpc_all,
    g_up, g_out, g_qkv, r_up, r_out, r_qkv, d_part, d_recv, d_recv2, final, extra, vec, vec_c, vec_cs, vec_r,
    load_sem, out_sem, ag_send, ag_recv, ps_send, ps_recv, a_send, a_recv, gp_send, gp_recv,
    c_send, c_recv, rs_send, rs_recv, d_send, d_recv_sem, f_send, f_recv, v_send, v_recv,
):
    R, C, captions, seq, group = shape
    rb, cb = log2(R), log2(C)
    r, c = lax.axis_index("row"), lax.axis_index("col")
    rbit = [lax.rem(lax.div(r, 1 << b), 2) for b in range(rb)]
    cbit = [lax.rem(lax.div(c, 1 << b), 2) for b in range(cb)]
    core, xh = rbit[0], rbit[1]
    rows, width = x_ref.shape
    hidden = wup.shape[1]
    half = width // 2
    sub = hidden // (4 * C)

    def flip_r(b):
        return (r + (1 - 2 * rbit[b]) * (1 << b), c)

    def flip_c(b):
        return (r, c + (1 - 2 * cbit[b]) * (1 << b))

    row_peers = [(lax.rem(r + d, R), c) for d in range(1, R)]
    col_peers = [(r, lax.rem(c + d, C)) for d in range(1, C)]

    def remote(src, dst, send, recv, to):
        return pltpu.make_async_remote_copy(
            src_ref=src, dst_ref=dst, send_sem=send, recv_sem=recv, device_id=to, device_id_type=MESH
        )

    sent = []

    def go(copy):
        copy.start()
        sent.append(copy)
        return copy

    barrier = pltpu.get_barrier_semaphore()
    for to in row_peers + col_peers:
        pl.semaphore_signal(barrier, inc=1, device_id=to, device_id_type=MESH)

    loads = []
    for k, (src, dst) in enumerate(
        ((x_hbm, x_ref), (wqkv_hbm, wqkv), (wout_hbm, wout), (wup_hbm, wup), (wdown_hbm, wdown))
    ):
        copy = pltpu.make_async_copy(src, dst, load_sem.at[k])
        if k < 2:
            copy.start()
        loads.append(copy)

    length_t, weight, count = token_columns(mask_ref, length_ref, seq)
    cols[:, 0:1] = weight
    cols[:, 1:2] = length_t
    loads[0].wait()
    pl.semaphore_wait(barrier, R + C - 2)

    mine = tuple(rbit[b] for b in reversed(range(rb))) + tuple(cbit[b] for b in reversed(range(cb)))
    part = captions // 2
    pairs = captions * R * C
    staged = len(images.shape) < 3 + rb + cb
    gather = images_hbm if staged else images
    for k in range(2):
        if staged:
            copy = pltpu.make_async_copy(unit_ref.at[pl.ds(k * part, part), :], gather.at[(k,) + mine], load_sem.at[5 + k])
            copy.start()
            loads.append(copy)
        else:
            images[(k,) + mine] = unit_ref[k * part : (k + 1) * part, :]
    if staged:
        loads[5].wait()
        loads[6].wait()

    def stage(i):
        if not staged:
            return images[...].reshape(pairs, width)
        lead = 3 + rb + cb - len(images.shape)
        where = tuple((i >> b) & 1 for b in reversed(range(lead)))
        copy = pltpu.make_async_copy(gather.at[where], images, load_sem.at[5])
        copy.start()
        copy.wait()
        return images[...].reshape(pairs >> lead, width)

    stages = pairs // math.prod(images.shape[:-1])
    order = [("c", b) for b in reversed(range(1, cb))]
    tail = [("r", b) for b in reversed(range(1, rb))]
    plans = (order + [("c", 0)] + tail + [("r", 0)], order + tail + [("c", 0)] + [("r", 0)])
    gathered = [set(), set()]
    pending = [None, None]
    phase = [0, 0]

    def gather_step():
        for k in range(2):
            if pending[k] is not None:
                pending[k].wait_recv()
                gathered[k].add(plans[k][phase[k] - 1])
                pending[k] = None
            if phase[k] < len(plans[k]):
                kind, b = plans[k][phase[k]]
                names = [("r", i) for i in reversed(range(rb))] + [("c", i) for i in reversed(range(cb))]
                where = tuple(slice(None) if nm in gathered[k] else v for nm, v in zip(names, mine))
                dst = gather.at[(k,) + where]
                src = unit_ref.at[pl.ds(k * part, part), :] if phase[k] == 0 else dst
                to = flip_r(b) if kind == "r" else flip_c(b)
                pending[k] = go(remote(src, dst, ag_send.at[k, phase[k]], ag_recv.at[k, phase[k]], to))
                phase[k] += 1

    gather_step()
    x = x_ref[...].astype(f32)
    scaled, _ = stats(x)
    n1[...] = (scaled * g1[...][None] + s1[...][None]).astype(bf16)
    loads[1].wait()
    for copy in loads[2:5]:
        copy.start()
    for q in range(3):
        cut = slice(q * width, (q + 1) * width)
        qkv[:, cut] = dot(n1[...], wqkv[:, cut]).astype(bf16)
    gather_step()
    attend = text_attention(heads, seq, group, width, qkv, probs, at, cols)
    groups = rows // group
    lax.fori_loop(0, groups, attend, 0)
    gather_step()
    loads[2].wait()
    mixed[...] = x_ref[...].astype(f32) + dot(at[...], wout[...])
    scaled, _ = stats(mixed[...])
    n2[...] = (scaled * g2[...][None] + s2[...][None]).astype(bf16)
    weight = cols[:, 0:1]
    loads[3].wait()
    gather_step()

    def up_block(f, carry):
        cut = pl.ds(pl.multiple_of(f * width, 128), width)
        h = dot(n2[...], wup[:, cut])
        phi = 0.5 + 0.5 * lax.erf(h * inv_root2)
        slope[:, cut] = (phi + h * (jnp.exp(-0.5 * h * h) * inv_root_2pi)).astype(bf16)
        act[:, cut] = jnp.sum((h * phi * cols[:, 0:1]).reshape(captions, seq, width), 1)
        return carry

    lax.fori_loop(0, hidden // width, up_block, 0)
    gather_step()
    loads[4].wait()
    pooled = jnp.sum((mixed[...] * weight).reshape(captions, seq, width), 1) + split_dot(act[...], wdown)
    pooled = pooled / count
    inverse = lax.rsqrt(jnp.sum(pooled * pooled, -1, keepdims=True) + epsilon)
    text_unit = (pooled * inverse).astype(bf16)
    span = hidden // C
    for k in range(C):
        pooled_act[k] = act[:, k * span : (k + 1) * span].astype(bf16)
    while pending[0] is not None or pending[1] is not None:
        gather_step()

    t = 2.0 * math.sqrt(width)
    sims = []
    for i in range(stages):
        every = stage(i)
        sims.append(dot_t(text_unit, every))
    e = jnp.exp2(jnp.concatenate(sims, 1) * (t * log2e))
    rowsum[...] = jnp.sum(e, 0, keepdims=True)
    first = [
        go(remote(rowsum, rowsum_c.at[d], ps_send.at[d], ps_recv.at[d], to)) for d, to in enumerate(col_peers)
    ]
    col_scale = 1.0 / jnp.sum(e, -1, keepdims=True)
    acts = []
    for d, to in enumerate(col_peers):
        acts.append(
            go(remote(pooled_act.at[lax.rem(c + d + 1, C)], act_all.at[d], a_send.at[d], a_recv.at[d], to))
        )
    act_all[C - 1] = pooled_act[c]
    total = rowsum[...]
    for d, copy in enumerate(first):
        copy.wait_recv()
        total += rowsum_c[d]
    rowsum_cs[...] = total
    second = [
        go(remote(rowsum_cs, rowsum_r.at[d], ps_send.at[C - 1 + d], ps_recv.at[C - 1 + d], to))
        for d, to in enumerate(row_peers)
    ]
    for d, copy in enumerate(second):
        copy.wait_recv()
        total += rowsum_r[d]
    grad_sim = (e * (1.0 / total + col_scale) * (0.5 / pairs)).astype(bf16)
    share = pairs // stages
    hits = sum(
        dot(grad_sim[:, i * share : (i + 1) * share], every if stages == 1 else stage(i)) for i in range(stages)
    )
    grad_unit = t * hits - (t / pairs) * unit_ref[...].astype(f32)
    along = jnp.sum(grad_unit * pooled, -1, keepdims=True)
    gpc = (inverse * grad_unit - pooled * (inverse * inverse * inverse * along)) / count
    gpc_r = gpc.astype(bf16)
    gpc_own[...] = gpc_r
    gps = [go(remote(gpc_own, gpc_all.at[d], gp_send.at[d], gp_recv.at[d], to)) for d, to in enumerate(col_peers)]
    gpc_all[C - 1] = gpc_r

    def emit(name, row, block, lead=()):
        scatter = scatters[name]
        sub = scatter.sub
        for i in range(0, block.shape[0], sub):
            index = (row + i) // sub
            to = index // (2 * COLORS)
            bits = lead + tuple((to >> b) & 1 for b in reversed(range(cb - len(lead))))
            color, xbit = index % (2 * COLORS) // 2, index % 2
            for s in range(2):
                scatter.buf[(s, color, xbit) + bits] = block[i : i + sub, s * half : (s + 1) * half].astype(bf16)

    class Scatter:
        def __init__(self, index, buf, recvs, offset):
            self.index, self.buf, self.recvs, self.offset = index, buf, recvs, offset
            self.sub = buf.shape[-2]
            self.plans = color_plans(cb)
            self.phase = [0] * COLORS
            self.copies = [None] * COLORS
            self.kept = [None] * COLORS
            self.pieces = []
            self.finals = None

        def rows(self, k):
            return slice(self.offset + k * self.sub, self.offset + (k + 1) * self.sub)

        def start(self, piece):
            self.copy(piece).start()
            if isinstance(piece, int):
                self.started(piece)

        def started(self, piece):
            self.pieces.append(self.copy(piece))
            sent.append(self.pieces[-1])

        def copy(self, piece):
            bits = (piece // 2, piece % 2) if isinstance(piece, int) else (lax.div(piece, 2), lax.rem(piece, 2))
            return remote(
                self.buf.at[(1 - core, slice(None), slice(None)) + bits], self.recvs[0].at[(slice(None), slice(None)) + bits],
                c_send.at[self.index, piece], c_recv.at[self.index, piece], flip_r(0),
            )

        def step(self, colors=range(3)):
            for copy in self.pieces:
                copy.wait_recv()
            self.pieces = []
            for k in colors:
                self.advance(k)

        def done(self):
            return min(self.phase) > len(self.plans[0])

        def advance(self, k):
            p = self.phase[k]
            plan = self.plans[k]
            self.phase[k] += 1
            if p == 0:
                before, here = self.buf.at[core, k], self.recvs[0].at[k]
            else:
                self.copies[k].wait_recv()
                before = self.recvs[0].at[(k,) + self.kept[k]] if p == 1 else self.recvs[p - 1][k].at[self.kept[k]]
                here = self.recvs[p][k]
            if p == len(plan):
                rows = self.rows(k)
                final[core, xh, rows, :] = before[...] + here[...]
                if self.finals:
                    self.finals[k].start()
                return
            kind, b = plan[p]
            left = [("r", 1)] + [("c", i) for i in reversed(range(cb))]
            for gone in plan[:p]:
                left.remove(gone)
            axis = left.index((kind, b))
            bit = xh if kind == "r" else cbit[b]
            give = (slice(None),) * axis + (1 - bit,)
            keep = (slice(None),) * axis + (bit,)
            here[give] = before[give] + here[give]
            to = flip_r(1) if kind == "r" else flip_c(b)
            self.copies[k] = go(
                remote(
                    here.at[give], self.recvs[p + 1][k],
                    rs_send.at[self.index, k, p], rs_recv.at[self.index, k, p], to,
                )
            )
            here[keep] = before[keep] + here[keep]
            self.kept[k] = keep

    up_rows = COLORS * g_up.shape[-2]
    out_rows = COLORS * g_out.shape[-2]
    down_rows = 2 * sub
    up = Scatter(0, g_up, r_up, 0)
    out = Scatter(1, g_out, r_out, up_rows + down_rows)
    rest = Scatter(2, g_qkv, r_qkv, up_rows + down_rows + out_rows)
    scatters = {"up": up, "out": out, "qkv": rest}
    early = slice(up_rows, up_rows + down_rows)

    class Finals:
        def __init__(self, index, rows):
            self.index, self.rows = index, rows

        def start(self):
            for b in range(2, rb):
                there = extra.at[b - 2, self.rows]
                swap = remote(final.at[core, xh, self.rows], there, f_send.at[self.index, b], f_recv.at[self.index, b], flip_r(b))
                swap.start()
                swap.wait()
                final[core, xh, self.rows, :] = final[core, xh, self.rows, :] + there[...]
            here = final.at[core, xh, self.rows]
            self.copy = go(remote(here, here, f_send.at[self.index, 0], f_recv.at[self.index, 0], flip_r(1)))

        def step(self):
            self.copy.wait_recv()
            here = final.at[core, :, self.rows]
            self.copy = go(remote(here, here, f_send.at[self.index, 1], f_recv.at[self.index, 1], flip_r(0)))

        def end(self):
            self.copy.wait_recv()

    first_finals, rest.finals = Finals(0, early), [Finals(1 + k, rest.rows(k)) for k in range(COLORS)]
    up.finals = [Finals(1 + COLORS + k, up.rows(k)) for k in range(COLORS)]
    out.finals = [Finals(1 + 2 * COLORS + k, out.rows(k)) for k in range(COLORS)]

    def up_back(f, carry):
        cut = pl.ds(pl.multiple_of(f * width, 128), width)
        hh = dot_t(gpc_own[...], wdown[cut, :])
        spread = jnp.broadcast_to(hh[:, None, :], (captions, seq, width)).reshape(rows, width)
        slope[:, cut] = (spread * cols[:, 0:1] * slope[:, cut].astype(f32)).astype(bf16)
        emit("up", 0, dot_0(slope[:, cut], n2[...]), (lax.div(f, 2), lax.rem(f, 2)))
        up.start(f)
        return carry

    lax.fori_loop(0, 4, up_back, 0)
    for piece in range(4):
        up.started(piece)
    gn2 = dot_t(slope[...], wup[...])
    up.step()
    scaled, inv2 = stats(mixed[...])
    vec[2:3, :] = jnp.sum(gn2 * scaled, 0, keepdims=True)
    vec[3:4, :] = jnp.sum(gn2, 0, keepdims=True)
    spread = jnp.broadcast_to(gpc[:, None, :], (captions, seq, width)).reshape(rows, width) * weight
    mixed[...] = spread + norm_back(gn2, scaled, inv2, g2[...][None])
    n2[...] = mixed[...].astype(bf16)
    emit("out", 0, dot_0(n2[...], at[...]))
    for piece in range(4):
        out.start(piece)
    at[...] = dot_t(n2[...], wout[...]).astype(bf16)
    attend_back = text_attention_back(heads, group, width, qkv, probs, at)
    lax.fori_loop(0, groups // 2, attend_back, 0)
    up.step()
    out.step()

    for copy in acts + gps:
        copy.wait_recv()
    down = dot_0(act_all[...].reshape(C * captions, span), gpc_all[...].reshape(C * captions, width))
    for j in range(4):
        for s in range(2):
            d_part[s, j // 2, j % 2] = down[j * sub : (j + 1) * sub, s * half : (s + 1) * half].astype(bf16)
    d0 = go(remote(d_part.at[1 - core], d_recv, d_send.at[0], d_recv_sem.at[0], flip_r(0)))

    lax.fori_loop(groups // 2, groups, attend_back, 0)
    up.step(range(2))
    pieces = 0
    for q in range(3):
        emit("qkv", q * width, dot_0(qkv[:, q * width : (q + 1) * width], n1[...]))
        while pieces < 4 * (q + 1) // 3:
            rest.start(pieces)
            pieces += 1
    up.step(range(2, 3))
    out.step()
    d0.wait_recv()
    d_recv[:, 1 - xh] = d_part[core, :, 1 - xh] + d_recv[:, 1 - xh]
    d1 = go(remote(d_recv.at[:, 1 - xh], d_recv2, d_send.at[1], d_recv_sem.at[1], flip_r(1)))
    d_recv[:, xh] = d_part[core, :, xh] + d_recv[:, xh]
    rest.step()
    gn1 = dot_t(qkv[...], wqkv[...])
    up.step()
    scaled, inv1 = stats(x_ref[...].astype(f32))
    vec[0:1, :] = jnp.sum(gn1 * scaled, 0, keepdims=True)
    vec[1:2, :] = jnp.sum(gn1, 0, keepdims=True)
    vfirst = [go(remote(vec, vec_c.at[d], v_send.at[d], v_recv.at[d], to)) for d, to in enumerate(col_peers)]
    out.step()
    mixed[...] = mixed[...] + norm_back(gn1, scaled, inv1, g1[...][None])
    gx_out = pltpu.make_async_copy(mixed, gx_hbm, out_sem.at[0])
    gx_out.start()
    d1.wait_recv()
    for k in range(2):
        final[core, xh, up_rows + k * sub : up_rows + (k + 1) * sub, :] = d_recv[k, xh] + d_recv2[k]
    first_finals.start()
    rest.step()
    while not up.done():
        up.step()
        if not out.done():
            out.step()
    while not out.done():
        out.step()
    vtotal = vec[...]
    for d, copy in enumerate(vfirst):
        copy.wait_recv()
        vtotal += vec_c[d]
    vec_cs[...] = vtotal
    vsecond = [
        go(remote(vec_cs, vec_r.at[d], v_send.at[C - 1 + d], v_recv.at[C - 1 + d], to)) for d, to in enumerate(row_peers)
    ]
    rest.step()
    for some in [first_finals] + up.finals + out.finals:
        some.step()
    while not rest.done():
        rest.step()
    for last in rest.finals:
        last.step()
    for d, copy in enumerate(vsecond):
        copy.wait_recv()
        vtotal += vec_r[d]
    vecs_ref[...] = vtotal
    for some in [first_finals] + up.finals + out.finals:
        some.end()
    for last in rest.finals:
        last.end()
    parts_out = pltpu.make_async_copy(final, parts_hbm, out_sem.at[1])
    parts_out.start()
    for copy in sent:
        copy.wait_send()
    gx_out.wait()
    parts_out.wait()


def text_call(R, C, unit, tokens, mask, length, g1, s1, wqkv, wout, g2, s2, wup, wdown, heads=12, group=128):
    captions, seq, width = tokens.shape
    rows, hidden = captions * seq, wup.shape[1]
    rb, cb = log2(R), log2(C)
    half, sub, span = width // 2, hidden // (4 * C), hidden // C
    V, S, D = pltpu.VMEM, jax.ShapeDtypeStruct, pltpu.SemaphoreType.DMA
    pairs = captions * R * C
    bits_c = (2,) * cb

    dims, tail = 1 + rb + cb, (captions // 2, width)
    lead = max(log2(pairs // 1024), 0)
    held_dims, staged_dims = dims - lead, dims if lead else 0

    subs = [hidden // (2 * COLORS * C), width // (2 * COLORS * C), 3 * width // (2 * COLORS * C)]

    def recvs(rows):
        phases = len(color_plans(cb)[0]) + 1
        return [V((COLORS, 2) + bits_c + (rows, half), bf16)] + [
            [V((2,) * (1 + cb - p) + (rows, half), bf16) for _ in range(COLORS)] for p in range(1, phases)
        ]

    total = COLORS * sum(subs) + 2 * sub
    vm = pl.BlockSpec(memory_space=pltpu.VMEM)
    hbm = pl.BlockSpec(memory_space=pl.ANY)
    out = pl.pallas_call(
        functools.partial(text_step, (R, C, captions, seq, group), heads),
        name="text",
        in_specs=[vm] * 7 + [hbm] * 5,
        out_specs=(hbm, hbm, vm, hbm),
        out_shape=(S((rows, width), f32), S((2, 2, total, half), bf16), S((4, width), f32), S((2,) * staged_dims + tail, bf16)),
        scratch_shapes=[
            V((rows, width), bf16), V(wqkv.shape, bf16), V(wout.shape, bf16), V(wup.shape, bf16), V(wdown.shape, bf16),
            V((rows, width), bf16), V((rows, 3 * width), bf16), V((rows, heads * group), f32), V((rows, width), bf16),
            V((rows, width), f32), V((rows, width), bf16), V((rows, hidden), bf16), V((captions, hidden), f32), V((rows, 128), f32),
            V((2,) * held_dims + tail, bf16),
            V((1, pairs), f32), V((C - 1, 1, pairs), f32), V((1, pairs), f32), V((R - 1, 1, pairs), f32),
            V((C, captions, span), bf16), V((C, captions, span), bf16), V((captions, width), bf16), V((C, captions, width), bf16),
            *[V((2, COLORS, 2) + bits_c + (n, half), bf16) for n in subs], *[recvs(n) for n in subs],
            V((2, 2, 2, sub, half), bf16), V((2, 2, sub, half), bf16), V((2, sub, half), bf16),
            V((2, 2, total, half), bf16), V((max(rb - 2, 1), total, half), bf16),
            V((4, width), f32), V((C - 1, 4, width), f32), V((4, width), f32), V((R - 1, 4, width), f32),
            D((7,)), D((2,)), D((2, rb + cb)), D((2, rb + cb)), D((R + C - 2,)), D((R + C - 2,)),
            D((C - 1,)), D((C - 1,)), D((C - 1,)), D((C - 1,)),
            D((3, 4)), D((3, 4)), D((3, COLORS, cb + 1)), D((3, COLORS, cb + 1)), D((2,)), D((2,)), D((1 + 3 * COLORS, max(rb, 2))), D((1 + 3 * COLORS, max(rb, 2))), D((R + C - 2,)), D((R + C - 2,)),
        ],
        compiler_params=pltpu.CompilerParams(collective_id=0, has_side_effects=True, vmem_limit_bytes=67043328),
    )(unit, mask.T, length[None], g1, s1, g2, s2, tokens.reshape(rows, width), wqkv, wout, wup, wdown)
    return out[:3]


def finish_kernel(
    col_size, parts, vecs, shift, gx_in, gx_out, up_out, out_out, qkv_out, down_out, v0, v1, v2, v3,
    gx, up, out, qkv, down, sems
):
    load = pltpu.make_async_copy(gx_in, gx, sems.at[0])
    load.start()
    stores = []

    def store(src, dst):
        copy = pltpu.make_async_copy(src, dst, sems.at[1 + len(stores)])
        copy.start()
        stores.append(copy)

    def blocks(lo, colors, sub):
        for j in range(2 * colors):
            rows = slice(lo + j // 2 * sub, lo + (j // 2 + 1) * sub)
            yield j * sub, jnp.concatenate([parts[0, j % 2, rows, :], parts[1, j % 2, rows, :]], -1).astype(f32)

    def fill(ref, lo, colors):
        sub = ref.shape[0] // (2 * colors)
        for at_row, block in blocks(lo, colors, sub):
            ref[at_row : at_row + sub, :] = block

    hidden_share = down.shape[0]
    fill(down, hidden_share // 2, 2)
    store(down, down_out)
    fill(qkv, hidden_share + out.shape[0] // 2, COLORS)
    store(qkv, qkv_out)
    fill(out, hidden_share, COLORS)
    store(out, out_out)
    load.wait()
    store(gx, gx_out)
    up[...] = jnp.concatenate([block for _, block in blocks(0, COLORS, hidden_share // (2 * COLORS))], 0).T
    store(up, up_out)
    width = vecs.shape[1]
    share = width // col_size
    lane = lax.broadcasted_iota(jnp.int32, (width, share), 1)
    row = lax.broadcasted_iota(jnp.int32, (width, share), 0)
    pick = jnp.where(row == lane + shift[0], 1.0, 0.0)
    own = jnp.dot(vecs[...], pick, precision=lax.Precision.HIGHEST, preferred_element_type=f32)
    for k, v in enumerate((v0, v1, v2, v3)):
        v[...] = own[k : k + 1, :]
    for copy in stores:
        copy.wait()


def finish_call(C, hidden, gx, parts, vecs):
    width = 2 * parts.shape[-1]
    share, hidden_share = width // C, hidden // C
    S, V = jax.ShapeDtypeStruct, pltpu.VMEM
    shift = (lax.axis_index("col") * share).astype(jnp.int32)[None]
    vm = pl.BlockSpec(memory_space=pltpu.VMEM)
    hbm = pl.BlockSpec(memory_space=pl.ANY)
    shapes = [gx.shape, (width, hidden_share), (share, width), (3 * share, width), (hidden_share, width)]
    return pl.pallas_call(
        functools.partial(finish_kernel, C),
        name="finish",
        in_specs=[vm, vm, pl.BlockSpec(memory_space=pltpu.SMEM), hbm],
        out_specs=(hbm,) * 5 + (vm,) * 4,
        out_shape=tuple(S(s, f32) for s in shapes) + (S((1, share), f32),) * 4,
        scratch_shapes=[V(s, f32) for s in shapes] + [pltpu.SemaphoreType.DMA((6,))],
    )(parts, vecs, shift, gx)


def on_device(
    image_tokens, caption_tokens, caption_mask, caption_length,
    image_gain1, image_shift1, image_qkv, image_out, image_gain2, image_shift2, image_up, image_down,
    text_gain1, text_shift1, text_qkv, text_out, text_gain2, text_shift2, text_up, text_down,
):
    R, C = lax.axis_size("row"), lax.axis_size("col")
    unit = image_unit(
        image_tokens, image_gain1, image_shift1, image_qkv, image_out,
        image_gain2, image_shift2, image_up, image_down,
    )
    grad_tokens, parts, vecs = text_call(
        R, C, unit, caption_tokens, caption_mask, caption_length, text_gain1, text_shift1, text_qkv, text_out,
        text_gain2, text_shift2, text_up, text_down,
    )
    grad_tokens, up, out, qkv, down, gain1, shift1, gain2, shift2 = finish_call(C, text_up.shape[1], grad_tokens, parts, vecs)
    return (
        grad_tokens.reshape(caption_tokens.shape), gain1[0], shift1[0], qkv.T, out.T, gain2[0], shift2[0], up, down,
    )


def solution(mesh):
    pair = P(("row", "col"))
    return jax.shard_map(
        on_device,
        mesh=mesh,
        in_specs=(pair,) * 4 + (P(),) * 16,
        out_specs=(pair, P("col"), P("col"), P(None, "col"), P(None, "col"), P("col"), P("col"), P(None, "col"), P("col")),
        check_vma=False,
    )
```
